512 devices in a mesh: ma: 64 (over x, y, core), freq: 8 (over z).
Axes of the slice: x: 4, y: 8, z: 8, core: 2. Of those that a mesh axis runs over, the one named last changes fastest.
Arguments:
- timestream: bfloat16 [32, 128, 8, 2048], P('freq', 'ma'), may hold values from -6 to 6
- beam_transfer: bfloat16 [64, 2048, 896], P('ma'), may hold values from -0.1875 to 0.1875
- chromatic_gain: float32 [32, 896], P('freq'), may hold values from 0.5 to 2
- noise_weight: float32 [32, 64, 2048], P('freq', 'ma'), may hold values from 0.25 to 4.5
- prior_diagonal: float32 [32, 896], P('freq'), may hold values from 0.3 to 3
- prior_modes: float32 [32, 2, 896], P('freq'), may hold values from -3 to 3
Outputs:
- sky_estimate: float32 [32, 64, 8, 896], P('freq', 'ma')
The draws below stay inside these ranges and needn't reach their ends.
All inputs are finite; a program needn't handle non-finite values.
Results may differ from the reference program's by a relative error of at most 0.015.
Values may be sent and summed in bfloat16 or wider, within the bound.
A program may use at most 64 MiB of HBM per device.

```python
import math
import jax
import jax.numpy as jnp
from jax import lax

NB = 2048
NS = 896
RANK = 2
K = 8
ITERS = 2
MMODES = 64
NT = 128
FREQS = 32


def draw_noise_weight(key, part):
    inner_key = jax.random.fold_in(key, 11)
    base = jnp.exp(jax.random.uniform(inner_key, (FREQS, MMODES, NB), jnp.float32, jnp.log(0.3), jnp.log(1.5)))
    rising = 1.0 + 2.0 * jnp.arange(MMODES).astype(jnp.float32) / max(MMODES - 1, 1)
    return base * rising[None, :, None]


def block_levels(stream_key, extent, shards, low, largest):
    factor_of, own = 1.0, jax.random.fold_in(stream_key, 6)
    for position, parts in shards:
        draws = jnp.exp(jax.random.uniform(jax.random.fold_in(own, position), (parts,), jnp.float32, low / len(shards), largest / len(shards)))
        factor_of = factor_of * jnp.repeat(draws, extent[position] // parts).reshape([-1 if axis == position else 1 for axis in range(len(extent))])
    return factor_of


def bell_draw(key, shape, width, reach, cuts=(), kind=jnp.bfloat16):
    drawn = width * jax.random.normal(key, shape, jnp.float32)
    if cuts:
        drawn = drawn * block_levels(key, shape, cuts, -0.22, 0.18)
    return jnp.clip(drawn, -reach, reach).astype(kind)


def setup_inputs(seed: int = 0) -> dict:
    arg_keys = jax.random.split(jax.random.key(seed), 7)
    timestream = bell_draw(arg_keys[0], (FREQS, NT, K, NB), 1.0, 6.0, ((0, 8), (1, 64)))
    beam_transfer = bell_draw(arg_keys[1], (MMODES, NB, NS), NS ** -0.5, 0.1875, ((0, 64),))
    chromatic_gain = jnp.clip(jnp.exp(math.log(2.0) - 1.3862944 * jax.random.uniform(arg_keys[2], (FREQS, NS), jnp.float32) ** block_levels(arg_keys[2], (FREQS, NS), ((0, 8),), -0.2, 0.2)), 0.5, 2.0)
    noise_weight = draw_noise_weight(jax.random.fold_in(arg_keys[6], 71), 0)
    prior_diagonal = jnp.clip(jnp.exp(math.log(3.0) - 2.3025851 * jax.random.uniform(arg_keys[4], (FREQS, NS), jnp.float32) ** block_levels(arg_keys[4], (FREQS, NS), ((0, 8),), -0.2, 0.2)), 0.3, 3.0)
    prior_modes = bell_draw(arg_keys[5], (FREQS, RANK, NS), 0.5, 3.0, ((0, 8),), jnp.float32)
    return dict(timestream=timestream, beam_transfer=beam_transfer, chromatic_gain=chromatic_gain, noise_weight=noise_weight, prior_diagonal=prior_diagonal, prior_modes=prior_modes)


def hartley_table(rows, cols):
    index_m = jnp.arange(rows, dtype=jnp.int32)[:, None]
    index_t = jnp.arange(cols, dtype=jnp.int32)[None, :]
    phase = (index_m * index_t % cols).astype(jnp.float32)
    angle = 2.0 * jnp.pi * phase / cols
    return (jnp.cos(angle) + jnp.sin(angle)) / jnp.sqrt(jnp.float32(cols))

def reference(timestream, beam_transfer, chromatic_gain, noise_weight, prior_diagonal, prior_modes):
    hartley = hartley_table(MMODES, NT)

    def transform(series):
        columns = series.reshape(NT, K * NB).astype(jnp.float32)
        result = jnp.dot(hartley, columns, precision=lax.Precision.HIGHEST)
        return result.reshape(MMODES, K, NB).astype(jnp.bfloat16)
    measured_visibility = lax.map(transform, timestream)
    weighted = (noise_weight[:, :, None, :] * measured_visibility.astype(jnp.float32)).astype(jnp.bfloat16)
    weighted = lax.optimization_barrier(weighted)
    weighted_m = jnp.transpose(weighted, (1, 0, 2, 3))
    weights_m = jnp.transpose(noise_weight, (1, 0, 2))

    def adjoint(pair):
        heard, block = pair
        summed = jnp.einsum('fkb,bs->fks', heard.astype(jnp.float32), block.astype(jnp.float32), precision=lax.Precision.HIGHEST)
        return chromatic_gain[:, None, :] * summed
    rhs = jnp.transpose(lax.map(adjoint, (weighted_m, beam_transfer)), (1, 0, 2, 3))

    def blockwise(triple):
        low, block, weight_rows = triple
        block_wide = block.astype(jnp.float32)
        seen = jnp.einsum('fks,bs->fkb', low.astype(jnp.float32), block_wide, precision=lax.Precision.HIGHEST)
        heard = (weight_rows[:, None, :] * seen).astype(jnp.bfloat16)
        heard = lax.optimization_barrier(heard)
        summed = jnp.einsum('fkb,bs->fks', heard.astype(jnp.float32), block_wide, precision=lax.Precision.HIGHEST)
        return chromatic_gain[:, None, :] * summed

    def apply_operator(vector):
        low = lax.optimization_barrier((chromatic_gain[:, None, None, :] * vector).astype(jnp.bfloat16))
        beam_part = lax.map(blockwise, (jnp.transpose(low, (1, 0, 2, 3)), beam_transfer, weights_m))
        beam_part = jnp.transpose(beam_part, (1, 0, 2, 3))
        projection = jnp.einsum('frs,fmks->rmks', prior_modes, vector, precision=lax.Precision.HIGHEST)
        spread = jnp.einsum('frs,rmks->fmks', prior_modes, projection, precision=lax.Precision.HIGHEST)
        return beam_part + prior_diagonal[:, None, None, :] * vector + spread

    def inner(left, right):
        return lax.optimization_barrier(jnp.sum(left * right, axis=(0, 1, 3)))
    estimate = jnp.zeros((FREQS, MMODES, K, NS), jnp.float32)
    residual = rhs
    direction = rhs
    norm_now = inner(residual, residual)
    for turn_index in range(ITERS):
        image = apply_operator(direction)
        step_size = norm_now / inner(direction, image)
        estimate = estimate + step_size[None, None, :, None] * direction
        residual = residual - step_size[None, None, :, None] * image
        norm_next = inner(residual, residual)
        direction = residual + (norm_next / norm_now)[None, None, :, None] * direction
        norm_now = norm_next
    return estimate
```

```python
import functools

import jax
import jax.numpy as jnp
from jax import lax
from jax.experimental import pallas as pl
from jax.experimental.pallas import tpu as pltpu
from jax.sharding import PartitionSpec as P

ITERS = 2
MESH = pl.DeviceIdType.MESH


def hartley_table(rows, cols):
    index_m = jnp.arange(rows, dtype=jnp.int32)[:, None]
    index_t = jnp.arange(cols, dtype=jnp.int32)[None, :]
    phase = (index_m * index_t % cols).astype(jnp.float32)
    angle = 2.0 * jnp.pi * phase / cols
    return (jnp.cos(angle) + jnp.sin(angle)) / jnp.sqrt(jnp.float32(cols))


def inner(left, right):
    return jnp.sum(left * right, axis=(0, 1, 3))


def reduce_kernel(axis_names, stages, x_ref, o_ref, cur, recv, send_sem, recv_sem):
    me = {name: lax.axis_index(name) for name in axis_names}

    def device(axis, coord):
        return tuple(coord if name == axis else me[name] for name in axis_names)

    plan = []
    base = 0
    for axis, stride, size in stages:
        own = (me[axis] // stride) % size
        root = me[axis] - own * stride
        peers = []
        for step in range(1, size):
            other = lax.rem(own + step, size)
            peers.append((other, device(axis, root + other * stride)))
        plan.append((base, own, size, peers))
        base += size

    barrier = pltpu.get_barrier_semaphore()
    for _, _, _, peers in plan:
        for _, peer in peers:
            pl.semaphore_signal(barrier, 1, device_id=peer, device_id_type=MESH)
    pl.semaphore_wait(barrier, sum(len(peers) for _, _, _, peers in plan))

    acc = x_ref[...].astype(jnp.float32)
    for index, (base, own, size, peers) in enumerate(plan):
        cur[index] = acc.astype(cur.dtype)
        copies = []
        for other, peer in peers:
            copy = pltpu.make_async_remote_copy(
                src_ref=cur.at[index],
                dst_ref=recv.at[base + own],
                send_sem=send_sem.at[base + other],
                recv_sem=recv_sem.at[base + own],
                device_id=peer,
                device_id_type=MESH,
            )
            copy.start()
            copies.append(copy)
        recv[base + own] = acc.astype(recv.dtype)
        for other, peer in peers:
            pltpu.make_async_remote_copy(
                src_ref=cur.at[index],
                dst_ref=recv.at[base + other],
                send_sem=send_sem.at[base + other],
                recv_sem=recv_sem.at[base + other],
                device_id=peer,
                device_id_type=MESH,
            ).wait_recv()
        for copy in copies:
            copy.wait_send()
        total = recv[base].astype(jnp.float32)
        for slot in range(1, size):
            total = total + recv[base + slot].astype(jnp.float32)
        acc = total
    o_ref[...] = acc.astype(o_ref.dtype)


def group_sum(x, axis_names, stages, wire_dtype, collective_id):
    slots = sum(size for _, _, size in stages)
    return pl.pallas_call(
        functools.partial(reduce_kernel, axis_names, stages),
        out_shape=jax.ShapeDtypeStruct(x.shape, jnp.float32),
        in_specs=[pl.BlockSpec(memory_space=pltpu.VMEM)],
        out_specs=pl.BlockSpec(memory_space=pltpu.VMEM),
        scratch_shapes=[
            pltpu.VMEM((len(stages),) + x.shape, wire_dtype),
            pltpu.VMEM((slots,) + x.shape, wire_dtype),
            pltpu.SemaphoreType.DMA((slots,)),
            pltpu.SemaphoreType.DMA((slots,)),
        ],
        compiler_params=pltpu.CompilerParams(collective_id=collective_id, has_side_effects=True),
    )(x)


def make_shards(mesh):
    axis_names = tuple(mesh.axis_names)
    mode_devices = mesh.shape["ma"]
    freq_devices = mesh.shape["freq"]
    if mode_devices % 16 == 0:
        mode_stages = [("ma", 1, 2), ("ma", 2, 8), ("ma", 16, mode_devices // 16)]
    else:
        mode_stages = [("ma", 1, mode_devices)]
    global_stages = mode_stages + [("freq", 1, freq_devices)]
    freq_stages = [("freq", 1, freq_devices)]

    def scalar_sum(*vectors):
        rows = jnp.stack(vectors)
        padded = jnp.pad(rows, ((0, 8 - rows.shape[0]), (0, 128 - rows.shape[1])))
        summed = group_sum(padded, axis_names, global_stages, jnp.float32, 2)
        return [summed[index, : rows.shape[1]] for index in range(len(vectors))]

    def freq_sum(partial_sum):
        shape = partial_sum.shape
        flat = partial_sum.reshape(-1, shape[-1])
        summed = group_sum(flat, axis_names, freq_stages, jnp.bfloat16, 1)
        return summed.reshape(shape)

    def shards(timestream, beam_transfer, chromatic_gain, noise_weight, prior_diagonal, prior_modes):
        spectral_channels = timestream.shape[0]
        device_time_samples = timestream.shape[1]
        noise_realizations = timestream.shape[2]
        antenna_pairs = timestream.shape[3]
        timestream_rows = timestream.reshape(
            spectral_channels, device_time_samples, noise_realizations * antenna_pairs
        )
        gathered = lax.all_to_all(timestream_rows, "ma", split_axis=2, concat_axis=1, tiled=True)
        all_times = gathered.shape[1]
        hartley = hartley_table(all_times // 2, all_times)
        hartley_high = hartley.astype(jnp.bfloat16)
        hartley_low = (hartley - hartley_high.astype(jnp.float32)).astype(jnp.bfloat16)
        mode_high = jnp.einsum(
            "mt,ftc->fmc", hartley_high, gathered, preferred_element_type=jnp.float32
        )
        mode_low = jnp.einsum("mt,ftc->fmc", hartley_low, gathered, preferred_element_type=jnp.float32)
        mode_rows = (mode_high + mode_low).astype(jnp.bfloat16)
        device_mode_count = lax.all_to_all(mode_rows, "ma", split_axis=1, concat_axis=2, tiled=True)
        resident_modes = device_mode_count.shape[1]
        measured_visibility = device_mode_count.reshape(
            spectral_channels, resident_modes, noise_realizations, antenna_pairs
        )
        chroma = chromatic_gain[:, None, None, :]
        diagonal = prior_diagonal[:, None, None, :]
        weighted = (noise_weight[:, :, None, :] * measured_visibility.astype(jnp.float32)).astype(
            jnp.bfloat16
        )
        rhs = chroma * jnp.einsum(
            "fmkb,mbs->fmks", weighted, beam_transfer, preferred_element_type=jnp.float32
        )

        estimate = jnp.zeros(rhs.shape, jnp.float32)
        residual = rhs
        direction = rhs
        norm_now = None
        for turn_index in range(ITERS):
            low = (chroma * direction).astype(jnp.bfloat16)
            seen = jnp.einsum("fmks,mbs->fmkb", low, beam_transfer, preferred_element_type=jnp.float32)
            heard = (noise_weight[:, :, None, :] * seen).astype(jnp.bfloat16)
            back = jnp.einsum(
                "fmkb,mbs->fmks", heard, beam_transfer, preferred_element_type=jnp.float32
            )
            partial_sum = jnp.einsum(
                "frs,fmks->rmks", prior_modes, direction, precision=lax.Precision.HIGHEST
            )
            projection = freq_sum(partial_sum)
            image = (
                chroma * back
                + diagonal * direction
                + jnp.einsum("frs,rmks->fmks", prior_modes, projection, precision=lax.Precision.HIGHEST)
            )
            if norm_now is None:
                norm_now, curve = scalar_sum(inner(residual, residual), inner(direction, image))
            else:
                (curve,) = scalar_sum(inner(direction, image))
            step_size = norm_now / curve
            estimate = estimate + step_size[None, None, :, None] * direction
            if turn_index + 1 < ITERS:
                residual = residual - step_size[None, None, :, None] * image
                (norm_next,) = scalar_sum(inner(residual, residual))
                direction = residual + (norm_next / norm_now)[None, None, :, None] * direction
                norm_now = norm_next
        return estimate

    return shards


def solution(mesh):
    in_specs = (
        P("freq", "ma", None, None),
        P("ma", None, None),
        P("freq", None),
        P("freq", "ma", None),
        P("freq", None),
        P("freq", None, None),
    )
    out_specs = P("freq", "ma", None, None)
    return jax.shard_map(make_shards(mesh), mesh=mesh, in_specs=in_specs, out_specs=out_specs, check_vma=False)
```

```python
import functools

import jax
import jax.numpy as jnp
from jax import lax
from jax.experimental import pallas as pl
from jax.experimental.pallas import tpu as pltpu
from jax.sharding import PartitionSpec as P

ITERS = 2
MESH = pl.DeviceIdType.MESH


def hartley_table(rows, cols):
    index_m = jnp.arange(rows, dtype=jnp.int32)[:, None]
    index_t = jnp.arange(cols, dtype=jnp.int32)[None, :]
    phase = (index_m * index_t % cols).astype(jnp.float32)
    angle = 2.0 * jnp.pi * phase / cols
    return (jnp.cos(angle) + jnp.sin(angle)) / jnp.sqrt(jnp.float32(cols))


def inner(left, right):
    return jnp.sum(left * right, axis=(0, 1, 3))


def reduce_kernel(axis_names, stages, x_ref, o_ref, cur, recv, send_sem, recv_sem):
    me = {name: lax.axis_index(name) for name in axis_names}

    def device(axis, coord):
        return tuple(coord if name == axis else me[name] for name in axis_names)

    plan = []
    base = 0
    for axis, stride, size in stages:
        own = (me[axis] // stride) % size
        root = me[axis] - own * stride
        peers = []
        for step in range(1, size):
            other = lax.rem(own + step, size)
            peers.append((other, device(axis, root + other * stride)))
        plan.append((base, own, size, peers))
        base += size

    barrier = pltpu.get_barrier_semaphore()
    for _, _, _, peers in plan:
        for _, peer in peers:
            pl.semaphore_signal(barrier, 1, device_id=peer, device_id_type=MESH)
    pl.semaphore_wait(barrier, sum(len(peers) for _, _, _, peers in plan))

    acc = x_ref[...].astype(jnp.float32)
    for index, (base, own, size, peers) in enumerate(plan):
        cur[index] = acc.astype(cur.dtype)
        copies = []
        for other, peer in peers:
            copy = pltpu.make_async_remote_copy(
                src_ref=cur.at[index],
                dst_ref=recv.at[base + own],
                send_sem=send_sem.at[base + other],
                recv_sem=recv_sem.at[base + own],
                device_id=peer,
                device_id_type=MESH,
            )
            copy.start()
            copies.append(copy)
        recv[base + own] = acc.astype(recv.dtype)
        for other, peer in peers:
            pltpu.make_async_remote_copy(
                src_ref=cur.at[index],
                dst_ref=recv.at[base + other],
                send_sem=send_sem.at[base + other],
                recv_sem=recv_sem.at[base + other],
                device_id=peer,
                device_id_type=MESH,
            ).wait_recv()
        for copy in copies:
            copy.wait_send()
        total = recv[base].astype(jnp.float32)
        for slot in range(1, size):
            total = total + recv[base + slot].astype(jnp.float32)
        acc = total
    o_ref[...] = acc.astype(o_ref.dtype)


def group_sum(x, axis_names, stages, wire_dtype, collective_id):
    slots = sum(size for _, _, size in stages)
    return pl.pallas_call(
        functools.partial(reduce_kernel, axis_names, stages),
        out_shape=jax.ShapeDtypeStruct(x.shape, jnp.float32),
        in_specs=[pl.BlockSpec(memory_space=pltpu.VMEM)],
        out_specs=pl.BlockSpec(memory_space=pltpu.VMEM),
        scratch_shapes=[
            pltpu.VMEM((len(stages),) + x.shape, wire_dtype),
            pltpu.VMEM((slots,) + x.shape, wire_dtype),
            pltpu.SemaphoreType.DMA((slots,)),
            pltpu.SemaphoreType.DMA((slots,)),
        ],
        compiler_params=pltpu.CompilerParams(collective_id=collective_id, has_side_effects=True),
    )(x)


def make_shards(mesh):
    axis_names = tuple(mesh.axis_names)
    mode_devices = mesh.shape["ma"]
    freq_devices = mesh.shape["freq"]
    if mode_devices % 16 == 0:
        mode_stages = [("ma", 1, 2), ("ma", 2, 8), ("ma", 16, mode_devices // 16)]
    else:
        mode_stages = [("ma", 1, mode_devices)]
    global_stages = mode_stages + [("freq", 1, freq_devices)]
    freq_stages = [("freq", 1, freq_devices)]

    def scalar_sum(*vectors):
        rows = jnp.stack(vectors)
        padded = jnp.pad(rows, ((0, 8 - rows.shape[0]), (0, 128 - rows.shape[1])))
        summed = group_sum(padded, axis_names, global_stages, jnp.float32, 2)
        return [summed[index, : rows.shape[1]] for index in range(len(vectors))]

    def freq_sum(partial_sum):
        shape = partial_sum.shape
        flat = partial_sum.reshape(-1, shape[-1])
        summed = group_sum(flat, axis_names, freq_stages, jnp.bfloat16, 1)
        return summed.reshape(shape)

    def shards(timestream, beam_transfer, chromatic_gain, noise_weight, prior_diagonal, prior_modes):
        spectral_channels = timestream.shape[0]
        device_time_samples = timestream.shape[1]
        noise_realizations = timestream.shape[2]
        antenna_pairs = timestream.shape[3]
        mode_devices_here = mode_devices
        columns = noise_realizations * antenna_pairs // mode_devices_here
        blocks = antenna_pairs // columns
        halves = columns // 128
        send = timestream.reshape(
            spectral_channels, device_time_samples, noise_realizations, blocks, halves, 128
        ).transpose(2, 3, 0, 1, 4, 5)
        send = send.reshape(mode_devices_here, spectral_channels * device_time_samples * halves, 128)
        received = lax.all_to_all(send, "ma", 0, 0, tiled=True)
        received = received.reshape(mode_devices_here, spectral_channels, device_time_samples, columns)
        all_times = mode_devices_here * device_time_samples
        hartley = hartley_table(all_times // 2, all_times)
        hartley_high = hartley.astype(jnp.bfloat16)
        hartley_low = (hartley - hartley_high.astype(jnp.float32)).astype(jnp.bfloat16)
        hartley_high = hartley_high.reshape(all_times // 2, mode_devices_here, device_time_samples)
        hartley_low = hartley_low.reshape(all_times // 2, mode_devices_here, device_time_samples)
        mode_high = jnp.einsum(
            "mit,iftc->mfc", hartley_high, received, preferred_element_type=jnp.float32
        )
        mode_low = jnp.einsum("mit,iftc->mfc", hartley_low, received, preferred_element_type=jnp.float32)
        mode_rows = (mode_high + mode_low).astype(jnp.bfloat16)
        back_rows = lax.all_to_all(mode_rows, "ma", 0, 0, tiled=True)
        resident_modes = back_rows.shape[0] // mode_devices_here
        back_rows = back_rows.reshape(
            noise_realizations, blocks, resident_modes, spectral_channels, columns
        )
        measured_visibility = back_rows.transpose(3, 2, 0, 1, 4).reshape(
            spectral_channels, resident_modes, noise_realizations, antenna_pairs
        )
        chroma = chromatic_gain[:, None, None, :]
        diagonal = prior_diagonal[:, None, None, :]
        weighted = (noise_weight[:, :, None, :] * measured_visibility.astype(jnp.float32)).astype(
            jnp.bfloat16
        )
        rhs = chroma * jnp.einsum(
            "fmkb,mbs->fmks", weighted, beam_transfer, preferred_element_type=jnp.float32
        )

        estimate = jnp.zeros(rhs.shape, jnp.float32)
        residual = rhs
        direction = rhs
        norm_now = None
        for turn_index in range(ITERS):
            low = (chroma * direction).astype(jnp.bfloat16)
            seen = jnp.einsum("fmks,mbs->fmkb", low, beam_transfer, preferred_element_type=jnp.float32)
            heard = (noise_weight[:, :, None, :] * seen).astype(jnp.bfloat16)
            back = jnp.einsum(
                "fmkb,mbs->fmks", heard, beam_transfer, preferred_element_type=jnp.float32
            )
            partial_sum = jnp.sum(prior_modes[:, :, None, None, :] * direction[:, None], axis=0)
            projection = freq_sum(partial_sum)
            image = (
                chroma * back
                + diagonal * direction
                + jnp.sum(prior_modes[:, :, None, None, :] * projection[None], axis=1)
            )
            if norm_now is None:
                norm_now, curve = scalar_sum(inner(residual, residual), inner(direction, image))
            else:
                (curve,) = scalar_sum(inner(direction, image))
            step_size = norm_now / curve
            estimate = estimate + step_size[None, None, :, None] * direction
            if turn_index + 1 < ITERS:
                residual = residual - step_size[None, None, :, None] * image
                (norm_next,) = scalar_sum(inner(residual, residual))
                direction = residual + (norm_next / norm_now)[None, None, :, None] * direction
                norm_now = norm_next
        return estimate

    return shards


def solution(mesh):
    in_specs = (
        P("freq", "ma", None, None),
        P("ma", None, None),
        P("freq", None),
        P("freq", "ma", None),
        P("freq", None),
        P("freq", None, None),
    )
    out_specs = P("freq", "ma", None, None)
    return jax.shard_map(make_shards(mesh), mesh=mesh, in_specs=in_specs, out_specs=out_specs, check_vma=False)
```

```python
import functools

import jax
import jax.numpy as jnp
from jax import lax
from jax.experimental import pallas as pl
from jax.experimental.pallas import tpu as pltpu
from jax.sharding import PartitionSpec as P

ITERS = 2
MESH = pl.DeviceIdType.MESH


def hartley_table(rows, cols):
    index_m = jnp.arange(rows, dtype=jnp.int32)[:, None]
    index_t = jnp.arange(cols, dtype=jnp.int32)[None, :]
    phase = (index_m * index_t % cols).astype(jnp.float32)
    angle = 2.0 * jnp.pi * phase / cols
    return (jnp.cos(angle) + jnp.sin(angle)) / jnp.sqrt(jnp.float32(cols))


def inner(left, right):
    return jnp.sum(left * right, axis=(0, 1, 3))


def reduce_kernel(axis_names, stages, x_ref, o_ref, cur, recv, send_sem, recv_sem):
    me = {name: lax.axis_index(name) for name in axis_names}

    def device(axis, coord):
        return tuple(coord if name == axis else me[name] for name in axis_names)

    plan = []
    base = 0
    for axis, stride, size in stages:
        own = (me[axis] // stride) % size
        root = me[axis] - own * stride
        peers = []
        for step in range(1, size):
            other = lax.rem(own + step, size)
            peers.append((other, device(axis, root + other * stride)))
        plan.append((base, own, size, peers))
        base += size

    barrier = pltpu.get_barrier_semaphore()
    for _, _, _, peers in plan:
        for _, peer in peers:
            pl.semaphore_signal(barrier, 1, device_id=peer, device_id_type=MESH)
    pl.semaphore_wait(barrier, sum(len(peers) for _, _, _, peers in plan))

    acc = x_ref[...].astype(jnp.float32)
    for index, (base, own, size, peers) in enumerate(plan):
        cur[index] = acc.astype(cur.dtype)
        copies = []
        for other, peer in peers:
            copy = pltpu.make_async_remote_copy(
                src_ref=cur.at[index],
                dst_ref=recv.at[base + own],
                send_sem=send_sem.at[base + other],
                recv_sem=recv_sem.at[base + own],
                device_id=peer,
                device_id_type=MESH,
            )
            copy.start()
            copies.append(copy)
        recv[base + own] = acc.astype(recv.dtype)
        for other, peer in peers:
            pltpu.make_async_remote_copy(
                src_ref=cur.at[index],
                dst_ref=recv.at[base + other],
                send_sem=send_sem.at[base + other],
                recv_sem=recv_sem.at[base + other],
                device_id=peer,
                device_id_type=MESH,
            ).wait_recv()
        for copy in copies:
            copy.wait_send()
        total = recv[base].astype(jnp.float32)
        for slot in range(1, size):
            total = total + recv[base + slot].astype(jnp.float32)
        acc = total
    o_ref[...] = acc.astype(o_ref.dtype)


def group_sum(x, axis_names, stages, wire_dtype, collective_id):
    slots = sum(size for _, _, size in stages)
    return pl.pallas_call(
        functools.partial(reduce_kernel, axis_names, stages),
        out_shape=jax.ShapeDtypeStruct(x.shape, jnp.float32),
        in_specs=[pl.BlockSpec(memory_space=pltpu.VMEM)],
        out_specs=pl.BlockSpec(memory_space=pltpu.VMEM),
        scratch_shapes=[
            pltpu.VMEM((len(stages),) + x.shape, wire_dtype),
            pltpu.VMEM((slots,) + x.shape, wire_dtype),
            pltpu.SemaphoreType.DMA((slots,)),
            pltpu.SemaphoreType.DMA((slots,)),
        ],
        compiler_params=pltpu.CompilerParams(collective_id=collective_id, has_side_effects=True),
    )(x)


def column_sum(x):
    return jnp.sum(jnp.sum(x, axis=0), axis=1, keepdims=True)


def to_row(columns):
    count = columns[0].shape[0]
    sub = lax.broadcasted_iota(jnp.int32, (count, 128), 0)
    lane = lax.broadcasted_iota(jnp.int32, (count, 128), 1)
    acc = jnp.zeros((count, 128), jnp.float32)
    for index, column in enumerate(columns):
        acc = acc + jnp.where(lane == sub + count * index, jnp.broadcast_to(column, (count, 128)), 0.0)
    return jnp.sum(acc, axis=0, keepdims=True)


def from_row(row, index, count):
    sub = lax.broadcasted_iota(jnp.int32, (count, 128), 0)
    lane = lax.broadcasted_iota(jnp.int32, (count, 128), 1)
    picked = jnp.where(lane == sub + count * index, jnp.broadcast_to(row, (count, 128)), 0.0)
    return jnp.sum(picked, axis=1, keepdims=True)


def cg_kernel(first, axis_names, sizes, *refs):
    if first:
        (d_ref, cb_ref, diag_ref, pm_ref, est_ref, next_ref, norm_ref,
         part, rows, recv_p, recv_rows, p_send, p_recv, r_send, r_recv) = refs
    else:
        (d_ref, cb_ref, diag_ref, pm_ref, est_in_ref, norm_in_ref, est_ref,
         part, rows, recv_p, recv_rows, p_send, p_recv, r_send, r_recv) = refs
    me = {name: lax.axis_index(name) for name in axis_names}

    def device(axis, coord):
        return tuple(coord if name == axis else me[name] for name in axis_names)

    barrier = pltpu.get_barrier_semaphore()
    for axis in axis_names:
        size = sizes[axis]

        def greet(step, carry, axis=axis, size=size):
            other = lax.rem(me[axis] + step, size)
            pl.semaphore_signal(barrier, 1, device_id=device(axis, other), device_id_type=MESH)
            return carry

        lax.fori_loop(1, size, greet, 0)
    pl.semaphore_wait(barrier, sum(sizes[axis] - 1 for axis in axis_names))

    def exchange(axis, src, recv, base, send_sems, recv_sems):
        size = sizes[axis]
        own = me[axis]

        def copy_to(other, slot):
            return pltpu.make_async_remote_copy(
                src_ref=src,
                dst_ref=recv.at[base + slot],
                send_sem=send_sems.at[base + other],
                recv_sem=recv_sems.at[base + slot],
                device_id=device(axis, other),
                device_id_type=MESH,
            )

        def start(step, carry):
            copy_to(lax.rem(own + step, size), own).start()
            return carry

        lax.fori_loop(1, size, start, 0)
        recv[base + own] = src[...]

        def arrive(step, carry):
            other = lax.rem(own + step, size)
            copy_to(other, other).wait_recv()
            return carry

        lax.fori_loop(1, size, arrive, 0)

        def drain(step, carry):
            copy_to(lax.rem(own + step, size), own).wait_send()
            return carry

        lax.fori_loop(1, size, drain, 0)

        def add(slot, acc):
            return acc + recv[base + slot]

        return lax.fori_loop(1, size, add, recv[base])

    fz, fm = "freq", "ma"
    nz, nm = sizes[fz], sizes[fm]
    d = d_ref[...]
    cb = cb_ref[...]
    diag = diag_ref[...]
    pm = pm_ref[...]
    count = d.shape[1]
    for rank in range(pm.shape[1]):
        part[rank] = jnp.sum(pm[:, rank] * d, axis=0)
    if first:
        rows[0] = to_row([column_sum(d * (cb + diag * d)), column_sum(d * d)])
    else:
        rows[0] = to_row([column_sum(d * (cb + diag * d))])
    projection = exchange(fz, part, recv_p, 0, p_send, p_recv)
    zrow = exchange(fz, rows.at[0], recv_rows, 0, r_send, r_recv)
    rows[1] = zrow + to_row([column_sum(projection * projection)])
    total = exchange(fm, rows.at[1], recv_rows, nz, r_send, r_recv)
    curve = from_row(total, 0, count)
    if first:
        norm_now = from_row(total, 1, count)
        step_size = (norm_now / curve)[None]
        est_ref[...] = step_size * d
        spread = pm[:, 0] * projection[0][None]
        for rank in range(1, pm.shape[1]):
            spread = spread + pm[:, rank] * projection[rank][None]
        image = cb + diag * d + spread
        residual = d - step_size * image
        rows[2] = to_row([column_sum(residual * residual)])
        zrow = exchange(fz, rows.at[2], recv_rows, nz + nm, r_send, r_recv)
        rows[3] = zrow
        total = exchange(fm, rows.at[3], recv_rows, 2 * nz + nm, r_send, r_recv)
        norm_next = from_row(total, 0, count)
        next_ref[...] = residual + (norm_next / norm_now)[None] * d
        norm_ref[...] = total
    else:
        norm_now = from_row(norm_in_ref[...], 0, count)
        est_ref[...] = est_in_ref[...] + (norm_now / curve)[None] * d


def cg_step(first, axis_names, sizes, d, cb, diag, pm, *extra):
    rounds = 4 if first else 2
    slots = (rounds // 2) * (sizes["ma"] + sizes["freq"])
    nz = sizes["freq"]
    vector = jax.ShapeDtypeStruct(d.shape, jnp.float32)
    row = jax.ShapeDtypeStruct((1, 128), jnp.float32)
    out_shape = (vector, vector, row) if first else vector
    vmem = pl.BlockSpec(memory_space=pltpu.VMEM)
    part_shape = (pm.shape[1],) + d.shape[1:]
    return pl.pallas_call(
        functools.partial(cg_kernel, first, axis_names, sizes),
        out_shape=out_shape,
        in_specs=[vmem] * (4 + len(extra)),
        out_specs=(vmem, vmem, vmem) if first else vmem,
        scratch_shapes=[
            pltpu.VMEM(part_shape, jnp.float32),
            pltpu.VMEM((rounds, 1, 128), jnp.float32),
            pltpu.VMEM((nz,) + part_shape, jnp.float32),
            pltpu.VMEM((slots, 1, 128), jnp.float32),
            pltpu.SemaphoreType.DMA((nz,)),
            pltpu.SemaphoreType.DMA((nz,)),
            pltpu.SemaphoreType.DMA((slots,)),
            pltpu.SemaphoreType.DMA((slots,)),
        ],
        compiler_params=pltpu.CompilerParams(
            collective_id=1 if first else 2, has_side_effects=True
        ),
    )(d, cb, diag, pm, *extra)


def make_shards(mesh):
    axis_names = tuple(mesh.axis_names)
    mode_devices = mesh.shape["ma"]
    freq_devices = mesh.shape["freq"]
    if mode_devices % 16 == 0:
        mode_stages = [("ma", 1, 2), ("ma", 2, 8), ("ma", 16, mode_devices // 16)]
    else:
        mode_stages = [("ma", 1, mode_devices)]
    global_stages = mode_stages + [("freq", 1, freq_devices)]
    freq_stages = [("freq", 1, freq_devices)]

    def scalar_sum(*vectors):
        rows = jnp.stack(vectors)
        padded = jnp.pad(rows, ((0, 8 - rows.shape[0]), (0, 128 - rows.shape[1])))
        summed = group_sum(padded, axis_names, global_stages, jnp.float32, 2)
        return [summed[index, : rows.shape[1]] for index in range(len(vectors))]

    def freq_sum(partial_sum):
        shape = partial_sum.shape
        flat = partial_sum.reshape(-1, shape[-1])
        summed = group_sum(flat, axis_names, freq_stages, jnp.bfloat16, 1)
        return summed.reshape(shape)

    def shards(timestream, beam_transfer, chromatic_gain, noise_weight, prior_diagonal, prior_modes):
        spectral_channels = timestream.shape[0]
        device_time_samples = timestream.shape[1]
        noise_realizations = timestream.shape[2]
        antenna_pairs = timestream.shape[3]
        mode_devices_here = mode_devices
        columns = noise_realizations * antenna_pairs // mode_devices_here
        blocks = antenna_pairs // columns
        halves = columns // 128
        send = timestream.reshape(
            spectral_channels, device_time_samples, noise_realizations, blocks, halves, 128
        ).transpose(2, 3, 0, 1, 4, 5)
        send = send.reshape(mode_devices_here, spectral_channels * device_time_samples * halves, 128)
        received = lax.all_to_all(send, "ma", 0, 0, tiled=True)
        received = received.reshape(mode_devices_here, spectral_channels, device_time_samples, columns)
        all_times = mode_devices_here * device_time_samples
        hartley = hartley_table(all_times // 2, all_times)
        hartley_high = hartley.astype(jnp.bfloat16)
        hartley_low = (hartley - hartley_high.astype(jnp.float32)).astype(jnp.bfloat16)
        hartley_high = hartley_high.reshape(all_times // 2, mode_devices_here, device_time_samples)
        hartley_low = hartley_low.reshape(all_times // 2, mode_devices_here, device_time_samples)
        mode_high = jnp.einsum(
            "mit,iftc->mfc", hartley_high, received, preferred_element_type=jnp.float32
        )
        mode_low = jnp.einsum("mit,iftc->mfc", hartley_low, received, preferred_element_type=jnp.float32)
        mode_rows = (mode_high + mode_low).astype(jnp.bfloat16)
        back_rows = lax.all_to_all(mode_rows, "ma", 0, 0, tiled=True)
        resident_modes = back_rows.shape[0] // mode_devices_here
        back_rows = back_rows.reshape(
            noise_realizations, blocks, resident_modes, spectral_channels, columns
        )
        measured_visibility = back_rows.transpose(3, 2, 0, 1, 4).reshape(
            spectral_channels, resident_modes, noise_realizations, antenna_pairs
        )
        chroma = chromatic_gain[:, None, None, :]
        diagonal = prior_diagonal[:, None, None, :]
        weighted = (noise_weight[:, :, None, :] * measured_visibility.astype(jnp.float32)).astype(
            jnp.bfloat16
        )
        rhs = chroma * jnp.einsum(
            "fmkb,mbs->fmks", weighted, beam_transfer, preferred_element_type=jnp.float32
        )

        assert resident_modes == 1
        sizes = {name: mesh.shape[name] for name in axis_names}
        diag_rows = prior_diagonal[:, None, :]
        mode_rows4 = prior_modes[:, :, None, :]

        def beam_back(direction):
            low = (chroma * direction).astype(jnp.bfloat16)
            seen = jnp.einsum("fmks,mbs->fmkb", low, beam_transfer, preferred_element_type=jnp.float32)
            heard = (noise_weight[:, :, None, :] * seen).astype(jnp.bfloat16)
            back = jnp.einsum(
                "fmkb,mbs->fmks", heard, beam_transfer, preferred_element_type=jnp.float32
            )
            return (chroma * back)[:, 0]

        direction = rhs[:, 0]
        estimate, direction, norm_row = cg_step(
            True, axis_names, sizes, direction, beam_back(direction[:, None]), diag_rows, mode_rows4
        )
        estimate = cg_step(
            False, axis_names, sizes, direction, beam_back(direction[:, None]), diag_rows, mode_rows4,
            estimate, norm_row,
        )
        estimate = estimate[:, None]
        return estimate

    return shards


def solution(mesh):
    in_specs = (
        P("freq", "ma", None, None),
        P("ma", None, None),
        P("freq", None),
        P("freq", "ma", None),
        P("freq", None),
        P("freq", None, None),
    )
    out_specs = P("freq", "ma", None, None)
    return jax.shard_map(make_shards(mesh), mesh=mesh, in_specs=in_specs, out_specs=out_specs, check_vma=False)
```

```python
import functools

import jax
import jax.numpy as jnp
from jax import lax
from jax.experimental import pallas as pl
from jax.experimental.pallas import tpu as pltpu
from jax.sharding import PartitionSpec as P

ITERS = 2
MESH = pl.DeviceIdType.MESH


def hartley_table(rows, cols):
    index_m = jnp.arange(rows, dtype=jnp.int32)[:, None]
    index_t = jnp.arange(cols, dtype=jnp.int32)[None, :]
    phase = (index_m * index_t % cols).astype(jnp.float32)
    angle = 2.0 * jnp.pi * phase / cols
    return (jnp.cos(angle) + jnp.sin(angle)) / jnp.sqrt(jnp.float32(cols))


def inner(left, right):
    return jnp.sum(left * right, axis=(0, 1, 3))


def reduce_kernel(axis_names, stages, x_ref, o_ref, cur, recv, send_sem, recv_sem):
    me = {name: lax.axis_index(name) for name in axis_names}

    def device(axis, coord):
        return tuple(coord if name == axis else me[name] for name in axis_names)

    plan = []
    base = 0
    for axis, stride, size in stages:
        own = (me[axis] // stride) % size
        root = me[axis] - own * stride
        peers = []
        for step in range(1, size):
            other = lax.rem(own + step, size)
            peers.append((other, device(axis, root + other * stride)))
        plan.append((base, own, size, peers))
        base += size

    barrier = pltpu.get_barrier_semaphore()
    for _, _, _, peers in plan:
        for _, peer in peers:
            pl.semaphore_signal(barrier, 1, device_id=peer, device_id_type=MESH)
    pl.semaphore_wait(barrier, sum(len(peers) for _, _, _, peers in plan))

    acc = x_ref[...].astype(jnp.float32)
    for index, (base, own, size, peers) in enumerate(plan):
        cur[index] = acc.astype(cur.dtype)
        copies = []
        for other, peer in peers:
            copy = pltpu.make_async_remote_copy(
                src_ref=cur.at[index],
                dst_ref=recv.at[base + own],
                send_sem=send_sem.at[base + other],
                recv_sem=recv_sem.at[base + own],
                device_id=peer,
                device_id_type=MESH,
            )
            copy.start()
            copies.append(copy)
        recv[base + own] = acc.astype(recv.dtype)
        for other, peer in peers:
            pltpu.make_async_remote_copy(
                src_ref=cur.at[index],
                dst_ref=recv.at[base + other],
                send_sem=send_sem.at[base + other],
                recv_sem=recv_sem.at[base + other],
                device_id=peer,
                device_id_type=MESH,
            ).wait_recv()
        for copy in copies:
            copy.wait_send()
        total = recv[base].astype(jnp.float32)
        for slot in range(1, size):
            total = total + recv[base + slot].astype(jnp.float32)
        acc = total
    o_ref[...] = acc.astype(o_ref.dtype)


def group_sum(x, axis_names, stages, wire_dtype, collective_id):
    slots = sum(size for _, _, size in stages)
    return pl.pallas_call(
        functools.partial(reduce_kernel, axis_names, stages),
        out_shape=jax.ShapeDtypeStruct(x.shape, jnp.float32),
        in_specs=[pl.BlockSpec(memory_space=pltpu.VMEM)],
        out_specs=pl.BlockSpec(memory_space=pltpu.VMEM),
        scratch_shapes=[
            pltpu.VMEM((len(stages),) + x.shape, wire_dtype),
            pltpu.VMEM((slots,) + x.shape, wire_dtype),
            pltpu.SemaphoreType.DMA((slots,)),
            pltpu.SemaphoreType.DMA((slots,)),
        ],
        compiler_params=pltpu.CompilerParams(collective_id=collective_id, has_side_effects=True),
    )(x)


def column_sum(x):
    return jnp.sum(jnp.sum(x, axis=0), axis=1, keepdims=True)


def to_row(columns):
    count = columns[0].shape[0]
    sub = lax.broadcasted_iota(jnp.int32, (count, 128), 0)
    lane = lax.broadcasted_iota(jnp.int32, (count, 128), 1)
    acc = jnp.zeros((count, 128), jnp.float32)
    for index, column in enumerate(columns):
        acc = acc + jnp.where(lane == sub + count * index, jnp.broadcast_to(column, (count, 128)), 0.0)
    return jnp.sum(acc, axis=0, keepdims=True)


def from_row(row, index, count):
    sub = lax.broadcasted_iota(jnp.int32, (count, 128), 0)
    lane = lax.broadcasted_iota(jnp.int32, (count, 128), 1)
    picked = jnp.where(lane == sub + count * index, jnp.broadcast_to(row, (count, 128)), 0.0)
    return jnp.sum(picked, axis=1, keepdims=True)


def cg_kernel(first, axis_names, stages, *refs):
    if first:
        (d_ref, cb_ref, diag_ref, pm_ref, est_ref, next_ref, norm_ref,
         part, rows, recv_p, recv_rows, p_send, p_recv, r_send, r_recv) = refs
    else:
        (d_ref, cb_ref, diag_ref, pm_ref, est_in_ref, norm_in_ref, est_ref,
         part, rows, recv_p, recv_rows, p_send, p_recv, r_send, r_recv) = refs
    me = {name: lax.axis_index(name) for name in axis_names}

    def place(stage):
        axis, stride, size = stage
        own = lax.rem(me[axis] // stride, size)
        root = me[axis] - own * stride

        def device(other):
            return tuple(root + other * stride if name == axis else me[name] for name in axis_names)

        return own, device

    barrier = pltpu.get_barrier_semaphore()
    for stage in stages:
        own, device = place(stage)
        for step in range(1, stage[2]):
            other = lax.rem(own + step, stage[2])
            pl.semaphore_signal(barrier, 1, device_id=device(other), device_id_type=MESH)
    pl.semaphore_wait(barrier, sum(size - 1 for _, _, size in stages))

    def exchange_start(stage, src, recv, base, send_sems, recv_sems):
        own, device = place(stage)
        size = stage[2]

        def copy_to(other, slot):
            return pltpu.make_async_remote_copy(
                src_ref=src,
                dst_ref=recv.at[base + slot],
                send_sem=send_sems.at[base + other],
                recv_sem=recv_sems.at[base + slot],
                device_id=device(other),
                device_id_type=MESH,
            )

        for step in range(1, size):
            copy_to(lax.rem(own + step, size), own).start()
        recv[base + own] = src[...]
        return own, size, base, recv, copy_to

    def exchange_finish(state):
        own, size, base, recv, copy_to = state
        for step in range(1, size):
            other = lax.rem(own + step, size)
            copy_to(other, other).wait_recv()
        for step in range(1, size):
            copy_to(lax.rem(own + step, size), own).wait_send()
        total = recv[base]
        for slot in range(1, size):
            total = total + recv[base + slot]
        return total

    counter = {"row": 0, "slot": 0}

    def next_row(value):
        index = counter["row"]
        counter["row"] += 1
        rows[index] = value
        return rows.at[index]

    def row_stage(stage, src):
        base = counter["slot"]
        counter["slot"] += stage[2]
        return exchange_start(stage, src, recv_rows, base, r_send, r_recv)

    def reduce_rest(value):
        for stage in stages[1:]:
            value = exchange_finish(row_stage(stage, next_row(value)))
        return value

    d = d_ref[...]
    cb = cb_ref[...]
    diag = diag_ref[...]
    pm = pm_ref[...]
    count = d.shape[1]
    for rank in range(pm.shape[1]):
        part[rank] = jnp.sum(pm[:, rank] * d, axis=0)
    if first:
        row = to_row([column_sum(d * (cb + diag * d)), column_sum(d * d)])
    else:
        row = to_row([column_sum(d * (cb + diag * d))])
    p_state = exchange_start(stages[0], part, recv_p, 0, p_send, p_recv)
    z_state = row_stage(stages[0], next_row(row))
    projection = exchange_finish(p_state)
    zrow = exchange_finish(z_state)
    total = reduce_rest(zrow + to_row([column_sum(projection * projection)]))
    curve = from_row(total, 0, count)
    if first:
        norm_now = from_row(total, 1, count)
        step_size = (norm_now / curve)[None]
        est_ref[...] = step_size * d
        spread = pm[:, 0] * projection[0][None]
        for rank in range(1, pm.shape[1]):
            spread = spread + pm[:, rank] * projection[rank][None]
        image = cb + diag * d + spread
        residual = d - step_size * image
        row = to_row([column_sum(residual * residual)])
        zrow = exchange_finish(row_stage(stages[0], next_row(row)))
        total = reduce_rest(zrow)
        norm_next = from_row(total, 0, count)
        next_ref[...] = residual + (norm_next / norm_now)[None] * d
        norm_ref[...] = total
    else:
        norm_now = from_row(norm_in_ref[...], 0, count)
        est_ref[...] = est_in_ref[...] + (norm_now / curve)[None] * d


def cg_step(first, axis_names, stages, d, cb, diag, pm, *extra):
    reductions = 2 if first else 1
    slots = reductions * sum(size for _, _, size in stages)
    rounds = reductions * len(stages)
    nz = stages[0][2]
    vector = jax.ShapeDtypeStruct(d.shape, jnp.float32)
    row = jax.ShapeDtypeStruct((1, 128), jnp.float32)
    out_shape = (vector, vector, row) if first else vector
    vmem = pl.BlockSpec(memory_space=pltpu.VMEM)
    part_shape = (pm.shape[1],) + d.shape[1:]
    return pl.pallas_call(
        functools.partial(cg_kernel, first, axis_names, stages),
        out_shape=out_shape,
        in_specs=[vmem] * (4 + len(extra)),
        out_specs=(vmem, vmem, vmem) if first else vmem,
        scratch_shapes=[
            pltpu.VMEM(part_shape, jnp.float32),
            pltpu.VMEM((rounds, 1, 128), jnp.float32),
            pltpu.VMEM((nz,) + part_shape, jnp.float32),
            pltpu.VMEM((slots, 1, 128), jnp.float32),
            pltpu.SemaphoreType.DMA((nz,)),
            pltpu.SemaphoreType.DMA((nz,)),
            pltpu.SemaphoreType.DMA((slots,)),
            pltpu.SemaphoreType.DMA((slots,)),
        ],
        compiler_params=pltpu.CompilerParams(
            collective_id=1 if first else 2, has_side_effects=True
        ),
    )(d, cb, diag, pm, *extra)


def make_shards(mesh):
    axis_names = tuple(mesh.axis_names)
    mode_devices = mesh.shape["ma"]
    freq_devices = mesh.shape["freq"]
    if mode_devices % 16 == 0:
        mode_stages = [("ma", 1, 2), ("ma", 2, 8), ("ma", 16, mode_devices // 16)]
    else:
        mode_stages = [("ma", 1, mode_devices)]
    global_stages = mode_stages + [("freq", 1, freq_devices)]
    freq_stages = [("freq", 1, freq_devices)]

    def scalar_sum(*vectors):
        rows = jnp.stack(vectors)
        padded = jnp.pad(rows, ((0, 8 - rows.shape[0]), (0, 128 - rows.shape[1])))
        summed = group_sum(padded, axis_names, global_stages, jnp.float32, 2)
        return [summed[index, : rows.shape[1]] for index in range(len(vectors))]

    def freq_sum(partial_sum):
        shape = partial_sum.shape
        flat = partial_sum.reshape(-1, shape[-1])
        summed = group_sum(flat, axis_names, freq_stages, jnp.bfloat16, 1)
        return summed.reshape(shape)

    def shards(timestream, beam_transfer, chromatic_gain, noise_weight, prior_diagonal, prior_modes):
        spectral_channels = timestream.shape[0]
        device_time_samples = timestream.shape[1]
        noise_realizations = timestream.shape[2]
        antenna_pairs = timestream.shape[3]
        mode_devices_here = mode_devices
        columns = noise_realizations * antenna_pairs // mode_devices_here
        blocks = antenna_pairs // columns
        halves = columns // 128
        send = timestream.reshape(
            spectral_channels, device_time_samples, noise_realizations, blocks, halves, 128
        ).transpose(2, 3, 0, 1, 4, 5)
        send = send.reshape(mode_devices_here, spectral_channels * device_time_samples * halves, 128)
        received = lax.all_to_all(send, "ma", 0, 0, tiled=True)
        received = received.reshape(mode_devices_here, spectral_channels, device_time_samples, columns)
        all_times = mode_devices_here * device_time_samples
        hartley = hartley_table(all_times // 2, all_times)
        hartley_high = hartley.astype(jnp.bfloat16)
        hartley_low = (hartley - hartley_high.astype(jnp.float32)).astype(jnp.bfloat16)
        hartley_high = hartley_high.reshape(all_times // 2, mode_devices_here, device_time_samples)
        hartley_low = hartley_low.reshape(all_times // 2, mode_devices_here, device_time_samples)
        mode_high = jnp.einsum(
            "mit,iftc->mfc", hartley_high, received, preferred_element_type=jnp.float32
        )
        mode_low = jnp.einsum("mit,iftc->mfc", hartley_low, received, preferred_element_type=jnp.float32)
        mode_rows = (mode_high + mode_low).astype(jnp.bfloat16)
        back_rows = lax.all_to_all(mode_rows, "ma", 0, 0, tiled=True)
        resident_modes = back_rows.shape[0] // mode_devices_here
        back_rows = back_rows.reshape(
            noise_realizations, blocks, resident_modes, spectral_channels, columns
        )
        measured_visibility = back_rows.transpose(3, 2, 0, 1, 4).reshape(
            spectral_channels, resident_modes, noise_realizations, antenna_pairs
        )
        chroma = chromatic_gain[:, None, None, :]
        diagonal = prior_diagonal[:, None, None, :]
        weighted = (noise_weight[:, :, None, :] * measured_visibility.astype(jnp.float32)).astype(
            jnp.bfloat16
        )
        rhs = chroma * jnp.einsum(
            "fmkb,mbs->fmks", weighted, beam_transfer, preferred_element_type=jnp.float32
        )

        assert resident_modes == 1
        cg_stages = [("freq", 1, freq_devices)] + mode_stages
        diag_rows = prior_diagonal[:, None, :]
        mode_rows4 = prior_modes[:, :, None, :]

        def beam_back(direction):
            low = (chroma * direction).astype(jnp.bfloat16)
            seen = jnp.einsum("fmks,mbs->fmkb", low, beam_transfer, preferred_element_type=jnp.float32)
            heard = (noise_weight[:, :, None, :] * seen).astype(jnp.bfloat16)
            back = jnp.einsum(
                "fmkb,mbs->fmks", heard, beam_transfer, preferred_element_type=jnp.float32
            )
            return (chroma * back)[:, 0]

        direction = rhs[:, 0]
        estimate, direction, norm_row = cg_step(
            True, axis_names, cg_stages, direction, beam_back(direction[:, None]), diag_rows, mode_rows4
        )
        estimate = cg_step(
            False, axis_names, cg_stages, direction, beam_back(direction[:, None]), diag_rows, mode_rows4,
            estimate, norm_row,
        )
        estimate = estimate[:, None]
        return estimate

    return shards


def solution(mesh):
    in_specs = (
        P("freq", "ma", None, None),
        P("ma", None, None),
        P("freq", None),
        P("freq", "ma", None),
        P("freq", None),
        P("freq", None, None),
    )
    out_specs = P("freq", "ma", None, None)
    return jax.shard_map(make_shards(mesh), mesh=mesh, in_specs=in_specs, out_specs=out_specs, check_vma=False)
```

```python
import functools

import jax
import jax.numpy as jnp
from jax import lax
from jax.experimental import pallas as pl
from jax.experimental.pallas import tpu as pltpu
from jax.sharding import PartitionSpec as P

ITERS = 2
MESH = pl.DeviceIdType.MESH


def hartley_table(rows, cols):
    index_m = jnp.arange(rows, dtype=jnp.int32)[:, None]
    index_t = jnp.arange(cols, dtype=jnp.int32)[None, :]
    phase = (index_m * index_t % cols).astype(jnp.float32)
    angle = 2.0 * jnp.pi * phase / cols
    return (jnp.cos(angle) + jnp.sin(angle)) / jnp.sqrt(jnp.float32(cols))


def inner(left, right):
    return jnp.sum(left * right, axis=(0, 1, 3))


def reduce_kernel(axis_names, stages, x_ref, o_ref, cur, recv, send_sem, recv_sem):
    me = {name: lax.axis_index(name) for name in axis_names}

    def device(axis, coord):
        return tuple(coord if name == axis else me[name] for name in axis_names)

    plan = []
    base = 0
    for axis, stride, size in stages:
        own = (me[axis] // stride) % size
        root = me[axis] - own * stride
        peers = []
        for step in range(1, size):
            other = lax.rem(own + step, size)
            peers.append((other, device(axis, root + other * stride)))
        plan.append((base, own, size, peers))
        base += size

    barrier = pltpu.get_barrier_semaphore()
    for _, _, _, peers in plan:
        for _, peer in peers:
            pl.semaphore_signal(barrier, 1, device_id=peer, device_id_type=MESH)
    pl.semaphore_wait(barrier, sum(len(peers) for _, _, _, peers in plan))

    acc = x_ref[...].astype(jnp.float32)
    for index, (base, own, size, peers) in enumerate(plan):
        cur[index] = acc.astype(cur.dtype)
        copies = []
        for other, peer in peers:
            copy = pltpu.make_async_remote_copy(
                src_ref=cur.at[index],
                dst_ref=recv.at[base + own],
                send_sem=send_sem.at[base + other],
                recv_sem=recv_sem.at[base + own],
                device_id=peer,
                device_id_type=MESH,
            )
            copy.start()
            copies.append(copy)
        recv[base + own] = acc.astype(recv.dtype)
        for other, peer in peers:
            pltpu.make_async_remote_copy(
                src_ref=cur.at[index],
                dst_ref=recv.at[base + other],
                send_sem=send_sem.at[base + other],
                recv_sem=recv_sem.at[base + other],
                device_id=peer,
                device_id_type=MESH,
            ).wait_recv()
        for copy in copies:
            copy.wait_send()
        total = recv[base].astype(jnp.float32)
        for slot in range(1, size):
            total = total + recv[base + slot].astype(jnp.float32)
        acc = total
    o_ref[...] = acc.astype(o_ref.dtype)


def group_sum(x, axis_names, stages, wire_dtype, collective_id):
    slots = sum(size for _, _, size in stages)
    return pl.pallas_call(
        functools.partial(reduce_kernel, axis_names, stages),
        out_shape=jax.ShapeDtypeStruct(x.shape, jnp.float32),
        in_specs=[pl.BlockSpec(memory_space=pltpu.VMEM)],
        out_specs=pl.BlockSpec(memory_space=pltpu.VMEM),
        scratch_shapes=[
            pltpu.VMEM((len(stages),) + x.shape, wire_dtype),
            pltpu.VMEM((slots,) + x.shape, wire_dtype),
            pltpu.SemaphoreType.DMA((slots,)),
            pltpu.SemaphoreType.DMA((slots,)),
        ],
        compiler_params=pltpu.CompilerParams(collective_id=collective_id, has_side_effects=True),
    )(x)


def column_sum(x):
    return jnp.sum(jnp.sum(x, axis=0), axis=1, keepdims=True)


def to_row(columns):
    count = columns[0].shape[0]
    sub = lax.broadcasted_iota(jnp.int32, (count, 128), 0)
    lane = lax.broadcasted_iota(jnp.int32, (count, 128), 1)
    acc = jnp.zeros((count, 128), jnp.float32)
    for index, column in enumerate(columns):
        acc = acc + jnp.where(lane == sub + count * index, jnp.broadcast_to(column, (count, 128)), 0.0)
    return jnp.sum(acc, axis=0, keepdims=True)


def from_row(row, index, count):
    sub = lax.broadcasted_iota(jnp.int32, (count, 128), 0)
    lane = lax.broadcasted_iota(jnp.int32, (count, 128), 1)
    picked = jnp.where(lane == sub + count * index, jnp.broadcast_to(row, (count, 128)), 0.0)
    return jnp.sum(picked, axis=1, keepdims=True)


def cg_kernel(first, axis_names, stages, *refs):
    if first:
        (d_ref, cb_ref, diag_ref, pm_ref, est_ref, next_ref, norm_ref,
         part, rows, recv_p, recv_rows, p_send, p_recv, r_send, r_recv) = refs
    else:
        (d_ref, cb_ref, diag_ref, pm_ref, est_in_ref, norm_in_ref, est_ref,
         part, rows, recv_p, recv_rows, p_send, p_recv, r_send, r_recv) = refs
    me = {name: lax.axis_index(name) for name in axis_names}

    def place(stage):
        axis, stride, size = stage
        own = lax.rem(me[axis] // stride, size)
        root = me[axis] - own * stride

        def device(other):
            return tuple(root + other * stride if name == axis else me[name] for name in axis_names)

        return own, device

    barrier = pltpu.get_barrier_semaphore()
    for stage in stages:
        own, device = place(stage)
        for step in range(1, stage[2]):
            other = lax.rem(own + step, stage[2])
            pl.semaphore_signal(barrier, 1, device_id=device(other), device_id_type=MESH)
    pl.semaphore_wait(barrier, sum(size - 1 for _, _, size in stages))

    def exchange_start(stage, src, recv, base, send_sems, recv_sems):
        own, device = place(stage)
        size = stage[2]

        def copy_to(other, slot):
            return pltpu.make_async_remote_copy(
                src_ref=src,
                dst_ref=recv.at[base + slot],
                send_sem=send_sems.at[base + other],
                recv_sem=recv_sems.at[base + slot],
                device_id=device(other),
                device_id_type=MESH,
            )

        for step in range(1, size):
            copy_to(lax.rem(own + step, size), own).start()
        recv[base + own] = src[...]
        return own, size, base, recv, copy_to

    sent = []

    def exchange_finish(state):
        own, size, base, recv, copy_to = state
        for step in range(1, size):
            other = lax.rem(own + step, size)
            copy_to(other, other).wait_recv()
        sent.append(state)
        total = recv[base]
        for slot in range(1, size):
            total = total + recv[base + slot]
        return total

    counter = {"row": 0, "slot": 0}

    def next_row(value):
        index = counter["row"]
        counter["row"] += 1
        rows[index] = value
        return rows.at[index]

    def row_stage(stage, src):
        base = counter["slot"]
        counter["slot"] += stage[2]
        return exchange_start(stage, src, recv_rows, base, r_send, r_recv)

    def reduce_rest(value):
        for stage in stages[1:]:
            value = exchange_finish(row_stage(stage, next_row(value)))
        return value

    d = d_ref[...]
    cb = cb_ref[...]
    diag = diag_ref[...]
    pm = pm_ref[...]
    count = d.shape[1]
    for rank in range(pm.shape[1]):
        part[rank] = jnp.sum(pm[:, rank] * d, axis=0)
    if first:
        row = to_row([column_sum(d * (cb + diag * d)), column_sum(d * d)])
    else:
        row = to_row([column_sum(d * (cb + diag * d))])
    p_state = exchange_start(stages[0], part, recv_p, 0, p_send, p_recv)
    z_state = row_stage(stages[0], next_row(row))
    projection = exchange_finish(p_state)
    zrow = exchange_finish(z_state)
    total = reduce_rest(zrow + to_row([column_sum(projection * projection)]))
    curve = from_row(total, 0, count)
    if first:
        norm_now = from_row(total, 1, count)
        step_size = (norm_now / curve)[None]
        est_ref[...] = step_size * d
        spread = pm[:, 0] * projection[0][None]
        for rank in range(1, pm.shape[1]):
            spread = spread + pm[:, rank] * projection[rank][None]
        image = cb + diag * d + spread
        residual = d - step_size * image
        row = to_row([column_sum(residual * residual)])
        zrow = exchange_finish(row_stage(stages[0], next_row(row)))
        total = reduce_rest(zrow)
        norm_next = from_row(total, 0, count)
        next_ref[...] = residual + (norm_next / norm_now)[None] * d
        norm_ref[...] = total
    else:
        norm_now = from_row(norm_in_ref[...], 0, count)
        est_ref[...] = est_in_ref[...] + (norm_now / curve)[None] * d
    for own, size, _, _, copy_to in sent:
        for step in range(1, size):
            copy_to(lax.rem(own + step, size), own).wait_send()


def cg_step(first, axis_names, stages, d, cb, diag, pm, *extra):
    reductions = 2 if first else 1
    slots = reductions * sum(size for _, _, size in stages)
    rounds = reductions * len(stages)
    nz = stages[0][2]
    vector = jax.ShapeDtypeStruct(d.shape, jnp.float32)
    row = jax.ShapeDtypeStruct((1, 128), jnp.float32)
    out_shape = (vector, vector, row) if first else vector
    vmem = pl.BlockSpec(memory_space=pltpu.VMEM)
    part_shape = (pm.shape[1],) + d.shape[1:]
    return pl.pallas_call(
        functools.partial(cg_kernel, first, axis_names, stages),
        out_shape=out_shape,
        in_specs=[vmem] * (4 + len(extra)),
        out_specs=(vmem, vmem, vmem) if first else vmem,
        scratch_shapes=[
            pltpu.VMEM(part_shape, jnp.float32),
            pltpu.VMEM((rounds, 1, 128), jnp.float32),
            pltpu.VMEM((nz,) + part_shape, jnp.float32),
            pltpu.VMEM((slots, 1, 128), jnp.float32),
            pltpu.SemaphoreType.DMA((nz,)),
            pltpu.SemaphoreType.DMA((nz,)),
            pltpu.SemaphoreType.DMA((slots,)),
            pltpu.SemaphoreType.DMA((slots,)),
        ],
        compiler_params=pltpu.CompilerParams(
            collective_id=1 if first else 2, has_side_effects=True
        ),
    )(d, cb, diag, pm, *extra)


def make_shards(mesh):
    axis_names = tuple(mesh.axis_names)
    mode_devices = mesh.shape["ma"]
    freq_devices = mesh.shape["freq"]
    if mode_devices % 16 == 0:
        mode_stages = [("ma", 1, 2), ("ma", 2, 8), ("ma", 16, mode_devices // 16)]
    else:
        mode_stages = [("ma", 1, mode_devices)]
    global_stages = mode_stages + [("freq", 1, freq_devices)]
    freq_stages = [("freq", 1, freq_devices)]

    def scalar_sum(*vectors):
        rows = jnp.stack(vectors)
        padded = jnp.pad(rows, ((0, 8 - rows.shape[0]), (0, 128 - rows.shape[1])))
        summed = group_sum(padded, axis_names, global_stages, jnp.float32, 2)
        return [summed[index, : rows.shape[1]] for index in range(len(vectors))]

    def freq_sum(partial_sum):
        shape = partial_sum.shape
        flat = partial_sum.reshape(-1, shape[-1])
        summed = group_sum(flat, axis_names, freq_stages, jnp.bfloat16, 1)
        return summed.reshape(shape)

    def shards(timestream, beam_transfer, chromatic_gain, noise_weight, prior_diagonal, prior_modes):
        spectral_channels = timestream.shape[0]
        device_time_samples = timestream.shape[1]
        noise_realizations = timestream.shape[2]
        antenna_pairs = timestream.shape[3]
        mode_devices_here = mode_devices
        columns = noise_realizations * antenna_pairs // mode_devices_here
        blocks = antenna_pairs // columns
        halves = columns // 128
        send = timestream.reshape(
            spectral_channels, device_time_samples, noise_realizations, blocks, halves, 128
        ).transpose(2, 3, 0, 1, 4, 5)
        send = send.reshape(mode_devices_here, spectral_channels * device_time_samples * halves, 128)
        received = lax.all_to_all(send, "ma", 0, 0, tiled=True)
        received = received.reshape(mode_devices_here, spectral_channels, device_time_samples, columns)
        all_times = mode_devices_here * device_time_samples
        hartley = hartley_table(all_times // 2, all_times)
        hartley_high = hartley.astype(jnp.bfloat16)
        hartley_low = (hartley - hartley_high.astype(jnp.float32)).astype(jnp.bfloat16)
        hartley_high = hartley_high.reshape(all_times // 2, mode_devices_here, device_time_samples)
        hartley_low = hartley_low.reshape(all_times // 2, mode_devices_here, device_time_samples)
        mode_high = jnp.einsum(
            "mit,iftc->mfc", hartley_high, received, preferred_element_type=jnp.float32
        )
        mode_low = jnp.einsum("mit,iftc->mfc", hartley_low, received, preferred_element_type=jnp.float32)
        mode_rows = (mode_high + mode_low).astype(jnp.bfloat16)
        back_rows = lax.all_to_all(mode_rows, "ma", 0, 0, tiled=True)
        resident_modes = back_rows.shape[0] // mode_devices_here
        back_rows = back_rows.reshape(
            noise_realizations, blocks, resident_modes, spectral_channels, columns
        )
        measured_visibility = back_rows.transpose(3, 2, 0, 1, 4).reshape(
            spectral_channels, resident_modes, noise_realizations, antenna_pairs
        )
        chroma = chromatic_gain[:, None, None, :]
        diagonal = prior_diagonal[:, None, None, :]
        weighted = (noise_weight[:, :, None, :] * measured_visibility.astype(jnp.float32)).astype(
            jnp.bfloat16
        )
        rhs = chroma * jnp.einsum(
            "fmkb,mbs->fmks", weighted, beam_transfer, preferred_element_type=jnp.float32
        )

        assert resident_modes == 1
        cg_stages = [("freq", 1, freq_devices)] + mode_stages
        diag_rows = prior_diagonal[:, None, :]
        mode_rows4 = prior_modes[:, :, None, :]

        def beam_back(direction):
            low = (chroma * direction).astype(jnp.bfloat16)
            seen = jnp.einsum("fmks,mbs->fmkb", low, beam_transfer, preferred_element_type=jnp.float32)
            heard = (noise_weight[:, :, None, :] * seen).astype(jnp.bfloat16)
            back = jnp.einsum(
                "fmkb,mbs->fmks", heard, beam_transfer, preferred_element_type=jnp.float32
            )
            return (chroma * back)[:, 0]

        direction = rhs[:, 0]
        estimate, direction, norm_row = cg_step(
            True, axis_names, cg_stages, direction, beam_back(direction[:, None]), diag_rows, mode_rows4
        )
        estimate = cg_step(
            False, axis_names, cg_stages, direction, beam_back(direction[:, None]), diag_rows, mode_rows4,
            estimate, norm_row,
        )
        estimate = estimate[:, None]
        return estimate

    return shards


def solution(mesh):
    in_specs = (
        P("freq", "ma", None, None),
        P("ma", None, None),
        P("freq", None),
        P("freq", "ma", None),
        P("freq", None),
        P("freq", None, None),
    )
    out_specs = P("freq", "ma", None, None)
    return jax.shard_map(make_shards(mesh), mesh=mesh, in_specs=in_specs, out_specs=out_specs, check_vma=False)
```

```python
import functools

import jax
import jax.numpy as jnp
from jax import lax
from jax.experimental import pallas as pl
from jax.experimental.pallas import tpu as pltpu
from jax.sharding import PartitionSpec as P

ITERS = 2
MESH = pl.DeviceIdType.MESH


def hartley_table(rows, cols):
    index_m = jnp.arange(rows, dtype=jnp.int32)[:, None]
    index_t = jnp.arange(cols, dtype=jnp.int32)[None, :]
    phase = (index_m * index_t % cols).astype(jnp.float32)
    angle = 2.0 * jnp.pi * phase / cols
    return (jnp.cos(angle) + jnp.sin(angle)) / jnp.sqrt(jnp.float32(cols))


def inner(left, right):
    return jnp.sum(left * right, axis=(0, 1, 3))


def reduce_kernel(axis_names, stages, x_ref, o_ref, cur, recv, send_sem, recv_sem):
    me = {name: lax.axis_index(name) for name in axis_names}

    def device(axis, coord):
        return tuple(coord if name == axis else me[name] for name in axis_names)

    plan = []
    base = 0
    for axis, stride, size in stages:
        own = (me[axis] // stride) % size
        root = me[axis] - own * stride
        peers = []
        for step in range(1, size):
            other = lax.rem(own + step, size)
            peers.append((other, device(axis, root + other * stride)))
        plan.append((base, own, size, peers))
        base += size

    barrier = pltpu.get_barrier_semaphore()
    for _, _, _, peers in plan:
        for _, peer in peers:
            pl.semaphore_signal(barrier, 1, device_id=peer, device_id_type=MESH)
    pl.semaphore_wait(barrier, sum(len(peers) for _, _, _, peers in plan))

    acc = x_ref[...].astype(jnp.float32)
    for index, (base, own, size, peers) in enumerate(plan):
        cur[index] = acc.astype(cur.dtype)
        copies = []
        for other, peer in peers:
            copy = pltpu.make_async_remote_copy(
                src_ref=cur.at[index],
                dst_ref=recv.at[base + own],
                send_sem=send_sem.at[base + other],
                recv_sem=recv_sem.at[base + own],
                device_id=peer,
                device_id_type=MESH,
            )
            copy.start()
            copies.append(copy)
        recv[base + own] = acc.astype(recv.dtype)
        for other, peer in peers:
            pltpu.make_async_remote_copy(
                src_ref=cur.at[index],
                dst_ref=recv.at[base + other],
                send_sem=send_sem.at[base + other],
                recv_sem=recv_sem.at[base + other],
                device_id=peer,
                device_id_type=MESH,
            ).wait_recv()
        for copy in copies:
            copy.wait_send()
        total = recv[base].astype(jnp.float32)
        for slot in range(1, size):
            total = total + recv[base + slot].astype(jnp.float32)
        acc = total
    o_ref[...] = acc.astype(o_ref.dtype)


def group_sum(x, axis_names, stages, wire_dtype, collective_id):
    slots = sum(size for _, _, size in stages)
    return pl.pallas_call(
        functools.partial(reduce_kernel, axis_names, stages),
        out_shape=jax.ShapeDtypeStruct(x.shape, jnp.float32),
        in_specs=[pl.BlockSpec(memory_space=pltpu.VMEM)],
        out_specs=pl.BlockSpec(memory_space=pltpu.VMEM),
        scratch_shapes=[
            pltpu.VMEM((len(stages),) + x.shape, wire_dtype),
            pltpu.VMEM((slots,) + x.shape, wire_dtype),
            pltpu.SemaphoreType.DMA((slots,)),
            pltpu.SemaphoreType.DMA((slots,)),
        ],
        compiler_params=pltpu.CompilerParams(collective_id=collective_id, has_side_effects=True),
    )(x)


def column_sum(x):
    return jnp.sum(jnp.sum(x, axis=0), axis=1, keepdims=True)


def to_row(columns):
    count = columns[0].shape[0]
    sub = lax.broadcasted_iota(jnp.int32, (count, 128), 0)
    lane = lax.broadcasted_iota(jnp.int32, (count, 128), 1)
    acc = jnp.zeros((count, 128), jnp.float32)
    for index, column in enumerate(columns):
        acc = acc + jnp.where(lane == sub + count * index, jnp.broadcast_to(column, (count, 128)), 0.0)
    return jnp.sum(acc, axis=0, keepdims=True)


def from_row(row, index, count):
    sub = lax.broadcasted_iota(jnp.int32, (count, 128), 0)
    lane = lax.broadcasted_iota(jnp.int32, (count, 128), 1)
    picked = jnp.where(lane == sub + count * index, jnp.broadcast_to(row, (count, 128)), 0.0)
    return jnp.sum(picked, axis=1, keepdims=True)


def group_size(stage):
    size = 1
    for _, extent in stage[1]:
        size *= extent
    return size


def cg_kernel(first, axis_names, stages, *refs):
    if first:
        (d_ref, cb_ref, diag_ref, pm_ref, est_ref, next_ref, norm_ref,
         part, rows, recv_p, recv_rows, p_send, p_recv, r_send, r_recv) = refs
    else:
        (d_ref, cb_ref, diag_ref, pm_ref, est_in_ref, norm_in_ref, est_ref,
         part, rows, recv_p, recv_rows, p_send, p_recv, r_send, r_recv) = refs
    me = {name: lax.axis_index(name) for name in axis_names}

    def place(stage):
        axis, dims = stage
        own = 0
        root = me[axis]
        scale = 1
        for stride, size in dims:
            digit = lax.rem(me[axis] // stride, size)
            own = own + digit * scale
            root = root - digit * stride
            scale *= size

        def device(other):
            coord = root
            scale = 1
            for stride, size in dims:
                coord = coord + lax.rem(other // scale, size) * stride
                scale *= size
            return tuple(coord if name == axis else me[name] for name in axis_names)

        return own, device

    barrier = pltpu.get_barrier_semaphore()
    for stage in stages:
        own, device = place(stage)
        for step in range(1, group_size(stage)):
            other = lax.rem(own + step, group_size(stage))
            pl.semaphore_signal(barrier, 1, device_id=device(other), device_id_type=MESH)
    pl.semaphore_wait(barrier, sum(group_size(stage) - 1 for stage in stages))

    def exchange_start(stage, src, recv, base, send_sems, recv_sems):
        own, device = place(stage)
        size = group_size(stage)

        def copy_to(other, slot):
            return pltpu.make_async_remote_copy(
                src_ref=src,
                dst_ref=recv.at[base + slot],
                send_sem=send_sems.at[base + other],
                recv_sem=recv_sems.at[base + slot],
                device_id=device(other),
                device_id_type=MESH,
            )

        for step in range(1, size):
            copy_to(lax.rem(own + step, size), own).start()
        recv[base + own] = src[...]
        return own, size, base, recv, copy_to

    sent = []

    def exchange_finish(state):
        own, size, base, recv, copy_to = state
        for step in range(1, size):
            other = lax.rem(own + step, size)
            copy_to(other, other).wait_recv()
        sent.append(state)
        total = recv[base]
        for slot in range(1, size):
            total = total + recv[base + slot]
        return total

    counter = {"row": 0, "slot": 0}

    def next_row(value):
        index = counter["row"]
        counter["row"] += 1
        rows[index] = value
        return rows.at[index]

    def row_stage(stage, src):
        base = counter["slot"]
        counter["slot"] += group_size(stage)
        return exchange_start(stage, src, recv_rows, base, r_send, r_recv)

    def reduce_rest(value):
        for stage in stages[1:]:
            value = exchange_finish(row_stage(stage, next_row(value)))
        return value

    d = d_ref[...]
    cb = cb_ref[...]
    diag = diag_ref[...]
    pm = pm_ref[...]
    count = d.shape[1]
    for rank in range(pm.shape[1]):
        part[rank] = jnp.sum(pm[:, rank] * d, axis=0)
    if first:
        row = to_row([column_sum(d * (cb + diag * d)), column_sum(d * d)])
    else:
        row = to_row([column_sum(d * (cb + diag * d))])
    p_state = exchange_start(stages[0], part, recv_p, 0, p_send, p_recv)
    z_state = row_stage(stages[0], next_row(row))
    projection = exchange_finish(p_state)
    zrow = exchange_finish(z_state)
    total = reduce_rest(zrow + to_row([column_sum(projection * projection)]))
    curve = from_row(total, 0, count)
    if first:
        norm_now = from_row(total, 1, count)
        step_size = (norm_now / curve)[None]
        est_ref[...] = step_size * d
        spread = pm[:, 0] * projection[0][None]
        for rank in range(1, pm.shape[1]):
            spread = spread + pm[:, rank] * projection[rank][None]
        image = cb + diag * d + spread
        residual = d - step_size * image
        row = to_row([column_sum(residual * residual)])
        zrow = exchange_finish(row_stage(stages[0], next_row(row)))
        total = reduce_rest(zrow)
        norm_next = from_row(total, 0, count)
        next_ref[...] = residual + (norm_next / norm_now)[None] * d
        norm_ref[...] = total
    else:
        norm_now = from_row(norm_in_ref[...], 0, count)
        est_ref[...] = est_in_ref[...] + (norm_now / curve)[None] * d
    for own, size, _, _, copy_to in sent:
        for step in range(1, size):
            copy_to(lax.rem(own + step, size), own).wait_send()


def cg_step(first, axis_names, stages, d, cb, diag, pm, *extra):
    reductions = 2 if first else 1
    slots = reductions * sum(group_size(stage) for stage in stages)
    rounds = reductions * len(stages)
    nz = group_size(stages[0])
    vector = jax.ShapeDtypeStruct(d.shape, jnp.float32)
    row = jax.ShapeDtypeStruct((1, 128), jnp.float32)
    out_shape = (vector, vector, row) if first else vector
    vmem = pl.BlockSpec(memory_space=pltpu.VMEM)
    part_shape = (pm.shape[1],) + d.shape[1:]
    return pl.pallas_call(
        functools.partial(cg_kernel, first, axis_names, stages),
        out_shape=out_shape,
        in_specs=[vmem] * (4 + len(extra)),
        out_specs=(vmem, vmem, vmem) if first else vmem,
        scratch_shapes=[
            pltpu.VMEM(part_shape, jnp.float32),
            pltpu.VMEM((rounds, 1, 128), jnp.float32),
            pltpu.VMEM((nz,) + part_shape, jnp.float32),
            pltpu.VMEM((slots, 1, 128), jnp.float32),
            pltpu.SemaphoreType.DMA((nz,)),
            pltpu.SemaphoreType.DMA((nz,)),
            pltpu.SemaphoreType.DMA((slots,)),
            pltpu.SemaphoreType.DMA((slots,)),
        ],
        compiler_params=pltpu.CompilerParams(
            collective_id=1 if first else 2, has_side_effects=True
        ),
    )(d, cb, diag, pm, *extra)


def make_shards(mesh):
    axis_names = tuple(mesh.axis_names)
    mode_devices = mesh.shape["ma"]
    freq_devices = mesh.shape["freq"]
    if mode_devices % 16 == 0:
        mode_stages = [("ma", 1, 2), ("ma", 2, 8), ("ma", 16, mode_devices // 16)]
    else:
        mode_stages = [("ma", 1, mode_devices)]
    global_stages = mode_stages + [("freq", 1, freq_devices)]
    freq_stages = [("freq", 1, freq_devices)]

    def scalar_sum(*vectors):
        rows = jnp.stack(vectors)
        padded = jnp.pad(rows, ((0, 8 - rows.shape[0]), (0, 128 - rows.shape[1])))
        summed = group_sum(padded, axis_names, global_stages, jnp.float32, 2)
        return [summed[index, : rows.shape[1]] for index in range(len(vectors))]

    def freq_sum(partial_sum):
        shape = partial_sum.shape
        flat = partial_sum.reshape(-1, shape[-1])
        summed = group_sum(flat, axis_names, freq_stages, jnp.bfloat16, 1)
        return summed.reshape(shape)

    def shards(timestream, beam_transfer, chromatic_gain, noise_weight, prior_diagonal, prior_modes):
        spectral_channels = timestream.shape[0]
        device_time_samples = timestream.shape[1]
        noise_realizations = timestream.shape[2]
        antenna_pairs = timestream.shape[3]
        mode_devices_here = mode_devices
        columns = noise_realizations * antenna_pairs // mode_devices_here
        blocks = antenna_pairs // columns
        halves = columns // 128
        send = timestream.reshape(
            spectral_channels, device_time_samples, noise_realizations, blocks, halves, 128
        ).transpose(2, 3, 0, 1, 4, 5)
        send = send.reshape(mode_devices_here, spectral_channels * device_time_samples * halves, 128)
        received = lax.all_to_all(send, "ma", 0, 0, tiled=True)
        received = received.reshape(mode_devices_here, spectral_channels, device_time_samples, columns)
        all_times = mode_devices_here * device_time_samples
        hartley = hartley_table(all_times // 2, all_times)
        hartley_high = hartley.astype(jnp.bfloat16)
        hartley_low = (hartley - hartley_high.astype(jnp.float32)).astype(jnp.bfloat16)
        hartley_high = hartley_high.reshape(all_times // 2, mode_devices_here, device_time_samples)
        hartley_low = hartley_low.reshape(all_times // 2, mode_devices_here, device_time_samples)
        mode_high = jnp.einsum(
            "mit,iftc->mfc", hartley_high, received, preferred_element_type=jnp.float32
        )
        mode_low = jnp.einsum("mit,iftc->mfc", hartley_low, received, preferred_element_type=jnp.float32)
        mode_rows = (mode_high + mode_low).astype(jnp.bfloat16)
        back_rows = lax.all_to_all(mode_rows, "ma", 0, 0, tiled=True)
        resident_modes = back_rows.shape[0] // mode_devices_here
        back_rows = back_rows.reshape(
            noise_realizations, blocks, resident_modes, spectral_channels, columns
        )
        measured_visibility = back_rows.transpose(3, 2, 0, 1, 4).reshape(
            spectral_channels, resident_modes, noise_realizations, antenna_pairs
        )
        chroma = chromatic_gain[:, None, None, :]
        diagonal = prior_diagonal[:, None, None, :]
        weighted = (noise_weight[:, :, None, :] * measured_visibility.astype(jnp.float32)).astype(
            jnp.bfloat16
        )
        rhs = chroma * jnp.einsum(
            "fmkb,mbs->fmks", weighted, beam_transfer, preferred_element_type=jnp.float32
        )

        assert resident_modes == 1
        if mode_devices % 16 == 0:
            cg_stages = [
                ("freq", [(1, freq_devices)]),
                ("ma", [(1, 2), (16, mode_devices // 16)]),
                ("ma", [(2, 8)]),
            ]
        else:
            cg_stages = [("freq", [(1, freq_devices)]), ("ma", [(1, mode_devices)])]
        diag_rows = prior_diagonal[:, None, :]
        mode_rows4 = prior_modes[:, :, None, :]

        def beam_back(direction):
            low = (chroma * direction).astype(jnp.bfloat16)
            seen = jnp.einsum("fmks,mbs->fmkb", low, beam_transfer, preferred_element_type=jnp.float32)
            heard = (noise_weight[:, :, None, :] * seen).astype(jnp.bfloat16)
            back = jnp.einsum(
                "fmkb,mbs->fmks", heard, beam_transfer, preferred_element_type=jnp.float32
            )
            return (chroma * back)[:, 0]

        direction = rhs[:, 0]
        estimate, direction, norm_row = cg_step(
            True, axis_names, cg_stages, direction, beam_back(direction[:, None]), diag_rows, mode_rows4
        )
        estimate = cg_step(
            False, axis_names, cg_stages, direction, beam_back(direction[:, None]), diag_rows, mode_rows4,
            estimate, norm_row,
        )
        estimate = estimate[:, None]
        return estimate

    return shards


def solution(mesh):
    in_specs = (
        P("freq", "ma", None, None),
        P("ma", None, None),
        P("freq", None),
        P("freq", "ma", None),
        P("freq", None),
        P("freq", None, None),
    )
    out_specs = P("freq", "ma", None, None)
    return jax.shard_map(make_shards(mesh), mesh=mesh, in_specs=in_specs, out_specs=out_specs, check_vma=False)
```

```python
import functools

import jax
import jax.numpy as jnp
from jax import lax
from jax.experimental import pallas as pl
from jax.experimental.pallas import tpu as pltpu
from jax.sharding import PartitionSpec as P

ITERS = 2
MESH = pl.DeviceIdType.MESH


def hartley_table(rows, cols):
    index_m = jnp.arange(rows, dtype=jnp.int32)[:, None]
    index_t = jnp.arange(cols, dtype=jnp.int32)[None, :]
    phase = (index_m * index_t % cols).astype(jnp.float32)
    angle = 2.0 * jnp.pi * phase / cols
    return (jnp.cos(angle) + jnp.sin(angle)) / jnp.sqrt(jnp.float32(cols))


def inner(left, right):
    return jnp.sum(left * right, axis=(0, 1, 3))


def reduce_kernel(axis_names, stages, x_ref, o_ref, cur, recv, send_sem, recv_sem):
    me = {name: lax.axis_index(name) for name in axis_names}

    def device(axis, coord):
        return tuple(coord if name == axis else me[name] for name in axis_names)

    plan = []
    base = 0
    for axis, stride, size in stages:
        own = (me[axis] // stride) % size
        root = me[axis] - own * stride
        peers = []
        for step in range(1, size):
            other = lax.rem(own + step, size)
            peers.append((other, device(axis, root + other * stride)))
        plan.append((base, own, size, peers))
        base += size

    barrier = pltpu.get_barrier_semaphore()
    for _, _, _, peers in plan:
        for _, peer in peers:
            pl.semaphore_signal(barrier, 1, device_id=peer, device_id_type=MESH)
    pl.semaphore_wait(barrier, sum(len(peers) for _, _, _, peers in plan))

    acc = x_ref[...].astype(jnp.float32)
    for index, (base, own, size, peers) in enumerate(plan):
        cur[index] = acc.astype(cur.dtype)
        copies = []
        for other, peer in peers:
            copy = pltpu.make_async_remote_copy(
                src_ref=cur.at[index],
                dst_ref=recv.at[base + own],
                send_sem=send_sem.at[base + other],
                recv_sem=recv_sem.at[base + own],
                device_id=peer,
                device_id_type=MESH,
            )
            copy.start()
            copies.append(copy)
        recv[base + own] = acc.astype(recv.dtype)
        for other, peer in peers:
            pltpu.make_async_remote_copy(
                src_ref=cur.at[index],
                dst_ref=recv.at[base + other],
                send_sem=send_sem.at[base + other],
                recv_sem=recv_sem.at[base + other],
                device_id=peer,
                device_id_type=MESH,
            ).wait_recv()
        for copy in copies:
            copy.wait_send()
        total = recv[base].astype(jnp.float32)
        for slot in range(1, size):
            total = total + recv[base + slot].astype(jnp.float32)
        acc = total
    o_ref[...] = acc.astype(o_ref.dtype)


def group_sum(x, axis_names, stages, wire_dtype, collective_id):
    slots = sum(size for _, _, size in stages)
    return pl.pallas_call(
        functools.partial(reduce_kernel, axis_names, stages),
        out_shape=jax.ShapeDtypeStruct(x.shape, jnp.float32),
        in_specs=[pl.BlockSpec(memory_space=pltpu.VMEM)],
        out_specs=pl.BlockSpec(memory_space=pltpu.VMEM),
        scratch_shapes=[
            pltpu.VMEM((len(stages),) + x.shape, wire_dtype),
            pltpu.VMEM((slots,) + x.shape, wire_dtype),
            pltpu.SemaphoreType.DMA((slots,)),
            pltpu.SemaphoreType.DMA((slots,)),
        ],
        compiler_params=pltpu.CompilerParams(collective_id=collective_id, has_side_effects=True),
    )(x)


def column_sum(x):
    return jnp.sum(jnp.sum(x, axis=0), axis=1, keepdims=True)


def to_row(columns):
    count = columns[0].shape[0]
    sub = lax.broadcasted_iota(jnp.int32, (count, 128), 0)
    lane = lax.broadcasted_iota(jnp.int32, (count, 128), 1)
    acc = jnp.zeros((count, 128), jnp.float32)
    for index, column in enumerate(columns):
        acc = acc + jnp.where(lane == sub + count * index, jnp.broadcast_to(column, (count, 128)), 0.0)
    return jnp.sum(acc, axis=0, keepdims=True)


def from_row(row, index, count):
    sub = lax.broadcasted_iota(jnp.int32, (count, 128), 0)
    lane = lax.broadcasted_iota(jnp.int32, (count, 128), 1)
    picked = jnp.where(lane == sub + count * index, jnp.broadcast_to(row, (count, 128)), 0.0)
    return jnp.sum(picked, axis=1, keepdims=True)


def group_size(stage):
    size = 1
    for _, extent in stage[1]:
        size *= extent
    return size


def cg_kernel(first, axis_names, stages, *refs):
    if first:
        (d_ref, cb_ref, diag_ref, pm_ref, est_ref, next_ref, norm_ref,
         part, rows, recv_p, recv_rows, p_send, p_recv, r_send, r_recv) = refs
    else:
        (d_ref, cb_ref, diag_ref, pm_ref, est_in_ref, norm_in_ref, est_ref,
         part, rows, recv_p, recv_rows, p_send, p_recv, r_send, r_recv) = refs
    me = {name: lax.axis_index(name) for name in axis_names}

    def place(stage):
        axis, dims = stage
        own = 0
        root = me[axis]
        scale = 1
        for stride, size in dims:
            digit = lax.rem(me[axis] // stride, size)
            own = own + digit * scale
            root = root - digit * stride
            scale *= size

        def device(other):
            coord = root
            scale = 1
            for stride, size in dims:
                coord = coord + lax.rem(other // scale, size) * stride
                scale *= size
            return tuple(coord if name == axis else me[name] for name in axis_names)

        return own, device

    barrier = pltpu.get_barrier_semaphore()
    for stage in stages:
        own, device = place(stage)
        for step in range(1, group_size(stage)):
            other = lax.rem(own + step, group_size(stage))
            pl.semaphore_signal(barrier, 1, device_id=device(other), device_id_type=MESH)
    pl.semaphore_wait(barrier, sum(group_size(stage) - 1 for stage in stages))

    def exchange_start(stage, src, recv, base, send_sems, recv_sems):
        own, device = place(stage)
        size = group_size(stage)

        def copy_to(other, slot):
            return pltpu.make_async_remote_copy(
                src_ref=src,
                dst_ref=recv.at[base + slot],
                send_sem=send_sems.at[base + other],
                recv_sem=recv_sems.at[base + slot],
                device_id=device(other),
                device_id_type=MESH,
            )

        for step in range(1, size):
            copy_to(lax.rem(own + step, size), own).start()
        recv[base + own] = src[...]
        return own, size, base, recv, copy_to

    sent = []

    def exchange_finish(state):
        own, size, base, recv, copy_to = state
        for step in range(1, size):
            other = lax.rem(own + step, size)
            copy_to(other, other).wait_recv()
        sent.append(state)
        total = recv[base].astype(jnp.float32)
        for slot in range(1, size):
            total = total + recv[base + slot].astype(jnp.float32)
        return total

    counter = {"row": 0, "slot": 0}

    def next_row(value):
        index = counter["row"]
        counter["row"] += 1
        rows[index] = value
        return rows.at[index]

    def row_stage(stage, src):
        base = counter["slot"]
        counter["slot"] += group_size(stage)
        return exchange_start(stage, src, recv_rows, base, r_send, r_recv)

    def reduce_rest(value):
        for stage in stages[1:]:
            value = exchange_finish(row_stage(stage, next_row(value)))
        return value

    d = d_ref[...]
    cb = cb_ref[...]
    diag = diag_ref[...]
    pm = pm_ref[...]
    count = d.shape[1]
    for rank in range(pm.shape[1]):
        part[rank] = jnp.sum(pm[:, rank] * d, axis=0).astype(part.dtype)
    if first:
        row = to_row([column_sum(d * (cb + diag * d)), column_sum(d * d)])
    else:
        row = to_row([column_sum(d * (cb + diag * d))])
    p_state = exchange_start(stages[0], part, recv_p, 0, p_send, p_recv)
    z_state = row_stage(stages[0], next_row(row))
    projection = exchange_finish(p_state)
    zrow = exchange_finish(z_state)
    total = reduce_rest(zrow + to_row([column_sum(projection * projection)]))
    curve = from_row(total, 0, count)
    if first:
        norm_now = from_row(total, 1, count)
        step_size = (norm_now / curve)[None]
        est_ref[...] = step_size * d
        spread = pm[:, 0] * projection[0][None]
        for rank in range(1, pm.shape[1]):
            spread = spread + pm[:, rank] * projection[rank][None]
        image = cb + diag * d + spread
        residual = d - step_size * image
        row = to_row([column_sum(residual * residual)])
        zrow = exchange_finish(row_stage(stages[0], next_row(row)))
        total = reduce_rest(zrow)
        norm_next = from_row(total, 0, count)
        next_ref[...] = residual + (norm_next / norm_now)[None] * d
        norm_ref[...] = total
    else:
        norm_now = from_row(norm_in_ref[...], 0, count)
        est_ref[...] = est_in_ref[...] + (norm_now / curve)[None] * d
    for own, size, _, _, copy_to in sent:
        for step in range(1, size):
            copy_to(lax.rem(own + step, size), own).wait_send()


def cg_step(first, axis_names, stages, d, cb, diag, pm, *extra):
    reductions = 2 if first else 1
    slots = reductions * sum(group_size(stage) for stage in stages)
    rounds = reductions * len(stages)
    nz = group_size(stages[0])
    vector = jax.ShapeDtypeStruct(d.shape, jnp.float32)
    row = jax.ShapeDtypeStruct((1, 128), jnp.float32)
    out_shape = (vector, vector, row) if first else vector
    vmem = pl.BlockSpec(memory_space=pltpu.VMEM)
    part_shape = (pm.shape[1],) + d.shape[1:]
    return pl.pallas_call(
        functools.partial(cg_kernel, first, axis_names, stages),
        out_shape=out_shape,
        in_specs=[vmem] * (4 + len(extra)),
        out_specs=(vmem, vmem, vmem) if first else vmem,
        scratch_shapes=[
            pltpu.VMEM(part_shape, jnp.bfloat16),
            pltpu.VMEM((rounds, 1, 128), jnp.float32),
            pltpu.VMEM((nz,) + part_shape, jnp.bfloat16),
            pltpu.VMEM((slots, 1, 128), jnp.float32),
            pltpu.SemaphoreType.DMA((nz,)),
            pltpu.SemaphoreType.DMA((nz,)),
            pltpu.SemaphoreType.DMA((slots,)),
            pltpu.SemaphoreType.DMA((slots,)),
        ],
        compiler_params=pltpu.CompilerParams(
            collective_id=1 if first else 2, has_side_effects=True
        ),
    )(d, cb, diag, pm, *extra)


def make_shards(mesh):
    axis_names = tuple(mesh.axis_names)
    mode_devices = mesh.shape["ma"]
    freq_devices = mesh.shape["freq"]
    if mode_devices % 16 == 0:
        mode_stages = [("ma", 1, 2), ("ma", 2, 8), ("ma", 16, mode_devices // 16)]
    else:
        mode_stages = [("ma", 1, mode_devices)]
    global_stages = mode_stages + [("freq", 1, freq_devices)]
    freq_stages = [("freq", 1, freq_devices)]

    def scalar_sum(*vectors):
        rows = jnp.stack(vectors)
        padded = jnp.pad(rows, ((0, 8 - rows.shape[0]), (0, 128 - rows.shape[1])))
        summed = group_sum(padded, axis_names, global_stages, jnp.float32, 2)
        return [summed[index, : rows.shape[1]] for index in range(len(vectors))]

    def freq_sum(partial_sum):
        shape = partial_sum.shape
        flat = partial_sum.reshape(-1, shape[-1])
        summed = group_sum(flat, axis_names, freq_stages, jnp.bfloat16, 1)
        return summed.reshape(shape)

    def shards(timestream, beam_transfer, chromatic_gain, noise_weight, prior_diagonal, prior_modes):
        spectral_channels = timestream.shape[0]
        device_time_samples = timestream.shape[1]
        noise_realizations = timestream.shape[2]
        antenna_pairs = timestream.shape[3]
        mode_devices_here = mode_devices
        columns = noise_realizations * antenna_pairs // mode_devices_here
        blocks = antenna_pairs // columns
        halves = columns // 128
        send = timestream.reshape(
            spectral_channels, device_time_samples, noise_realizations, blocks, halves, 128
        ).transpose(2, 3, 0, 1, 4, 5)
        send = send.reshape(mode_devices_here, spectral_channels * device_time_samples * halves, 128)
        received = lax.all_to_all(send, "ma", 0, 0, tiled=True)
        received = received.reshape(mode_devices_here, spectral_channels, device_time_samples, columns)
        all_times = mode_devices_here * device_time_samples
        hartley = hartley_table(all_times // 2, all_times)
        hartley_high = hartley.astype(jnp.bfloat16)
        hartley_low = (hartley - hartley_high.astype(jnp.float32)).astype(jnp.bfloat16)
        hartley_high = hartley_high.reshape(all_times // 2, mode_devices_here, device_time_samples)
        hartley_low = hartley_low.reshape(all_times // 2, mode_devices_here, device_time_samples)
        mode_high = jnp.einsum(
            "mit,iftc->mfc", hartley_high, received, preferred_element_type=jnp.float32
        )
        mode_low = jnp.einsum("mit,iftc->mfc", hartley_low, received, preferred_element_type=jnp.float32)
        mode_rows = (mode_high + mode_low).astype(jnp.bfloat16)
        back_rows = lax.all_to_all(mode_rows, "ma", 0, 0, tiled=True)
        resident_modes = back_rows.shape[0] // mode_devices_here
        back_rows = back_rows.reshape(
            noise_realizations, blocks, resident_modes, spectral_channels, columns
        )
        measured_visibility = back_rows.transpose(3, 2, 0, 1, 4).reshape(
            spectral_channels, resident_modes, noise_realizations, antenna_pairs
        )
        chroma = chromatic_gain[:, None, None, :]
        diagonal = prior_diagonal[:, None, None, :]
        weighted = (noise_weight[:, :, None, :] * measured_visibility.astype(jnp.float32)).astype(
            jnp.bfloat16
        )
        rhs = chroma * jnp.einsum(
            "fmkb,mbs->fmks", weighted, beam_transfer, preferred_element_type=jnp.float32
        )

        assert resident_modes == 1
        if mode_devices % 16 == 0:
            cg_stages = [
                ("freq", [(1, freq_devices)]),
                ("ma", [(1, 2), (16, mode_devices // 16)]),
                ("ma", [(2, 8)]),
            ]
        else:
            cg_stages = [("freq", [(1, freq_devices)]), ("ma", [(1, mode_devices)])]
        diag_rows = prior_diagonal[:, None, :]
        mode_rows4 = prior_modes[:, :, None, :]

        def beam_back(direction):
            low = (chroma * direction).astype(jnp.bfloat16)
            seen = jnp.einsum("fmks,mbs->fmkb", low, beam_transfer, preferred_element_type=jnp.float32)
            heard = (noise_weight[:, :, None, :] * seen).astype(jnp.bfloat16)
            back = jnp.einsum(
                "fmkb,mbs->fmks", heard, beam_transfer, preferred_element_type=jnp.float32
            )
            return (chroma * back)[:, 0]

        direction = rhs[:, 0]
        estimate, direction, norm_row = cg_step(
            True, axis_names, cg_stages, direction, beam_back(direction[:, None]), diag_rows, mode_rows4
        )
        estimate = cg_step(
            False, axis_names, cg_stages, direction, beam_back(direction[:, None]), diag_rows, mode_rows4,
            estimate, norm_row,
        )
        estimate = estimate[:, None]
        return estimate

    return shards


def solution(mesh):
    in_specs = (
        P("freq", "ma", None, None),
        P("ma", None, None),
        P("freq", None),
        P("freq", "ma", None),
        P("freq", None),
        P("freq", None, None),
    )
    out_specs = P("freq", "ma", None, None)
    return jax.shard_map(make_shards(mesh), mesh=mesh, in_specs=in_specs, out_specs=out_specs, check_vma=False)
```

```python
import functools

import jax
import jax.numpy as jnp
from jax import lax
from jax.experimental import pallas as pl
from jax.experimental.pallas import tpu as pltpu
from jax.sharding import PartitionSpec as P

ITERS = 2
MESH = pl.DeviceIdType.MESH


def hartley_table(rows, cols):
    index_m = jnp.arange(rows, dtype=jnp.int32)[:, None]
    index_t = jnp.arange(cols, dtype=jnp.int32)[None, :]
    phase = (index_m * index_t % cols).astype(jnp.float32)
    angle = 2.0 * jnp.pi * phase / cols
    return (jnp.cos(angle) + jnp.sin(angle)) / jnp.sqrt(jnp.float32(cols))


def inner(left, right):
    return jnp.sum(left * right, axis=(0, 1, 3))


def reduce_kernel(axis_names, stages, x_ref, o_ref, cur, recv, send_sem, recv_sem):
    me = {name: lax.axis_index(name) for name in axis_names}

    def device(axis, coord):
        return tuple(coord if name == axis else me[name] for name in axis_names)

    plan = []
    base = 0
    for axis, stride, size in stages:
        own = (me[axis] // stride) % size
        root = me[axis] - own * stride
        peers = []
        for step in range(1, size):
            other = lax.rem(own + step, size)
            peers.append((other, device(axis, root + other * stride)))
        plan.append((base, own, size, peers))
        base += size

    barrier = pltpu.get_barrier_semaphore()
    for _, _, _, peers in plan:
        for _, peer in peers:
            pl.semaphore_signal(barrier, 1, device_id=peer, device_id_type=MESH)
    pl.semaphore_wait(barrier, sum(len(peers) for _, _, _, peers in plan))

    acc = x_ref[...].astype(jnp.float32)
    for index, (base, own, size, peers) in enumerate(plan):
        cur[index] = acc.astype(cur.dtype)
        copies = []
        for other, peer in peers:
            copy = pltpu.make_async_remote_copy(
                src_ref=cur.at[index],
                dst_ref=recv.at[base + own],
                send_sem=send_sem.at[base + other],
                recv_sem=recv_sem.at[base + own],
                device_id=peer,
                device_id_type=MESH,
            )
            copy.start()
            copies.append(copy)
        recv[base + own] = acc.astype(recv.dtype)
        for other, peer in peers:
            pltpu.make_async_remote_copy(
                src_ref=cur.at[index],
                dst_ref=recv.at[base + other],
                send_sem=send_sem.at[base + other],
                recv_sem=recv_sem.at[base + other],
                device_id=peer,
                device_id_type=MESH,
            ).wait_recv()
        for copy in copies:
            copy.wait_send()
        total = recv[base].astype(jnp.float32)
        for slot in range(1, size):
            total = total + recv[base + slot].astype(jnp.float32)
        acc = total
    o_ref[...] = acc.astype(o_ref.dtype)


def group_sum(x, axis_names, stages, wire_dtype, collective_id):
    slots = sum(size for _, _, size in stages)
    return pl.pallas_call(
        functools.partial(reduce_kernel, axis_names, stages),
        out_shape=jax.ShapeDtypeStruct(x.shape, jnp.float32),
        in_specs=[pl.BlockSpec(memory_space=pltpu.VMEM)],
        out_specs=pl.BlockSpec(memory_space=pltpu.VMEM),
        scratch_shapes=[
            pltpu.VMEM((len(stages),) + x.shape, wire_dtype),
            pltpu.VMEM((slots,) + x.shape, wire_dtype),
            pltpu.SemaphoreType.DMA((slots,)),
            pltpu.SemaphoreType.DMA((slots,)),
        ],
        compiler_params=pltpu.CompilerParams(collective_id=collective_id, has_side_effects=True),
    )(x)


def column_sum(x):
    return jnp.sum(jnp.sum(x, axis=0), axis=1, keepdims=True)


def to_row(columns):
    count = columns[0].shape[0]
    sub = lax.broadcasted_iota(jnp.int32, (count, 128), 0)
    lane = lax.broadcasted_iota(jnp.int32, (count, 128), 1)
    acc = jnp.zeros((count, 128), jnp.float32)
    for index, column in enumerate(columns):
        acc = acc + jnp.where(lane == sub + count * index, jnp.broadcast_to(column, (count, 128)), 0.0)
    return jnp.sum(acc, axis=0, keepdims=True)


def from_row(row, index, count):
    sub = lax.broadcasted_iota(jnp.int32, (count, 128), 0)
    lane = lax.broadcasted_iota(jnp.int32, (count, 128), 1)
    picked = jnp.where(lane == sub + count * index, jnp.broadcast_to(row, (count, 128)), 0.0)
    return jnp.sum(picked, axis=1, keepdims=True)


def group_size(stage):
    size = 1
    for _, extent in stage[1]:
        size *= extent
    return size


def cg_kernel(first, axis_names, stages, *refs):
    if first:
        (d_ref, beam_ref, chroma_ref, weight_ref, diag_ref, pm_ref, est_ref, next_ref, norm_ref,
         part, rows, recv_p, recv_rows, p_send, p_recv, r_send, r_recv) = refs
    else:
        (d_ref, beam_ref, chroma_ref, weight_ref, diag_ref, pm_ref, est_in_ref, norm_in_ref, est_ref,
         part, rows, recv_p, recv_rows, p_send, p_recv, r_send, r_recv) = refs
    me = {name: lax.axis_index(name) for name in axis_names}

    def place(stage):
        axis, dims = stage
        own = 0
        root = me[axis]
        scale = 1
        for stride, size in dims:
            digit = lax.rem(me[axis] // stride, size)
            own = own + digit * scale
            root = root - digit * stride
            scale *= size

        def device(other):
            coord = root
            scale = 1
            for stride, size in dims:
                coord = coord + lax.rem(other // scale, size) * stride
                scale *= size
            return tuple(coord if name == axis else me[name] for name in axis_names)

        return own, device

    barrier = pltpu.get_barrier_semaphore()
    for stage in stages:
        own, device = place(stage)
        for step in range(1, group_size(stage)):
            other = lax.rem(own + step, group_size(stage))
            pl.semaphore_signal(barrier, 1, device_id=device(other), device_id_type=MESH)

    d = d_ref[...]
    chroma = chroma_ref[...]
    channels, count, modes = d.shape
    beam = beam_ref[...]
    low = (chroma * d).astype(jnp.bfloat16).reshape(channels * count, modes)
    seen = lax.dot_general(low, beam, (((1,), (1,)), ((), ())), preferred_element_type=jnp.float32)
    heard = (weight_ref[...] * seen.reshape(channels, count, -1)).astype(jnp.bfloat16)
    back = jnp.dot(heard.reshape(channels * count, -1), beam, preferred_element_type=jnp.float32)
    cb = chroma * back.reshape(channels, count, modes)
    pl.semaphore_wait(barrier, sum(group_size(stage) - 1 for stage in stages))

    def exchange_start(stage, src, recv, base, send_sems, recv_sems):
        own, device = place(stage)
        size = group_size(stage)

        def copy_to(other, slot):
            return pltpu.make_async_remote_copy(
                src_ref=src,
                dst_ref=recv.at[base + slot],
                send_sem=send_sems.at[base + other],
                recv_sem=recv_sems.at[base + slot],
                device_id=device(other),
                device_id_type=MESH,
            )

        for step in range(1, size):
            copy_to(lax.rem(own + step, size), own).start()
        recv[base + own] = src[...]
        return own, size, base, recv, copy_to

    sent = []

    def exchange_finish(state):
        own, size, base, recv, copy_to = state
        for step in range(1, size):
            other = lax.rem(own + step, size)
            copy_to(other, other).wait_recv()
        sent.append(state)
        total = recv[base].astype(jnp.float32)
        for slot in range(1, size):
            total = total + recv[base + slot].astype(jnp.float32)
        return total

    counter = {"row": 0, "slot": 0}

    def next_row(value):
        index = counter["row"]
        counter["row"] += 1
        rows[index] = value
        return rows.at[index]

    def row_stage(stage, src):
        base = counter["slot"]
        counter["slot"] += group_size(stage)
        return exchange_start(stage, src, recv_rows, base, r_send, r_recv)

    def reduce_rest(value):
        for stage in stages[1:]:
            value = exchange_finish(row_stage(stage, next_row(value)))
        return value

    diag = diag_ref[...]
    pm = pm_ref[...]
    count = d.shape[1]
    for rank in range(pm.shape[1]):
        part[rank] = jnp.sum(pm[:, rank] * d, axis=0).astype(part.dtype)
    if first:
        row = to_row([column_sum(d * (cb + diag * d)), column_sum(d * d)])
    else:
        row = to_row([column_sum(d * (cb + diag * d))])
    p_state = exchange_start(stages[0], part, recv_p, 0, p_send, p_recv)
    z_state = row_stage(stages[0], next_row(row))
    projection = exchange_finish(p_state)
    zrow = exchange_finish(z_state)
    total = reduce_rest(zrow + to_row([column_sum(projection * projection)]))
    curve = from_row(total, 0, count)
    if first:
        norm_now = from_row(total, 1, count)
        step_size = (norm_now / curve)[None]
        est_ref[...] = step_size * d
        spread = pm[:, 0] * projection[0][None]
        for rank in range(1, pm.shape[1]):
            spread = spread + pm[:, rank] * projection[rank][None]
        image = cb + diag * d + spread
        residual = d - step_size * image
        row = to_row([column_sum(residual * residual)])
        zrow = exchange_finish(row_stage(stages[0], next_row(row)))
        total = reduce_rest(zrow)
        norm_next = from_row(total, 0, count)
        next_ref[...] = residual + (norm_next / norm_now)[None] * d
        norm_ref[...] = total
    else:
        norm_now = from_row(norm_in_ref[...], 0, count)
        est_ref[...] = est_in_ref[...] + (norm_now / curve)[None] * d
    for own, size, _, _, copy_to in sent:
        for step in range(1, size):
            copy_to(lax.rem(own + step, size), own).wait_send()


def cg_step(first, axis_names, stages, d, beam, chroma, weight, diag, pm, *extra):
    reductions = 2 if first else 1
    slots = reductions * sum(group_size(stage) for stage in stages)
    rounds = reductions * len(stages)
    nz = group_size(stages[0])
    vector = jax.ShapeDtypeStruct(d.shape, jnp.float32)
    row = jax.ShapeDtypeStruct((1, 128), jnp.float32)
    out_shape = (vector, vector, row) if first else vector
    vmem = pl.BlockSpec(memory_space=pltpu.VMEM)
    part_shape = (pm.shape[1],) + d.shape[1:]
    return pl.pallas_call(
        functools.partial(cg_kernel, first, axis_names, stages),
        out_shape=out_shape,
        in_specs=[vmem] * (6 + len(extra)),
        out_specs=(vmem, vmem, vmem) if first else vmem,
        scratch_shapes=[
            pltpu.VMEM(part_shape, jnp.bfloat16),
            pltpu.VMEM((rounds, 1, 128), jnp.float32),
            pltpu.VMEM((nz,) + part_shape, jnp.bfloat16),
            pltpu.VMEM((slots, 1, 128), jnp.float32),
            pltpu.SemaphoreType.DMA((nz,)),
            pltpu.SemaphoreType.DMA((nz,)),
            pltpu.SemaphoreType.DMA((slots,)),
            pltpu.SemaphoreType.DMA((slots,)),
        ],
        compiler_params=pltpu.CompilerParams(
            collective_id=1 if first else 2, has_side_effects=True
        ),
    )(d, beam, chroma, weight, diag, pm, *extra)


def make_shards(mesh):
    axis_names = tuple(mesh.axis_names)
    mode_devices = mesh.shape["ma"]
    freq_devices = mesh.shape["freq"]
    if mode_devices % 16 == 0:
        mode_stages = [("ma", 1, 2), ("ma", 2, 8), ("ma", 16, mode_devices // 16)]
    else:
        mode_stages = [("ma", 1, mode_devices)]
    global_stages = mode_stages + [("freq", 1, freq_devices)]
    freq_stages = [("freq", 1, freq_devices)]

    def scalar_sum(*vectors):
        rows = jnp.stack(vectors)
        padded = jnp.pad(rows, ((0, 8 - rows.shape[0]), (0, 128 - rows.shape[1])))
        summed = group_sum(padded, axis_names, global_stages, jnp.float32, 2)
        return [summed[index, : rows.shape[1]] for index in range(len(vectors))]

    def freq_sum(partial_sum):
        shape = partial_sum.shape
        flat = partial_sum.reshape(-1, shape[-1])
        summed = group_sum(flat, axis_names, freq_stages, jnp.bfloat16, 1)
        return summed.reshape(shape)

    def shards(timestream, beam_transfer, chromatic_gain, noise_weight, prior_diagonal, prior_modes):
        spectral_channels = timestream.shape[0]
        device_time_samples = timestream.shape[1]
        noise_realizations = timestream.shape[2]
        antenna_pairs = timestream.shape[3]
        mode_devices_here = mode_devices
        columns = noise_realizations * antenna_pairs // mode_devices_here
        blocks = antenna_pairs // columns
        halves = columns // 128
        send = timestream.reshape(
            spectral_channels, device_time_samples, noise_realizations, blocks, halves, 128
        ).transpose(2, 3, 0, 1, 4, 5)
        send = send.reshape(mode_devices_here, spectral_channels * device_time_samples * halves, 128)
        received = lax.all_to_all(send, "ma", 0, 0, tiled=True)
        received = received.reshape(mode_devices_here, spectral_channels, device_time_samples, columns)
        all_times = mode_devices_here * device_time_samples
        hartley = hartley_table(all_times // 2, all_times)
        hartley_high = hartley.astype(jnp.bfloat16)
        hartley_low = (hartley - hartley_high.astype(jnp.float32)).astype(jnp.bfloat16)
        hartley_high = hartley_high.reshape(all_times // 2, mode_devices_here, device_time_samples)
        hartley_low = hartley_low.reshape(all_times // 2, mode_devices_here, device_time_samples)
        mode_high = jnp.einsum(
            "mit,iftc->mfc", hartley_high, received, preferred_element_type=jnp.float32
        )
        mode_low = jnp.einsum("mit,iftc->mfc", hartley_low, received, preferred_element_type=jnp.float32)
        mode_rows = (mode_high + mode_low).astype(jnp.bfloat16)
        back_rows = lax.all_to_all(mode_rows, "ma", 0, 0, tiled=True)
        resident_modes = back_rows.shape[0] // mode_devices_here
        back_rows = back_rows.reshape(
            noise_realizations, blocks, resident_modes, spectral_channels, columns
        )
        measured_visibility = back_rows.transpose(3, 2, 0, 1, 4).reshape(
            spectral_channels, resident_modes, noise_realizations, antenna_pairs
        )
        chroma = chromatic_gain[:, None, None, :]
        diagonal = prior_diagonal[:, None, None, :]
        weighted = (noise_weight[:, :, None, :] * measured_visibility.astype(jnp.float32)).astype(
            jnp.bfloat16
        )
        rhs = chroma * jnp.einsum(
            "fmkb,mbs->fmks", weighted, beam_transfer, preferred_element_type=jnp.float32
        )

        assert resident_modes == 1
        if mode_devices % 16 == 0:
            cg_stages = [
                ("freq", [(1, freq_devices)]),
                ("ma", [(1, 2), (16, mode_devices // 16)]),
                ("ma", [(2, 8)]),
            ]
        else:
            cg_stages = [("freq", [(1, freq_devices)]), ("ma", [(1, mode_devices)])]
        diag_rows = prior_diagonal[:, None, :]
        mode_rows4 = prior_modes[:, :, None, :]

        def beam_back(direction):
            low = (chroma * direction).astype(jnp.bfloat16)
            seen = jnp.einsum("fmks,mbs->fmkb", low, beam_transfer, preferred_element_type=jnp.float32)
            heard = (noise_weight[:, :, None, :] * seen).astype(jnp.bfloat16)
            back = jnp.einsum(
                "fmkb,mbs->fmks", heard, beam_transfer, preferred_element_type=jnp.float32
            )
            return (chroma * back)[:, 0]

        direction = rhs[:, 0]
        operands = (beam_transfer[0], chromatic_gain[:, None, :], noise_weight, diag_rows, mode_rows4)
        estimate, direction, norm_row = cg_step(True, axis_names, cg_stages, direction, *operands)
        estimate = cg_step(
            False, axis_names, cg_stages, direction, *operands, estimate, norm_row
        )
        estimate = estimate[:, None]
        return estimate

    return shards


def solution(mesh):
    in_specs = (
        P("freq", "ma", None, None),
        P("ma", None, None),
        P("freq", None),
        P("freq", "ma", None),
        P("freq", None),
        P("freq", None, None),
    )
    out_specs = P("freq", "ma", None, None)
    return jax.shard_map(make_shards(mesh), mesh=mesh, in_specs=in_specs, out_specs=out_specs, check_vma=False)
```

```python
import functools

import jax
import jax.numpy as jnp
from jax import lax
from jax.experimental import pallas as pl
from jax.experimental.pallas import tpu as pltpu
from jax.sharding import PartitionSpec as P

ITERS = 2
MESH = pl.DeviceIdType.MESH


def hartley_table(rows, cols):
    index_m = jnp.arange(rows, dtype=jnp.int32)[:, None]
    index_t = jnp.arange(cols, dtype=jnp.int32)[None, :]
    phase = (index_m * index_t % cols).astype(jnp.float32)
    angle = 2.0 * jnp.pi * phase / cols
    return (jnp.cos(angle) + jnp.sin(angle)) / jnp.sqrt(jnp.float32(cols))


def inner(left, right):
    return jnp.sum(left * right, axis=(0, 1, 3))


def reduce_kernel(axis_names, stages, x_ref, o_ref, cur, recv, send_sem, recv_sem):
    me = {name: lax.axis_index(name) for name in axis_names}

    def device(axis, coord):
        return tuple(coord if name == axis else me[name] for name in axis_names)

    plan = []
    base = 0
    for axis, stride, size in stages:
        own = (me[axis] // stride) % size
        root = me[axis] - own * stride
        peers = []
        for step in range(1, size):
            other = lax.rem(own + step, size)
            peers.append((other, device(axis, root + other * stride)))
        plan.append((base, own, size, peers))
        base += size

    barrier = pltpu.get_barrier_semaphore()
    for _, _, _, peers in plan:
        for _, peer in peers:
            pl.semaphore_signal(barrier, 1, device_id=peer, device_id_type=MESH)
    pl.semaphore_wait(barrier, sum(len(peers) for _, _, _, peers in plan))

    acc = x_ref[...].astype(jnp.float32)
    for index, (base, own, size, peers) in enumerate(plan):
        cur[index] = acc.astype(cur.dtype)
        copies = []
        for other, peer in peers:
            copy = pltpu.make_async_remote_copy(
                src_ref=cur.at[index],
                dst_ref=recv.at[base + own],
                send_sem=send_sem.at[base + other],
                recv_sem=recv_sem.at[base + own],
                device_id=peer,
                device_id_type=MESH,
            )
            copy.start()
            copies.append(copy)
        recv[base + own] = acc.astype(recv.dtype)
        for other, peer in peers:
            pltpu.make_async_remote_copy(
                src_ref=cur.at[index],
                dst_ref=recv.at[base + other],
                send_sem=send_sem.at[base + other],
                recv_sem=recv_sem.at[base + other],
                device_id=peer,
                device_id_type=MESH,
            ).wait_recv()
        for copy in copies:
            copy.wait_send()
        total = recv[base].astype(jnp.float32)
        for slot in range(1, size):
            total = total + recv[base + slot].astype(jnp.float32)
        acc = total
    o_ref[...] = acc.astype(o_ref.dtype)


def group_sum(x, axis_names, stages, wire_dtype, collective_id):
    slots = sum(size for _, _, size in stages)
    return pl.pallas_call(
        functools.partial(reduce_kernel, axis_names, stages),
        out_shape=jax.ShapeDtypeStruct(x.shape, jnp.float32),
        in_specs=[pl.BlockSpec(memory_space=pltpu.VMEM)],
        out_specs=pl.BlockSpec(memory_space=pltpu.VMEM),
        scratch_shapes=[
            pltpu.VMEM((len(stages),) + x.shape, wire_dtype),
            pltpu.VMEM((slots,) + x.shape, wire_dtype),
            pltpu.SemaphoreType.DMA((slots,)),
            pltpu.SemaphoreType.DMA((slots,)),
        ],
        compiler_params=pltpu.CompilerParams(collective_id=collective_id, has_side_effects=True),
    )(x)


def column_sum(x):
    return jnp.sum(jnp.sum(x, axis=0), axis=1, keepdims=True)


def to_row(columns):
    count = columns[0].shape[0]
    sub = lax.broadcasted_iota(jnp.int32, (count, 128), 0)
    lane = lax.broadcasted_iota(jnp.int32, (count, 128), 1)
    acc = jnp.zeros((count, 128), jnp.float32)
    for index, column in enumerate(columns):
        acc = acc + jnp.where(lane == sub + count * index, jnp.broadcast_to(column, (count, 128)), 0.0)
    return jnp.sum(acc, axis=0, keepdims=True)


def from_row(row, index, count):
    sub = lax.broadcasted_iota(jnp.int32, (count, 128), 0)
    lane = lax.broadcasted_iota(jnp.int32, (count, 128), 1)
    picked = jnp.where(lane == sub + count * index, jnp.broadcast_to(row, (count, 128)), 0.0)
    return jnp.sum(picked, axis=1, keepdims=True)


def group_size(stage):
    size = 1
    for _, extent in stage[1]:
        size *= extent
    return size


def cg_kernel(axis_names, stages, d_ref, beam_ref, chroma_ref, weight_ref, diag_ref, pm_ref,
              est_ref, next_ref, step_ref, parts, rows, recv_p, recv_rows, p_send, p_recv, r_send, r_recv):
    me = {name: lax.axis_index(name) for name in axis_names}

    def place(stage):
        axis, dims = stage
        own = 0
        root = me[axis]
        scale = 1
        for stride, size in dims:
            digit = lax.rem(me[axis] // stride, size)
            own = own + digit * scale
            root = root - digit * stride
            scale *= size

        def device(other):
            coord = root
            scale = 1
            for stride, size in dims:
                coord = coord + lax.rem(other // scale, size) * stride
                scale *= size
            return tuple(coord if name == axis else me[name] for name in axis_names)

        return own, device

    barrier = pltpu.get_barrier_semaphore()
    for stage in stages:
        own, device = place(stage)
        for step in range(1, group_size(stage)):
            other = lax.rem(own + step, group_size(stage))
            pl.semaphore_signal(barrier, 1, device_id=device(other), device_id_type=MESH)

    chroma = chroma_ref[...]
    weight = weight_ref[...]
    diag = diag_ref[...]
    pm = pm_ref[...]
    d = d_ref[...]
    channels, count, modes = d.shape

    def beam_part(vector):
        beam = beam_ref[...]
        low = (chroma * vector).astype(jnp.bfloat16).reshape(channels * count, modes)
        seen = lax.dot_general(low, beam, (((1,), (1,)), ((), ())), preferred_element_type=jnp.float32)
        heard = (weight * seen.reshape(channels, count, -1)).astype(jnp.bfloat16)
        back = jnp.dot(heard.reshape(channels * count, -1), beam, preferred_element_type=jnp.float32)
        return chroma * back.reshape(channels, count, modes)

    cb = beam_part(d)
    pl.semaphore_wait(barrier, sum(group_size(stage) - 1 for stage in stages))

    def exchange_start(stage, src, recv, base, send_sems, recv_sems):
        own, device = place(stage)
        size = group_size(stage)

        def copy_to(other, slot):
            return pltpu.make_async_remote_copy(
                src_ref=src,
                dst_ref=recv.at[base + slot],
                send_sem=send_sems.at[base + other],
                recv_sem=recv_sems.at[base + slot],
                device_id=device(other),
                device_id_type=MESH,
            )

        for step in range(1, size):
            copy_to(lax.rem(own + step, size), own).start()
        recv[base + own] = src[...]
        return own, size, base, recv, copy_to

    sent = []

    def exchange_finish(state):
        own, size, base, recv, copy_to = state
        for step in range(1, size):
            other = lax.rem(own + step, size)
            copy_to(other, other).wait_recv()
        sent.append(state)
        total = recv[base].astype(jnp.float32)
        for slot in range(1, size):
            total = total + recv[base + slot].astype(jnp.float32)
        return total

    counter = {"row": 0, "slot": 0, "part": 0}

    def next_row(value):
        index = counter["row"]
        counter["row"] += 1
        rows[index] = value
        return rows.at[index]

    def row_stage(stage, src):
        base = counter["slot"]
        counter["slot"] += group_size(stage)
        return exchange_start(stage, src, recv_rows, base, r_send, r_recv)

    def reduce_rest(value):
        for stage in stages[1:]:
            value = exchange_finish(row_stage(stage, next_row(value)))
        return value

    def curve_sum(vector, image_part, extra):
        index = counter["part"]
        counter["part"] += 1
        for rank in range(pm.shape[1]):
            parts[index, rank] = jnp.sum(pm[:, rank] * vector, axis=0).astype(parts.dtype)
        row = to_row([column_sum(vector * image_part)] + extra)
        nz = group_size(stages[0])
        p_state = exchange_start(stages[0], parts.at[index], recv_p, index * nz, p_send, p_recv)
        z_state = row_stage(stages[0], next_row(row))
        projection = exchange_finish(p_state)
        zrow = exchange_finish(z_state)
        total = reduce_rest(zrow + to_row([column_sum(projection * projection)]))
        return projection, total

    projection, total = curve_sum(d, cb + diag * d, [column_sum(d * d)])
    curve = from_row(total, 0, count)
    norm_now = from_row(total, 1, count)
    step_size = (norm_now / curve)[None]
    estimate = step_size * d
    spread = pm[:, 0] * projection[0][None]
    for rank in range(1, pm.shape[1]):
        spread = spread + pm[:, rank] * projection[rank][None]
    residual = d - step_size * (cb + diag * d + spread)
    z_state = row_stage(stages[0], next_row(to_row([column_sum(residual * residual)])))
    cb_residual = beam_part(residual)
    total = reduce_rest(exchange_finish(z_state))
    norm_next = from_row(total, 0, count)
    ratio = (norm_next / norm_now)[None]
    direction = residual + ratio * d
    cb_direction = cb_residual + ratio * cb
    projection, total = curve_sum(direction, cb_direction + diag * direction, [])
    curve = from_row(total, 0, count)
    est_ref[...] = estimate
    next_ref[...] = direction
    step_ref[...] = to_row([norm_next / curve])
    for own, size, _, _, copy_to in sent:
        for step in range(1, size):
            copy_to(lax.rem(own + step, size), own).wait_send()


def cg_solve(axis_names, stages, d, beam, chroma, weight, diag, pm):
    reductions = 3
    slots = reductions * sum(group_size(stage) for stage in stages)
    rounds = reductions * len(stages)
    nz = group_size(stages[0])
    vector = jax.ShapeDtypeStruct(d.shape, jnp.float32)
    row = jax.ShapeDtypeStruct((1, 128), jnp.float32)
    vmem = pl.BlockSpec(memory_space=pltpu.VMEM)
    part_shape = (pm.shape[1],) + d.shape[1:]
    estimate, direction, step_row = pl.pallas_call(
        functools.partial(cg_kernel, axis_names, stages),
        out_shape=(vector, vector, row),
        in_specs=[vmem] * 6,
        out_specs=(vmem, vmem, vmem),
        scratch_shapes=[
            pltpu.VMEM((2,) + part_shape, jnp.bfloat16),
            pltpu.VMEM((rounds, 1, 128), jnp.float32),
            pltpu.VMEM((2 * nz,) + part_shape, jnp.bfloat16),
            pltpu.VMEM((slots, 1, 128), jnp.float32),
            pltpu.SemaphoreType.DMA((2 * nz,)),
            pltpu.SemaphoreType.DMA((2 * nz,)),
            pltpu.SemaphoreType.DMA((slots,)),
            pltpu.SemaphoreType.DMA((slots,)),
        ],
        compiler_params=pltpu.CompilerParams(collective_id=1, has_side_effects=True),
    )(d, beam, chroma, weight, diag, pm)
    step_size = step_row[0, : d.shape[1]]
    return estimate + step_size[None, :, None] * direction


def make_shards(mesh):
    axis_names = tuple(mesh.axis_names)
    mode_devices = mesh.shape["ma"]
    freq_devices = mesh.shape["freq"]
    if mode_devices % 16 == 0:
        mode_stages = [("ma", 1, 2), ("ma", 2, 8), ("ma", 16, mode_devices // 16)]
    else:
        mode_stages = [("ma", 1, mode_devices)]
    global_stages = mode_stages + [("freq", 1, freq_devices)]
    freq_stages = [("freq", 1, freq_devices)]

    def scalar_sum(*vectors):
        rows = jnp.stack(vectors)
        padded = jnp.pad(rows, ((0, 8 - rows.shape[0]), (0, 128 - rows.shape[1])))
        summed = group_sum(padded, axis_names, global_stages, jnp.float32, 2)
        return [summed[index, : rows.shape[1]] for index in range(len(vectors))]

    def freq_sum(partial_sum):
        shape = partial_sum.shape
        flat = partial_sum.reshape(-1, shape[-1])
        summed = group_sum(flat, axis_names, freq_stages, jnp.bfloat16, 1)
        return summed.reshape(shape)

    def shards(timestream, beam_transfer, chromatic_gain, noise_weight, prior_diagonal, prior_modes):
        spectral_channels = timestream.shape[0]
        device_time_samples = timestream.shape[1]
        noise_realizations = timestream.shape[2]
        antenna_pairs = timestream.shape[3]
        mode_devices_here = mode_devices
        columns = noise_realizations * antenna_pairs // mode_devices_here
        blocks = antenna_pairs // columns
        halves = columns // 128
        send = timestream.reshape(
            spectral_channels, device_time_samples, noise_realizations, blocks, halves, 128
        ).transpose(2, 3, 0, 1, 4, 5)
        send = send.reshape(mode_devices_here, spectral_channels * device_time_samples * halves, 128)
        received = lax.all_to_all(send, "ma", 0, 0, tiled=True)
        received = received.reshape(mode_devices_here, spectral_channels, device_time_samples, columns)
        all_times = mode_devices_here * device_time_samples
        hartley = hartley_table(all_times // 2, all_times)
        hartley_high = hartley.astype(jnp.bfloat16)
        hartley_low = (hartley - hartley_high.astype(jnp.float32)).astype(jnp.bfloat16)
        hartley_high = hartley_high.reshape(all_times // 2, mode_devices_here, device_time_samples)
        hartley_low = hartley_low.reshape(all_times // 2, mode_devices_here, device_time_samples)
        mode_high = jnp.einsum(
            "mit,iftc->mfc", hartley_high, received, preferred_element_type=jnp.float32
        )
        mode_low = jnp.einsum("mit,iftc->mfc", hartley_low, received, preferred_element_type=jnp.float32)
        mode_rows = (mode_high + mode_low).astype(jnp.bfloat16)
        back_rows = lax.all_to_all(mode_rows, "ma", 0, 0, tiled=True)
        resident_modes = back_rows.shape[0] // mode_devices_here
        back_rows = back_rows.reshape(
            noise_realizations, blocks, resident_modes, spectral_channels, columns
        )
        measured_visibility = back_rows.transpose(3, 2, 0, 1, 4).reshape(
            spectral_channels, resident_modes, noise_realizations, antenna_pairs
        )
        chroma = chromatic_gain[:, None, None, :]
        diagonal = prior_diagonal[:, None, None, :]
        weighted = (noise_weight[:, :, None, :] * measured_visibility.astype(jnp.float32)).astype(
            jnp.bfloat16
        )
        rhs = chroma * jnp.einsum(
            "fmkb,mbs->fmks", weighted, beam_transfer, preferred_element_type=jnp.float32
        )

        assert resident_modes == 1
        if mode_devices % 16 == 0:
            cg_stages = [
                ("freq", [(1, freq_devices)]),
                ("ma", [(1, 2), (16, mode_devices // 16)]),
                ("ma", [(2, 8)]),
            ]
        else:
            cg_stages = [("freq", [(1, freq_devices)]), ("ma", [(1, mode_devices)])]
        diag_rows = prior_diagonal[:, None, :]
        mode_rows4 = prior_modes[:, :, None, :]

        def beam_back(direction):
            low = (chroma * direction).astype(jnp.bfloat16)
            seen = jnp.einsum("fmks,mbs->fmkb", low, beam_transfer, preferred_element_type=jnp.float32)
            heard = (noise_weight[:, :, None, :] * seen).astype(jnp.bfloat16)
            back = jnp.einsum(
                "fmkb,mbs->fmks", heard, beam_transfer, preferred_element_type=jnp.float32
            )
            return (chroma * back)[:, 0]

        direction = rhs[:, 0]
        operands = (beam_transfer[0], chromatic_gain[:, None, :], noise_weight, diag_rows, mode_rows4)
        estimate = cg_solve(axis_names, cg_stages, direction, *operands)
        estimate = estimate[:, None]
        return estimate

    return shards


def solution(mesh):
    in_specs = (
        P("freq", "ma", None, None),
        P("ma", None, None),
        P("freq", None),
        P("freq", "ma", None),
        P("freq", None),
        P("freq", None, None),
    )
    out_specs = P("freq", "ma", None, None)
    return jax.shard_map(make_shards(mesh), mesh=mesh, in_specs=in_specs, out_specs=out_specs, check_vma=False)
```

```python
import functools

import jax
import jax.numpy as jnp
from jax import lax
from jax.experimental import pallas as pl
from jax.experimental.pallas import tpu as pltpu
from jax.sharding import PartitionSpec as P

ITERS = 2
MESH = pl.DeviceIdType.MESH


def hartley_table(rows, cols):
    index_m = jnp.arange(rows, dtype=jnp.int32)[:, None]
    index_t = jnp.arange(cols, dtype=jnp.int32)[None, :]
    phase = (index_m * index_t % cols).astype(jnp.float32)
    angle = 2.0 * jnp.pi * phase / cols
    return (jnp.cos(angle) + jnp.sin(angle)) / jnp.sqrt(jnp.float32(cols))


def inner(left, right):
    return jnp.sum(left * right, axis=(0, 1, 3))


def reduce_kernel(axis_names, stages, x_ref, o_ref, cur, recv, send_sem, recv_sem):
    me = {name: lax.axis_index(name) for name in axis_names}

    def device(axis, coord):
        return tuple(coord if name == axis else me[name] for name in axis_names)

    plan = []
    base = 0
    for axis, stride, size in stages:
        own = (me[axis] // stride) % size
        root = me[axis] - own * stride
        peers = []
        for step in range(1, size):
            other = lax.rem(own + step, size)
            peers.append((other, device(axis, root + other * stride)))
        plan.append((base, own, size, peers))
        base += size

    barrier = pltpu.get_barrier_semaphore()
    for _, _, _, peers in plan:
        for _, peer in peers:
            pl.semaphore_signal(barrier, 1, device_id=peer, device_id_type=MESH)
    pl.semaphore_wait(barrier, sum(len(peers) for _, _, _, peers in plan))

    acc = x_ref[...].astype(jnp.float32)
    for index, (base, own, size, peers) in enumerate(plan):
        cur[index] = acc.astype(cur.dtype)
        copies = []
        for other, peer in peers:
            copy = pltpu.make_async_remote_copy(
                src_ref=cur.at[index],
                dst_ref=recv.at[base + own],
                send_sem=send_sem.at[base + other],
                recv_sem=recv_sem.at[base + own],
                device_id=peer,
                device_id_type=MESH,
            )
            copy.start()
            copies.append(copy)
        recv[base + own] = acc.astype(recv.dtype)
        for other, peer in peers:
            pltpu.make_async_remote_copy(
                src_ref=cur.at[index],
                dst_ref=recv.at[base + other],
                send_sem=send_sem.at[base + other],
                recv_sem=recv_sem.at[base + other],
                device_id=peer,
                device_id_type=MESH,
            ).wait_recv()
        for copy in copies:
            copy.wait_send()
        total = recv[base].astype(jnp.float32)
        for slot in range(1, size):
            total = total + recv[base + slot].astype(jnp.float32)
        acc = total
    o_ref[...] = acc.astype(o_ref.dtype)


def group_sum(x, axis_names, stages, wire_dtype, collective_id):
    slots = sum(size for _, _, size in stages)
    return pl.pallas_call(
        functools.partial(reduce_kernel, axis_names, stages),
        out_shape=jax.ShapeDtypeStruct(x.shape, jnp.float32),
        in_specs=[pl.BlockSpec(memory_space=pltpu.VMEM)],
        out_specs=pl.BlockSpec(memory_space=pltpu.VMEM),
        scratch_shapes=[
            pltpu.VMEM((len(stages),) + x.shape, wire_dtype),
            pltpu.VMEM((slots,) + x.shape, wire_dtype),
            pltpu.SemaphoreType.DMA((slots,)),
            pltpu.SemaphoreType.DMA((slots,)),
        ],
        compiler_params=pltpu.CompilerParams(collective_id=collective_id, has_side_effects=True),
    )(x)


def column_sum(x):
    return jnp.sum(jnp.sum(x, axis=0), axis=1, keepdims=True)


def to_row(columns):
    count = columns[0].shape[0]
    sub = lax.broadcasted_iota(jnp.int32, (count, 128), 0)
    lane = lax.broadcasted_iota(jnp.int32, (count, 128), 1)
    acc = jnp.zeros((count, 128), jnp.float32)
    for index, column in enumerate(columns):
        acc = acc + jnp.where(lane == sub + count * index, jnp.broadcast_to(column, (count, 128)), 0.0)
    return jnp.sum(acc, axis=0, keepdims=True)


def from_row(row, index, count):
    sub = lax.broadcasted_iota(jnp.int32, (count, 128), 0)
    lane = lax.broadcasted_iota(jnp.int32, (count, 128), 1)
    picked = jnp.where(lane == sub + count * index, jnp.broadcast_to(row, (count, 128)), 0.0)
    return jnp.sum(picked, axis=1, keepdims=True)


def group_size(stage):
    size = 1
    for _, extent in stage[1]:
        size *= extent
    return size


def cg_kernel(axis_names, stages, d_ref, beam_ref, chroma_ref, weight_ref, diag_ref, pm_ref,
              est_ref, next_ref, step_ref, parts, rows, recv_p, recv_rows, p_send, p_recv, r_send, r_recv):
    me = {name: lax.axis_index(name) for name in axis_names}

    def place(stage):
        axis, dims = stage
        own = 0
        root = me[axis]
        scale = 1
        for stride, size in dims:
            digit = lax.rem(me[axis] // stride, size)
            own = own + digit * scale
            root = root - digit * stride
            scale *= size

        def device(other):
            coord = root
            scale = 1
            for stride, size in dims:
                coord = coord + lax.rem(other // scale, size) * stride
                scale *= size
            return tuple(coord if name == axis else me[name] for name in axis_names)

        return own, device

    barrier = pltpu.get_barrier_semaphore()
    for stage in stages:
        own, device = place(stage)
        for step in range(1, group_size(stage)):
            other = lax.rem(own + step, group_size(stage))
            pl.semaphore_signal(barrier, 1, device_id=device(other), device_id_type=MESH)

    chroma = chroma_ref[...]
    weight = weight_ref[...]
    diag = diag_ref[...]
    pm = pm_ref[...]
    d = d_ref[...]
    channels, count, modes = d.shape

    def beam_forward(vector):
        low = (chroma * vector).astype(jnp.bfloat16).reshape(channels * count, modes)
        seen = lax.dot_general(
            low, beam_ref[...], (((1,), (1,)), ((), ())), preferred_element_type=jnp.float32
        )
        return (weight * seen.reshape(channels, count, -1)).astype(jnp.bfloat16)

    def beam_backward(heard):
        back = jnp.dot(heard.reshape(channels * count, -1), beam_ref[...], preferred_element_type=jnp.float32)
        return chroma * back.reshape(channels, count, modes)

    heard = beam_forward(d)
    pl.semaphore_wait(barrier, sum(group_size(stage) - 1 for stage in stages))

    def exchange_start(stage, src, recv, base, send_sems, recv_sems):
        own, device = place(stage)
        size = group_size(stage)

        def copy_to(other, slot):
            return pltpu.make_async_remote_copy(
                src_ref=src,
                dst_ref=recv.at[base + slot],
                send_sem=send_sems.at[base + other],
                recv_sem=recv_sems.at[base + slot],
                device_id=device(other),
                device_id_type=MESH,
            )

        for step in range(1, size):
            copy_to(lax.rem(own + step, size), own).start()
        recv[base + own] = src[...]
        return own, size, base, recv, copy_to

    sent = []

    def exchange_finish(state):
        own, size, base, recv, copy_to = state
        for step in range(1, size):
            other = lax.rem(own + step, size)
            copy_to(other, other).wait_recv()
        sent.append(state)
        total = recv[base].astype(jnp.float32)
        for slot in range(1, size):
            total = total + recv[base + slot].astype(jnp.float32)
        return total

    counter = {"row": 0, "slot": 0, "part": 0}

    def next_row(value):
        index = counter["row"]
        counter["row"] += 1
        rows[index] = value
        return rows.at[index]

    def row_stage(stage, src):
        base = counter["slot"]
        counter["slot"] += group_size(stage)
        return exchange_start(stage, src, recv_rows, base, r_send, r_recv)

    def reduce_rest(value):
        for stage in stages[1:]:
            value = exchange_finish(row_stage(stage, next_row(value)))
        return value

    def projection_start(vector):
        index = counter["part"]
        counter["part"] += 1
        for rank in range(pm.shape[1]):
            parts[index, rank] = jnp.sum(pm[:, rank] * vector, axis=0).astype(parts.dtype)
        nz = group_size(stages[0])
        return exchange_start(stages[0], parts.at[index], recv_p, index * nz, p_send, p_recv)

    p_state = projection_start(d)
    cb = beam_backward(heard)
    z_state = row_stage(stages[0], next_row(to_row([column_sum(d * (cb + diag * d)), column_sum(d * d)])))
    projection = exchange_finish(p_state)
    zrow = exchange_finish(z_state)
    total = reduce_rest(zrow + to_row([column_sum(projection * projection)]))
    curve = from_row(total, 0, count)
    norm_now = from_row(total, 1, count)
    step_size = (norm_now / curve)[None]
    estimate = step_size * d
    spread = pm[:, 0] * projection[0][None]
    for rank in range(1, pm.shape[1]):
        spread = spread + pm[:, rank] * projection[rank][None]
    residual = d - step_size * (cb + diag * d + spread)
    z_state = row_stage(stages[0], next_row(to_row([column_sum(residual * residual)])))
    p_state = projection_start(residual)
    cb_residual = beam_backward(beam_forward(residual))
    total = reduce_rest(exchange_finish(z_state))
    projection_residual = exchange_finish(p_state)
    norm_next = from_row(total, 0, count)
    ratio = (norm_next / norm_now)[None]
    direction = residual + ratio * d
    cb_direction = cb_residual + ratio * cb
    projection = projection_residual + ratio * projection
    zrow = exchange_finish(
        row_stage(stages[0], next_row(to_row([column_sum(direction * (cb_direction + diag * direction))])))
    )
    total = reduce_rest(zrow + to_row([column_sum(projection * projection)]))
    curve = from_row(total, 0, count)
    est_ref[...] = estimate
    next_ref[...] = direction
    step_ref[...] = to_row([norm_next / curve])
    for own, size, _, _, copy_to in sent:
        for step in range(1, size):
            copy_to(lax.rem(own + step, size), own).wait_send()


def cg_solve(axis_names, stages, d, beam, chroma, weight, diag, pm):
    reductions = 3
    slots = reductions * sum(group_size(stage) for stage in stages)
    rounds = reductions * len(stages)
    nz = group_size(stages[0])
    vector = jax.ShapeDtypeStruct(d.shape, jnp.float32)
    row = jax.ShapeDtypeStruct((1, 128), jnp.float32)
    vmem = pl.BlockSpec(memory_space=pltpu.VMEM)
    part_shape = (pm.shape[1],) + d.shape[1:]
    estimate, direction, step_row = pl.pallas_call(
        functools.partial(cg_kernel, axis_names, stages),
        out_shape=(vector, vector, row),
        in_specs=[vmem] * 6,
        out_specs=(vmem, vmem, vmem),
        scratch_shapes=[
            pltpu.VMEM((2,) + part_shape, jnp.bfloat16),
            pltpu.VMEM((rounds, 1, 128), jnp.float32),
            pltpu.VMEM((2 * nz,) + part_shape, jnp.bfloat16),
            pltpu.VMEM((slots, 1, 128), jnp.float32),
            pltpu.SemaphoreType.DMA((2 * nz,)),
            pltpu.SemaphoreType.DMA((2 * nz,)),
            pltpu.SemaphoreType.DMA((slots,)),
            pltpu.SemaphoreType.DMA((slots,)),
        ],
        compiler_params=pltpu.CompilerParams(collective_id=1, has_side_effects=True),
    )(d, beam, chroma, weight, diag, pm)
    step_size = step_row[0, : d.shape[1]]
    return estimate + step_size[None, :, None] * direction


def make_shards(mesh):
    axis_names = tuple(mesh.axis_names)
    mode_devices = mesh.shape["ma"]
    freq_devices = mesh.shape["freq"]
    if mode_devices % 16 == 0:
        mode_stages = [("ma", 1, 2), ("ma", 2, 8), ("ma", 16, mode_devices // 16)]
    else:
        mode_stages = [("ma", 1, mode_devices)]
    global_stages = mode_stages + [("freq", 1, freq_devices)]
    freq_stages = [("freq", 1, freq_devices)]

    def scalar_sum(*vectors):
        rows = jnp.stack(vectors)
        padded = jnp.pad(rows, ((0, 8 - rows.shape[0]), (0, 128 - rows.shape[1])))
        summed = group_sum(padded, axis_names, global_stages, jnp.float32, 2)
        return [summed[index, : rows.shape[1]] for index in range(len(vectors))]

    def freq_sum(partial_sum):
        shape = partial_sum.shape
        flat = partial_sum.reshape(-1, shape[-1])
        summed = group_sum(flat, axis_names, freq_stages, jnp.bfloat16, 1)
        return summed.reshape(shape)

    def shards(timestream, beam_transfer, chromatic_gain, noise_weight, prior_diagonal, prior_modes):
        spectral_channels = timestream.shape[0]
        device_time_samples = timestream.shape[1]
        noise_realizations = timestream.shape[2]
        antenna_pairs = timestream.shape[3]
        mode_devices_here = mode_devices
        columns = noise_realizations * antenna_pairs // mode_devices_here
        blocks = antenna_pairs // columns
        halves = columns // 128
        send = timestream.reshape(
            spectral_channels, device_time_samples, noise_realizations, blocks, halves, 128
        ).transpose(2, 3, 0, 1, 4, 5)
        send = send.reshape(mode_devices_here, spectral_channels * device_time_samples * halves, 128)
        received = lax.all_to_all(send, "ma", 0, 0, tiled=True)
        received = received.reshape(mode_devices_here, spectral_channels, device_time_samples, columns)
        all_times = mode_devices_here * device_time_samples
        hartley = hartley_table(all_times // 2, all_times)
        hartley_high = hartley.astype(jnp.bfloat16)
        hartley_low = (hartley - hartley_high.astype(jnp.float32)).astype(jnp.bfloat16)
        hartley_high = hartley_high.reshape(all_times // 2, mode_devices_here, device_time_samples)
        hartley_low = hartley_low.reshape(all_times // 2, mode_devices_here, device_time_samples)
        mode_high = jnp.einsum(
            "mit,iftc->mfc", hartley_high, received, preferred_element_type=jnp.float32
        )
        mode_low = jnp.einsum("mit,iftc->mfc", hartley_low, received, preferred_element_type=jnp.float32)
        mode_rows = (mode_high + mode_low).astype(jnp.bfloat16)
        back_rows = lax.all_to_all(mode_rows, "ma", 0, 0, tiled=True)
        resident_modes = back_rows.shape[0] // mode_devices_here
        back_rows = back_rows.reshape(
            noise_realizations, blocks, resident_modes, spectral_channels, columns
        )
        measured_visibility = back_rows.transpose(3, 2, 0, 1, 4).reshape(
            spectral_channels, resident_modes, noise_realizations, antenna_pairs
        )
        chroma = chromatic_gain[:, None, None, :]
        diagonal = prior_diagonal[:, None, None, :]
        weighted = (noise_weight[:, :, None, :] * measured_visibility.astype(jnp.float32)).astype(
            jnp.bfloat16
        )
        rhs = chroma * jnp.einsum(
            "fmkb,mbs->fmks", weighted, beam_transfer, preferred_element_type=jnp.float32
        )

        assert resident_modes == 1
        if mode_devices % 16 == 0:
            cg_stages = [
                ("freq", [(1, freq_devices)]),
                ("ma", [(1, 2), (16, mode_devices // 16)]),
                ("ma", [(2, 8)]),
            ]
        else:
            cg_stages = [("freq", [(1, freq_devices)]), ("ma", [(1, mode_devices)])]
        diag_rows = prior_diagonal[:, None, :]
        mode_rows4 = prior_modes[:, :, None, :]

        def beam_back(direction):
            low = (chroma * direction).astype(jnp.bfloat16)
            seen = jnp.einsum("fmks,mbs->fmkb", low, beam_transfer, preferred_element_type=jnp.float32)
            heard = (noise_weight[:, :, None, :] * seen).astype(jnp.bfloat16)
            back = jnp.einsum(
                "fmkb,mbs->fmks", heard, beam_transfer, preferred_element_type=jnp.float32
            )
            return (chroma * back)[:, 0]

        direction = rhs[:, 0]
        operands = (beam_transfer[0], chromatic_gain[:, None, :], noise_weight, diag_rows, mode_rows4)
        estimate = cg_solve(axis_names, cg_stages, direction, *operands)
        estimate = estimate[:, None]
        return estimate

    return shards


def solution(mesh):
    in_specs = (
        P("freq", "ma", None, None),
        P("ma", None, None),
        P("freq", None),
        P("freq", "ma", None),
        P("freq", None),
        P("freq", None, None),
    )
    out_specs = P("freq", "ma", None, None)
    return jax.shard_map(make_shards(mesh), mesh=mesh, in_specs=in_specs, out_specs=out_specs, check_vma=False)
```

```python
import functools

import jax
import jax.numpy as jnp
from jax import lax
from jax.experimental import pallas as pl
from jax.experimental.pallas import tpu as pltpu
from jax.sharding import PartitionSpec as P

ITERS = 2
MESH = pl.DeviceIdType.MESH


def hartley_table(rows, cols):
    index_m = jnp.arange(rows, dtype=jnp.int32)[:, None]
    index_t = jnp.arange(cols, dtype=jnp.int32)[None, :]
    phase = (index_m * index_t % cols).astype(jnp.float32)
    angle = 2.0 * jnp.pi * phase / cols
    return (jnp.cos(angle) + jnp.sin(angle)) / jnp.sqrt(jnp.float32(cols))


def inner(left, right):
    return jnp.sum(left * right, axis=(0, 1, 3))


def reduce_kernel(axis_names, stages, x_ref, o_ref, cur, recv, send_sem, recv_sem):
    me = {name: lax.axis_index(name) for name in axis_names}

    def device(axis, coord):
        return tuple(coord if name == axis else me[name] for name in axis_names)

    plan = []
    base = 0
    for axis, stride, size in stages:
        own = (me[axis] // stride) % size
        root = me[axis] - own * stride
        peers = []
        for step in range(1, size):
            other = lax.rem(own + step, size)
            peers.append((other, device(axis, root + other * stride)))
        plan.append((base, own, size, peers))
        base += size

    barrier = pltpu.get_barrier_semaphore()
    for _, _, _, peers in plan:
        for _, peer in peers:
            pl.semaphore_signal(barrier, 1, device_id=peer, device_id_type=MESH)
    pl.semaphore_wait(barrier, sum(len(peers) for _, _, _, peers in plan))

    acc = x_ref[...].astype(jnp.float32)
    for index, (base, own, size, peers) in enumerate(plan):
        cur[index] = acc.astype(cur.dtype)
        copies = []
        for other, peer in peers:
            copy = pltpu.make_async_remote_copy(
                src_ref=cur.at[index],
                dst_ref=recv.at[base + own],
                send_sem=send_sem.at[base + other],
                recv_sem=recv_sem.at[base + own],
                device_id=peer,
                device_id_type=MESH,
            )
            copy.start()
            copies.append(copy)
        recv[base + own] = acc.astype(recv.dtype)
        for other, peer in peers:
            pltpu.make_async_remote_copy(
                src_ref=cur.at[index],
                dst_ref=recv.at[base + other],
                send_sem=send_sem.at[base + other],
                recv_sem=recv_sem.at[base + other],
                device_id=peer,
                device_id_type=MESH,
            ).wait_recv()
        for copy in copies:
            copy.wait_send()
        total = recv[base].astype(jnp.float32)
        for slot in range(1, size):
            total = total + recv[base + slot].astype(jnp.float32)
        acc = total
    o_ref[...] = acc.astype(o_ref.dtype)


def group_sum(x, axis_names, stages, wire_dtype, collective_id):
    slots = sum(size for _, _, size in stages)
    return pl.pallas_call(
        functools.partial(reduce_kernel, axis_names, stages),
        out_shape=jax.ShapeDtypeStruct(x.shape, jnp.float32),
        in_specs=[pl.BlockSpec(memory_space=pltpu.VMEM)],
        out_specs=pl.BlockSpec(memory_space=pltpu.VMEM),
        scratch_shapes=[
            pltpu.VMEM((len(stages),) + x.shape, wire_dtype),
            pltpu.VMEM((slots,) + x.shape, wire_dtype),
            pltpu.SemaphoreType.DMA((slots,)),
            pltpu.SemaphoreType.DMA((slots,)),
        ],
        compiler_params=pltpu.CompilerParams(collective_id=collective_id, has_side_effects=True),
    )(x)


def column_sum(x):
    return jnp.sum(jnp.sum(x, axis=0), axis=1, keepdims=True)


def to_row(columns):
    count = columns[0].shape[0]
    sub = lax.broadcasted_iota(jnp.int32, (count, 128), 0)
    lane = lax.broadcasted_iota(jnp.int32, (count, 128), 1)
    acc = jnp.zeros((count, 128), jnp.float32)
    for index, column in enumerate(columns):
        acc = acc + jnp.where(lane == sub + count * index, jnp.broadcast_to(column, (count, 128)), 0.0)
    return jnp.sum(acc, axis=0, keepdims=True)


def from_row(row, index, count):
    sub = lax.broadcasted_iota(jnp.int32, (count, 128), 0)
    lane = lax.broadcasted_iota(jnp.int32, (count, 128), 1)
    picked = jnp.where(lane == sub + count * index, jnp.broadcast_to(row, (count, 128)), 0.0)
    return jnp.sum(picked, axis=1, keepdims=True)


def group_size(stage):
    size = 1
    for _, extent in stage[1]:
        size *= extent
    return size


def cg_kernel(axis_names, stages, d_ref, beam_ref, chroma_ref, weight_ref, diag_ref, pm_ref,
              est_ref, next_ref, step_ref, parts, rows, recv_p, recv_rows, p_send, p_recv, r_send, r_recv):
    me = {name: lax.axis_index(name) for name in axis_names}

    def place(stage):
        axis, dims = stage
        own = 0
        root = me[axis]
        scale = 1
        for stride, size in dims:
            digit = lax.rem(me[axis] // stride, size)
            own = own + digit * scale
            root = root - digit * stride
            scale *= size

        def device(other):
            coord = root
            scale = 1
            for stride, size in dims:
                coord = coord + lax.rem(other // scale, size) * stride
                scale *= size
            return tuple(coord if name == axis else me[name] for name in axis_names)

        return own, device

    barrier = pltpu.get_barrier_semaphore()
    for stage in stages:
        own, device = place(stage)
        for step in range(1, group_size(stage)):
            other = lax.rem(own + step, group_size(stage))
            pl.semaphore_signal(barrier, 1, device_id=device(other), device_id_type=MESH)

    chroma = chroma_ref[...]
    weight = weight_ref[...]
    diag = diag_ref[...]
    pm = pm_ref[...]
    channels, count = d_ref.shape[:2]
    modes = beam_ref.shape[1]

    def beam_forward(vector):
        low = (chroma * vector).astype(jnp.bfloat16).reshape(channels * count, modes)
        seen = lax.dot_general(
            low, beam_ref[...], (((1,), (1,)), ((), ())), preferred_element_type=jnp.float32
        )
        return (weight * seen.reshape(channels, count, -1)).astype(jnp.bfloat16)

    def beam_backward(heard):
        back = jnp.dot(heard.reshape(channels * count, -1), beam_ref[...], preferred_element_type=jnp.float32)
        return chroma * back.reshape(channels, count, modes)

    d = beam_backward(d_ref[...])
    heard = beam_forward(d)
    pl.semaphore_wait(barrier, sum(group_size(stage) - 1 for stage in stages))

    def exchange_start(stage, src, recv, base, send_sems, recv_sems):
        own, device = place(stage)
        size = group_size(stage)

        def copy_to(other, slot):
            return pltpu.make_async_remote_copy(
                src_ref=src,
                dst_ref=recv.at[base + slot],
                send_sem=send_sems.at[base + other],
                recv_sem=recv_sems.at[base + slot],
                device_id=device(other),
                device_id_type=MESH,
            )

        for step in range(1, size):
            copy_to(lax.rem(own + step, size), own).start()
        recv[base + own] = src[...]
        return own, size, base, recv, copy_to

    sent = []

    def exchange_finish(state):
        own, size, base, recv, copy_to = state
        for step in range(1, size):
            other = lax.rem(own + step, size)
            copy_to(other, other).wait_recv()
        sent.append(state)
        total = recv[base].astype(jnp.float32)
        for slot in range(1, size):
            total = total + recv[base + slot].astype(jnp.float32)
        return total

    counter = {"row": 0, "slot": 0, "part": 0}

    def next_row(value):
        index = counter["row"]
        counter["row"] += 1
        rows[index] = value
        return rows.at[index]

    def row_stage(stage, src):
        base = counter["slot"]
        counter["slot"] += group_size(stage)
        return exchange_start(stage, src, recv_rows, base, r_send, r_recv)

    def reduce_rest(value):
        for stage in stages[1:]:
            value = exchange_finish(row_stage(stage, next_row(value)))
        return value

    def projection_start(vector):
        index = counter["part"]
        counter["part"] += 1
        for rank in range(pm.shape[1]):
            parts[index, rank] = jnp.sum(pm[:, rank] * vector, axis=0).astype(parts.dtype)
        nz = group_size(stages[0])
        return exchange_start(stages[0], parts.at[index], recv_p, index * nz, p_send, p_recv)

    p_state = projection_start(d)
    cb = beam_backward(heard)
    z_state = row_stage(stages[0], next_row(to_row([column_sum(d * (cb + diag * d)), column_sum(d * d)])))
    projection = exchange_finish(p_state)
    zrow = exchange_finish(z_state)
    total = reduce_rest(zrow + to_row([column_sum(projection * projection)]))
    curve = from_row(total, 0, count)
    norm_now = from_row(total, 1, count)
    step_size = (norm_now / curve)[None]
    estimate = step_size * d
    spread = pm[:, 0] * projection[0][None]
    for rank in range(1, pm.shape[1]):
        spread = spread + pm[:, rank] * projection[rank][None]
    residual = d - step_size * (cb + diag * d + spread)
    z_state = row_stage(stages[0], next_row(to_row([column_sum(residual * residual)])))
    p_state = projection_start(residual)
    cb_residual = beam_backward(beam_forward(residual))
    total = reduce_rest(exchange_finish(z_state))
    projection_residual = exchange_finish(p_state)
    norm_next = from_row(total, 0, count)
    ratio = (norm_next / norm_now)[None]
    direction = residual + ratio * d
    cb_direction = cb_residual + ratio * cb
    projection = projection_residual + ratio * projection
    zrow = exchange_finish(
        row_stage(stages[0], next_row(to_row([column_sum(direction * (cb_direction + diag * direction))])))
    )
    total = reduce_rest(zrow + to_row([column_sum(projection * projection)]))
    curve = from_row(total, 0, count)
    est_ref[...] = estimate
    next_ref[...] = direction
    step_ref[...] = to_row([norm_next / curve])
    for own, size, _, _, copy_to in sent:
        for step in range(1, size):
            copy_to(lax.rem(own + step, size), own).wait_send()


def cg_solve(axis_names, stages, d, beam, chroma, weight, diag, pm):
    reductions = 3
    slots = reductions * sum(group_size(stage) for stage in stages)
    rounds = reductions * len(stages)
    nz = group_size(stages[0])
    vector = jax.ShapeDtypeStruct(d.shape[:2] + beam.shape[1:], jnp.float32)
    row = jax.ShapeDtypeStruct((1, 128), jnp.float32)
    vmem = pl.BlockSpec(memory_space=pltpu.VMEM)
    part_shape = (pm.shape[1],) + vector.shape[1:]
    estimate, direction, step_row = pl.pallas_call(
        functools.partial(cg_kernel, axis_names, stages),
        out_shape=(vector, vector, row),
        in_specs=[vmem] * 6,
        out_specs=(vmem, vmem, vmem),
        scratch_shapes=[
            pltpu.VMEM((2,) + part_shape, jnp.bfloat16),
            pltpu.VMEM((rounds, 1, 128), jnp.float32),
            pltpu.VMEM((2 * nz,) + part_shape, jnp.bfloat16),
            pltpu.VMEM((slots, 1, 128), jnp.float32),
            pltpu.SemaphoreType.DMA((2 * nz,)),
            pltpu.SemaphoreType.DMA((2 * nz,)),
            pltpu.SemaphoreType.DMA((slots,)),
            pltpu.SemaphoreType.DMA((slots,)),
        ],
        compiler_params=pltpu.CompilerParams(collective_id=1, has_side_effects=True),
    )(d, beam, chroma, weight, diag, pm)
    step_size = step_row[0, : d.shape[1]]
    return estimate + step_size[None, :, None] * direction


def make_shards(mesh):
    axis_names = tuple(mesh.axis_names)
    mode_devices = mesh.shape["ma"]
    freq_devices = mesh.shape["freq"]
    if mode_devices % 16 == 0:
        mode_stages = [("ma", 1, 2), ("ma", 2, 8), ("ma", 16, mode_devices // 16)]
    else:
        mode_stages = [("ma", 1, mode_devices)]
    global_stages = mode_stages + [("freq", 1, freq_devices)]
    freq_stages = [("freq", 1, freq_devices)]

    def scalar_sum(*vectors):
        rows = jnp.stack(vectors)
        padded = jnp.pad(rows, ((0, 8 - rows.shape[0]), (0, 128 - rows.shape[1])))
        summed = group_sum(padded, axis_names, global_stages, jnp.float32, 2)
        return [summed[index, : rows.shape[1]] for index in range(len(vectors))]

    def freq_sum(partial_sum):
        shape = partial_sum.shape
        flat = partial_sum.reshape(-1, shape[-1])
        summed = group_sum(flat, axis_names, freq_stages, jnp.bfloat16, 1)
        return summed.reshape(shape)

    def shards(timestream, beam_transfer, chromatic_gain, noise_weight, prior_diagonal, prior_modes):
        spectral_channels = timestream.shape[0]
        device_time_samples = timestream.shape[1]
        noise_realizations = timestream.shape[2]
        antenna_pairs = timestream.shape[3]
        mode_devices_here = mode_devices
        columns = noise_realizations * antenna_pairs // mode_devices_here
        blocks = antenna_pairs // columns
        halves = columns // 128
        send = timestream.reshape(
            spectral_channels, device_time_samples, noise_realizations, blocks, halves, 128
        ).transpose(2, 3, 0, 1, 4, 5)
        send = send.reshape(mode_devices_here, spectral_channels * device_time_samples * halves, 128)
        received = lax.all_to_all(send, "ma", 0, 0, tiled=True)
        received = received.reshape(mode_devices_here, spectral_channels, device_time_samples, columns)
        all_times = mode_devices_here * device_time_samples
        hartley = hartley_table(all_times // 2, all_times)
        hartley_high = hartley.astype(jnp.bfloat16)
        hartley_low = (hartley - hartley_high.astype(jnp.float32)).astype(jnp.bfloat16)
        hartley_high = hartley_high.reshape(all_times // 2, mode_devices_here, device_time_samples)
        hartley_low = hartley_low.reshape(all_times // 2, mode_devices_here, device_time_samples)
        mode_high = jnp.einsum(
            "mit,iftc->mfc", hartley_high, received, preferred_element_type=jnp.float32
        )
        mode_low = jnp.einsum("mit,iftc->mfc", hartley_low, received, preferred_element_type=jnp.float32)
        mode_rows = (mode_high + mode_low).astype(jnp.bfloat16)
        back_rows = lax.all_to_all(mode_rows, "ma", 0, 0, tiled=True)
        resident_modes = back_rows.shape[0] // mode_devices_here
        back_rows = back_rows.reshape(
            noise_realizations, blocks, resident_modes, spectral_channels, columns
        )
        measured_visibility = back_rows.transpose(3, 2, 0, 1, 4).reshape(
            spectral_channels, resident_modes, noise_realizations, antenna_pairs
        )
        chroma = chromatic_gain[:, None, None, :]
        diagonal = prior_diagonal[:, None, None, :]
        weighted = (noise_weight[:, :, None, :] * measured_visibility.astype(jnp.float32)).astype(
            jnp.bfloat16
        )

        assert resident_modes == 1
        if mode_devices % 16 == 0:
            cg_stages = [
                ("freq", [(1, freq_devices)]),
                ("ma", [(1, 2), (16, mode_devices // 16)]),
                ("ma", [(2, 8)]),
            ]
        else:
            cg_stages = [("freq", [(1, freq_devices)]), ("ma", [(1, mode_devices)])]
        diag_rows = prior_diagonal[:, None, :]
        mode_rows4 = prior_modes[:, :, None, :]

        def beam_back(direction):
            low = (chroma * direction).astype(jnp.bfloat16)
            seen = jnp.einsum("fmks,mbs->fmkb", low, beam_transfer, preferred_element_type=jnp.float32)
            heard = (noise_weight[:, :, None, :] * seen).astype(jnp.bfloat16)
            back = jnp.einsum(
                "fmkb,mbs->fmks", heard, beam_transfer, preferred_element_type=jnp.float32
            )
            return (chroma * back)[:, 0]

        direction = weighted[:, 0]
        operands = (beam_transfer[0], chromatic_gain[:, None, :], noise_weight, diag_rows, mode_rows4)
        estimate = cg_solve(axis_names, cg_stages, direction, *operands)
        estimate = estimate[:, None]
        return estimate

    return shards


def solution(mesh):
    in_specs = (
        P("freq", "ma", None, None),
        P("ma", None, None),
        P("freq", None),
        P("freq", "ma", None),
        P("freq", None),
        P("freq", None, None),
    )
    out_specs = P("freq", "ma", None, None)
    return jax.shard_map(make_shards(mesh), mesh=mesh, in_specs=in_specs, out_specs=out_specs, check_vma=False)
```

```python
import functools

import jax
import jax.numpy as jnp
from jax import lax
from jax.experimental import pallas as pl
from jax.experimental.pallas import tpu as pltpu
from jax.sharding import PartitionSpec as P

ITERS = 2
MESH = pl.DeviceIdType.MESH


def hartley_table(rows, cols):
    index_m = jnp.arange(rows, dtype=jnp.int32)[:, None]
    index_t = jnp.arange(cols, dtype=jnp.int32)[None, :]
    phase = (index_m * index_t % cols).astype(jnp.float32)
    angle = 2.0 * jnp.pi * phase / cols
    return (jnp.cos(angle) + jnp.sin(angle)) / jnp.sqrt(jnp.float32(cols))


def inner(left, right):
    return jnp.sum(left * right, axis=(0, 1, 3))


def reduce_kernel(axis_names, stages, x_ref, o_ref, cur, recv, send_sem, recv_sem):
    me = {name: lax.axis_index(name) for name in axis_names}

    def device(axis, coord):
        return tuple(coord if name == axis else me[name] for name in axis_names)

    plan = []
    base = 0
    for axis, stride, size in stages:
        own = (me[axis] // stride) % size
        root = me[axis] - own * stride
        peers = []
        for step in range(1, size):
            other = lax.rem(own + step, size)
            peers.append((other, device(axis, root + other * stride)))
        plan.append((base, own, size, peers))
        base += size

    barrier = pltpu.get_barrier_semaphore()
    for _, _, _, peers in plan:
        for _, peer in peers:
            pl.semaphore_signal(barrier, 1, device_id=peer, device_id_type=MESH)
    pl.semaphore_wait(barrier, sum(len(peers) for _, _, _, peers in plan))

    acc = x_ref[...].astype(jnp.float32)
    for index, (base, own, size, peers) in enumerate(plan):
        cur[index] = acc.astype(cur.dtype)
        copies = []
        for other, peer in peers:
            copy = pltpu.make_async_remote_copy(
                src_ref=cur.at[index],
                dst_ref=recv.at[base + own],
                send_sem=send_sem.at[base + other],
                recv_sem=recv_sem.at[base + own],
                device_id=peer,
                device_id_type=MESH,
            )
            copy.start()
            copies.append(copy)
        recv[base + own] = acc.astype(recv.dtype)
        for other, peer in peers:
            pltpu.make_async_remote_copy(
                src_ref=cur.at[index],
                dst_ref=recv.at[base + other],
                send_sem=send_sem.at[base + other],
                recv_sem=recv_sem.at[base + other],
                device_id=peer,
                device_id_type=MESH,
            ).wait_recv()
        for copy in copies:
            copy.wait_send()
        total = recv[base].astype(jnp.float32)
        for slot in range(1, size):
            total = total + recv[base + slot].astype(jnp.float32)
        acc = total
    o_ref[...] = acc.astype(o_ref.dtype)


def group_sum(x, axis_names, stages, wire_dtype, collective_id):
    slots = sum(size for _, _, size in stages)
    return pl.pallas_call(
        functools.partial(reduce_kernel, axis_names, stages),
        out_shape=jax.ShapeDtypeStruct(x.shape, jnp.float32),
        in_specs=[pl.BlockSpec(memory_space=pltpu.VMEM)],
        out_specs=pl.BlockSpec(memory_space=pltpu.VMEM),
        scratch_shapes=[
            pltpu.VMEM((len(stages),) + x.shape, wire_dtype),
            pltpu.VMEM((slots,) + x.shape, wire_dtype),
            pltpu.SemaphoreType.DMA((slots,)),
            pltpu.SemaphoreType.DMA((slots,)),
        ],
        compiler_params=pltpu.CompilerParams(collective_id=collective_id, has_side_effects=True),
    )(x)


def column_sum(x):
    return jnp.sum(jnp.sum(x, axis=0), axis=1, keepdims=True)


def to_row(columns):
    count = columns[0].shape[0]
    sub = lax.broadcasted_iota(jnp.int32, (count, 128), 0)
    lane = lax.broadcasted_iota(jnp.int32, (count, 128), 1)
    acc = jnp.zeros((count, 128), jnp.float32)
    for index, column in enumerate(columns):
        acc = acc + jnp.where(lane == sub + count * index, jnp.broadcast_to(column, (count, 128)), 0.0)
    return jnp.sum(acc, axis=0, keepdims=True)


def from_row(row, index, count):
    sub = lax.broadcasted_iota(jnp.int32, (count, 128), 0)
    lane = lax.broadcasted_iota(jnp.int32, (count, 128), 1)
    picked = jnp.where(lane == sub + count * index, jnp.broadcast_to(row, (count, 128)), 0.0)
    return jnp.sum(picked, axis=1, keepdims=True)


def group_size(stage):
    size = 1
    for _, extent in stage[1]:
        size *= extent
    return size


def cg_kernel(axis_names, stages, d_ref, beam_ref, chroma_ref, weight_ref, diag_ref, pm_ref,
              est_ref, next_ref, step_ref, parts, rows, recv_p, recv_rows, p_send, p_recv, r_send, r_recv):
    me = {name: lax.axis_index(name) for name in axis_names}

    def place(stage):
        axis, dims = stage
        own = 0
        root = me[axis]
        scale = 1
        for stride, size in dims:
            digit = lax.rem(me[axis] // stride, size)
            own = own + digit * scale
            root = root - digit * stride
            scale *= size

        def device(other):
            coord = root
            scale = 1
            for stride, size in dims:
                coord = coord + lax.rem(other // scale, size) * stride
                scale *= size
            return tuple(coord if name == axis else me[name] for name in axis_names)

        return own, device

    barrier = pltpu.get_barrier_semaphore()
    for stage in stages:
        own, device = place(stage)
        for step in range(1, group_size(stage)):
            other = lax.rem(own + step, group_size(stage))
            pl.semaphore_signal(barrier, 1, device_id=device(other), device_id_type=MESH)

    chroma = chroma_ref[...]
    weight = weight_ref[...]
    diag = diag_ref[...]
    pm = pm_ref[...]
    channels, count = d_ref.shape[:2]
    modes = beam_ref.shape[1]

    def beam_forward(vector):
        low = (chroma * vector).astype(jnp.bfloat16).reshape(channels * count, modes)
        seen = lax.dot_general(
            low, beam_ref[...], (((1,), (1,)), ((), ())), preferred_element_type=jnp.float32
        )
        return (weight * seen.reshape(channels, count, -1)).astype(jnp.bfloat16)

    def beam_backward(heard):
        back = jnp.dot(heard.reshape(channels * count, -1), beam_ref[...], preferred_element_type=jnp.float32)
        return chroma * back.reshape(channels, count, modes)


    def exchange_start(stage, src, recv, base, send_sems, recv_sems):
        own, device = place(stage)
        size = group_size(stage)

        def copy_to(other, slot):
            return pltpu.make_async_remote_copy(
                src_ref=src,
                dst_ref=recv.at[base + slot],
                send_sem=send_sems.at[base + other],
                recv_sem=recv_sems.at[base + slot],
                device_id=device(other),
                device_id_type=MESH,
            )

        for step in range(1, size):
            copy_to(lax.rem(own + step, size), own).start()
        recv[base + own] = src[...]
        return own, size, base, recv, copy_to

    sent = []

    def exchange_finish(state):
        own, size, base, recv, copy_to = state
        for step in range(1, size):
            other = lax.rem(own + step, size)
            copy_to(other, other).wait_recv()
        sent.append(state)
        total = recv[base].astype(jnp.float32)
        for slot in range(1, size):
            total = total + recv[base + slot].astype(jnp.float32)
        return total

    counter = {"row": 0, "slot": 0, "part": 0}

    def next_row(value):
        index = counter["row"]
        counter["row"] += 1
        rows[index] = value
        return rows.at[index]

    def row_stage(stage, src):
        base = counter["slot"]
        counter["slot"] += group_size(stage)
        return exchange_start(stage, src, recv_rows, base, r_send, r_recv)

    def reduce_rest(value):
        for stage in stages[1:]:
            value = exchange_finish(row_stage(stage, next_row(value)))
        return value

    def projection_start(vector):
        index = counter["part"]
        counter["part"] += 1
        for rank in range(pm.shape[1]):
            parts[index, rank] = jnp.sum(pm[:, rank] * vector, axis=0).astype(parts.dtype)
        nz = group_size(stages[0])
        return exchange_start(stages[0], parts.at[index], recv_p, index * nz, p_send, p_recv)

    d = beam_backward(d_ref[...])
    pl.semaphore_wait(barrier, sum(group_size(stage) - 1 for stage in stages))
    p_state = projection_start(d)
    cb = beam_backward(beam_forward(d))
    z_state = row_stage(stages[0], next_row(to_row([column_sum(d * (cb + diag * d)), column_sum(d * d)])))
    projection = exchange_finish(p_state)
    zrow = exchange_finish(z_state)
    total = reduce_rest(zrow + to_row([column_sum(projection * projection)]))
    curve = from_row(total, 0, count)
    norm_now = from_row(total, 1, count)
    step_size = (norm_now / curve)[None]
    estimate = step_size * d
    spread = pm[:, 0] * projection[0][None]
    for rank in range(1, pm.shape[1]):
        spread = spread + pm[:, rank] * projection[rank][None]
    residual = d - step_size * (cb + diag * d + spread)
    z_state = row_stage(stages[0], next_row(to_row([column_sum(residual * residual)])))
    p_state = projection_start(residual)
    cb_residual = beam_backward(beam_forward(residual))
    total = reduce_rest(exchange_finish(z_state))
    projection_residual = exchange_finish(p_state)
    norm_next = from_row(total, 0, count)
    ratio = (norm_next / norm_now)[None]
    direction = residual + ratio * d
    cb_direction = cb_residual + ratio * cb
    projection = projection_residual + ratio * projection
    zrow = exchange_finish(
        row_stage(stages[0], next_row(to_row([column_sum(direction * (cb_direction + diag * direction))])))
    )
    total = reduce_rest(zrow + to_row([column_sum(projection * projection)]))
    curve = from_row(total, 0, count)
    est_ref[...] = estimate
    next_ref[...] = direction
    step_ref[...] = to_row([norm_next / curve])
    for own, size, _, _, copy_to in sent:
        for step in range(1, size):
            copy_to(lax.rem(own + step, size), own).wait_send()


def cg_solve(axis_names, stages, d, beam, chroma, weight, diag, pm):
    reductions = 3
    slots = reductions * sum(group_size(stage) for stage in stages)
    rounds = reductions * len(stages)
    nz = group_size(stages[0])
    vector = jax.ShapeDtypeStruct(d.shape[:2] + beam.shape[1:], jnp.float32)
    row = jax.ShapeDtypeStruct((1, 128), jnp.float32)
    vmem = pl.BlockSpec(memory_space=pltpu.VMEM)
    part_shape = (pm.shape[1],) + vector.shape[1:]
    estimate, direction, step_row = pl.pallas_call(
        functools.partial(cg_kernel, axis_names, stages),
        out_shape=(vector, vector, row),
        in_specs=[vmem] * 6,
        out_specs=(vmem, vmem, vmem),
        scratch_shapes=[
            pltpu.VMEM((2,) + part_shape, jnp.bfloat16),
            pltpu.VMEM((rounds, 1, 128), jnp.float32),
            pltpu.VMEM((2 * nz,) + part_shape, jnp.bfloat16),
            pltpu.VMEM((slots, 1, 128), jnp.float32),
            pltpu.SemaphoreType.DMA((2 * nz,)),
            pltpu.SemaphoreType.DMA((2 * nz,)),
            pltpu.SemaphoreType.DMA((slots,)),
            pltpu.SemaphoreType.DMA((slots,)),
        ],
        compiler_params=pltpu.CompilerParams(collective_id=1, has_side_effects=True),
    )(d, beam, chroma, weight, diag, pm)
    step_size = step_row[0, : d.shape[1]]
    return estimate + step_size[None, :, None] * direction


def make_shards(mesh):
    axis_names = tuple(mesh.axis_names)
    mode_devices = mesh.shape["ma"]
    freq_devices = mesh.shape["freq"]
    if mode_devices % 16 == 0:
        mode_stages = [("ma", 1, 2), ("ma", 2, 8), ("ma", 16, mode_devices // 16)]
    else:
        mode_stages = [("ma", 1, mode_devices)]
    global_stages = mode_stages + [("freq", 1, freq_devices)]
    freq_stages = [("freq", 1, freq_devices)]

    def scalar_sum(*vectors):
        rows = jnp.stack(vectors)
        padded = jnp.pad(rows, ((0, 8 - rows.shape[0]), (0, 128 - rows.shape[1])))
        summed = group_sum(padded, axis_names, global_stages, jnp.float32, 2)
        return [summed[index, : rows.shape[1]] for index in range(len(vectors))]

    def freq_sum(partial_sum):
        shape = partial_sum.shape
        flat = partial_sum.reshape(-1, shape[-1])
        summed = group_sum(flat, axis_names, freq_stages, jnp.bfloat16, 1)
        return summed.reshape(shape)

    def shards(timestream, beam_transfer, chromatic_gain, noise_weight, prior_diagonal, prior_modes):
        spectral_channels = timestream.shape[0]
        device_time_samples = timestream.shape[1]
        noise_realizations = timestream.shape[2]
        antenna_pairs = timestream.shape[3]
        mode_devices_here = mode_devices
        columns = noise_realizations * antenna_pairs // mode_devices_here
        blocks = antenna_pairs // columns
        halves = columns // 128
        send = timestream.reshape(
            spectral_channels, device_time_samples, noise_realizations, blocks, halves, 128
        ).transpose(2, 3, 0, 1, 4, 5)
        send = send.reshape(mode_devices_here, spectral_channels * device_time_samples * halves, 128)
        received = lax.all_to_all(send, "ma", 0, 0, tiled=True)
        received = received.reshape(mode_devices_here, spectral_channels, device_time_samples, columns)
        all_times = mode_devices_here * device_time_samples
        hartley = hartley_table(all_times // 2, all_times)
        hartley_high = hartley.astype(jnp.bfloat16)
        hartley_low = (hartley - hartley_high.astype(jnp.float32)).astype(jnp.bfloat16)
        hartley_high = hartley_high.reshape(all_times // 2, mode_devices_here, device_time_samples)
        hartley_low = hartley_low.reshape(all_times // 2, mode_devices_here, device_time_samples)
        mode_high = jnp.einsum(
            "mit,iftc->mfc", hartley_high, received, preferred_element_type=jnp.float32
        )
        mode_low = jnp.einsum("mit,iftc->mfc", hartley_low, received, preferred_element_type=jnp.float32)
        mode_rows = (mode_high + mode_low).astype(jnp.bfloat16)
        back_rows = lax.all_to_all(mode_rows, "ma", 0, 0, tiled=True)
        resident_modes = back_rows.shape[0] // mode_devices_here
        back_rows = back_rows.reshape(
            noise_realizations, blocks, resident_modes, spectral_channels, columns
        )
        measured_visibility = back_rows.transpose(3, 2, 0, 1, 4).reshape(
            spectral_channels, resident_modes, noise_realizations, antenna_pairs
        )
        chroma = chromatic_gain[:, None, None, :]
        diagonal = prior_diagonal[:, None, None, :]
        weighted = (noise_weight[:, :, None, :] * measured_visibility.astype(jnp.float32)).astype(
            jnp.bfloat16
        )

        assert resident_modes == 1
        if mode_devices % 16 == 0:
            cg_stages = [
                ("freq", [(1, freq_devices)]),
                ("ma", [(1, 2), (16, mode_devices // 16)]),
                ("ma", [(2, 8)]),
            ]
        else:
            cg_stages = [("freq", [(1, freq_devices)]), ("ma", [(1, mode_devices)])]
        diag_rows = prior_diagonal[:, None, :]
        mode_rows4 = prior_modes[:, :, None, :]

        def beam_back(direction):
            low = (chroma * direction).astype(jnp.bfloat16)
            seen = jnp.einsum("fmks,mbs->fmkb", low, beam_transfer, preferred_element_type=jnp.float32)
            heard = (noise_weight[:, :, None, :] * seen).astype(jnp.bfloat16)
            back = jnp.einsum(
                "fmkb,mbs->fmks", heard, beam_transfer, preferred_element_type=jnp.float32
            )
            return (chroma * back)[:, 0]

        direction = weighted[:, 0]
        operands = (beam_transfer[0], chromatic_gain[:, None, :], noise_weight, diag_rows, mode_rows4)
        estimate = cg_solve(axis_names, cg_stages, direction, *operands)
        estimate = estimate[:, None]
        return estimate

    return shards


def solution(mesh):
    in_specs = (
        P("freq", "ma", None, None),
        P("ma", None, None),
        P("freq", None),
        P("freq", "ma", None),
        P("freq", None),
        P("freq", None, None),
    )
    out_specs = P("freq", "ma", None, None)
    return jax.shard_map(make_shards(mesh), mesh=mesh, in_specs=in_specs, out_specs=out_specs, check_vma=False)
```

```python
import functools

import jax
import jax.numpy as jnp
from jax import lax
from jax.experimental import pallas as pl
from jax.experimental.pallas import tpu as pltpu
from jax.sharding import PartitionSpec as P

ITERS = 2
MESH = pl.DeviceIdType.MESH


def hartley_table(rows, cols):
    index_m = jnp.arange(rows, dtype=jnp.int32)[:, None]
    index_t = jnp.arange(cols, dtype=jnp.int32)[None, :]
    phase = (index_m * index_t % cols).astype(jnp.float32)
    angle = 2.0 * jnp.pi * phase / cols
    return (jnp.cos(angle) + jnp.sin(angle)) / jnp.sqrt(jnp.float32(cols))


def inner(left, right):
    return jnp.sum(left * right, axis=(0, 1, 3))


def reduce_kernel(axis_names, stages, x_ref, o_ref, cur, recv, send_sem, recv_sem):
    me = {name: lax.axis_index(name) for name in axis_names}

    def device(axis, coord):
        return tuple(coord if name == axis else me[name] for name in axis_names)

    plan = []
    base = 0
    for axis, stride, size in stages:
        own = (me[axis] // stride) % size
        root = me[axis] - own * stride
        peers = []
        for step in range(1, size):
            other = lax.rem(own + step, size)
            peers.append((other, device(axis, root + other * stride)))
        plan.append((base, own, size, peers))
        base += size

    barrier = pltpu.get_barrier_semaphore()
    for _, _, _, peers in plan:
        for _, peer in peers:
            pl.semaphore_signal(barrier, 1, device_id=peer, device_id_type=MESH)
    pl.semaphore_wait(barrier, sum(len(peers) for _, _, _, peers in plan))

    acc = x_ref[...].astype(jnp.float32)
    for index, (base, own, size, peers) in enumerate(plan):
        cur[index] = acc.astype(cur.dtype)
        copies = []
        for other, peer in peers:
            copy = pltpu.make_async_remote_copy(
                src_ref=cur.at[index],
                dst_ref=recv.at[base + own],
                send_sem=send_sem.at[base + other],
                recv_sem=recv_sem.at[base + own],
                device_id=peer,
                device_id_type=MESH,
            )
            copy.start()
            copies.append(copy)
        recv[base + own] = acc.astype(recv.dtype)
        for other, peer in peers:
            pltpu.make_async_remote_copy(
                src_ref=cur.at[index],
                dst_ref=recv.at[base + other],
                send_sem=send_sem.at[base + other],
                recv_sem=recv_sem.at[base + other],
                device_id=peer,
                device_id_type=MESH,
            ).wait_recv()
        for copy in copies:
            copy.wait_send()
        total = recv[base].astype(jnp.float32)
        for slot in range(1, size):
            total = total + recv[base + slot].astype(jnp.float32)
        acc = total
    o_ref[...] = acc.astype(o_ref.dtype)


def group_sum(x, axis_names, stages, wire_dtype, collective_id):
    slots = sum(size for _, _, size in stages)
    return pl.pallas_call(
        functools.partial(reduce_kernel, axis_names, stages),
        out_shape=jax.ShapeDtypeStruct(x.shape, jnp.float32),
        in_specs=[pl.BlockSpec(memory_space=pltpu.VMEM)],
        out_specs=pl.BlockSpec(memory_space=pltpu.VMEM),
        scratch_shapes=[
            pltpu.VMEM((len(stages),) + x.shape, wire_dtype),
            pltpu.VMEM((slots,) + x.shape, wire_dtype),
            pltpu.SemaphoreType.DMA((slots,)),
            pltpu.SemaphoreType.DMA((slots,)),
        ],
        compiler_params=pltpu.CompilerParams(collective_id=collective_id, has_side_effects=True),
    )(x)


def column_sum(x):
    return jnp.sum(jnp.sum(x, axis=0), axis=1, keepdims=True)


def to_row(columns):
    count = columns[0].shape[0]
    sub = lax.broadcasted_iota(jnp.int32, (count, 128), 0)
    lane = lax.broadcasted_iota(jnp.int32, (count, 128), 1)
    acc = jnp.zeros((count, 128), jnp.float32)
    for index, column in enumerate(columns):
        acc = acc + jnp.where(lane == sub + count * index, jnp.broadcast_to(column, (count, 128)), 0.0)
    return jnp.sum(acc, axis=0, keepdims=True)


def from_row(row, index, count):
    sub = lax.broadcasted_iota(jnp.int32, (count, 128), 0)
    lane = lax.broadcasted_iota(jnp.int32, (count, 128), 1)
    picked = jnp.where(lane == sub + count * index, jnp.broadcast_to(row, (count, 128)), 0.0)
    return jnp.sum(picked, axis=1, keepdims=True)


def group_size(stage):
    size = 1
    for _, extent in stage[1]:
        size *= extent
    return size


def cg_kernel(axis_names, stages, d_ref, beam_ref, chroma_ref, weight_ref, diag_ref, pm_ref,
              est_ref, next_ref, step_ref, parts, rows, recv_p, recv_rows, p_send, p_recv, r_send, r_recv):
    me = {name: lax.axis_index(name) for name in axis_names}

    def place(stage):
        axis, dims = stage
        own = 0
        root = me[axis]
        scale = 1
        for stride, size in dims:
            digit = lax.rem(me[axis] // stride, size)
            own = own + digit * scale
            root = root - digit * stride
            scale *= size

        def device(other):
            coord = root
            scale = 1
            for stride, size in dims:
                coord = coord + lax.rem(other // scale, size) * stride
                scale *= size
            return tuple(coord if name == axis else me[name] for name in axis_names)

        return own, device

    barrier = pltpu.get_barrier_semaphore()
    for stage in stages:
        own, device = place(stage)
        for step in range(1, group_size(stage)):
            other = lax.rem(own + step, group_size(stage))
            pl.semaphore_signal(barrier, 1, device_id=device(other), device_id_type=MESH)

    chroma = chroma_ref[...]
    weight = weight_ref[...]
    diag = diag_ref[...]
    pm = pm_ref[...]
    channels, count = d_ref.shape[:2]
    modes = beam_ref.shape[1]

    def beam_seen(vector):
        low = (chroma * vector).astype(jnp.bfloat16).reshape(channels * count, modes)
        seen = lax.dot_general(
            low, beam_ref[...], (((1,), (1,)), ((), ())), preferred_element_type=jnp.float32
        )
        return seen.reshape(channels, count, -1)

    def beam_forward(vector):
        return (weight * beam_seen(vector)).astype(jnp.bfloat16)

    def beam_backward(heard):
        back = jnp.dot(heard.reshape(channels * count, -1), beam_ref[...], preferred_element_type=jnp.float32)
        return chroma * back.reshape(channels, count, modes)


    def exchange_start(stage, src, recv, base, send_sems, recv_sems):
        own, device = place(stage)
        size = group_size(stage)

        def copy_to(other, slot):
            return pltpu.make_async_remote_copy(
                src_ref=src,
                dst_ref=recv.at[base + slot],
                send_sem=send_sems.at[base + other],
                recv_sem=recv_sems.at[base + slot],
                device_id=device(other),
                device_id_type=MESH,
            )

        for step in range(1, size):
            copy_to(lax.rem(own + step, size), own).start()
        recv[base + own] = src[...]
        return own, size, base, recv, copy_to

    sent = []

    def exchange_finish(state):
        own, size, base, recv, copy_to = state
        for step in range(1, size):
            other = lax.rem(own + step, size)
            copy_to(other, other).wait_recv()
        sent.append(state)
        total = recv[base].astype(jnp.float32)
        for slot in range(1, size):
            total = total + recv[base + slot].astype(jnp.float32)
        return total

    counter = {"row": 0, "slot": 0, "part": 0}

    def next_row(value):
        index = counter["row"]
        counter["row"] += 1
        rows[index] = value
        return rows.at[index]

    def row_stage(stage, src):
        base = counter["slot"]
        counter["slot"] += group_size(stage)
        return exchange_start(stage, src, recv_rows, base, r_send, r_recv)

    def reduce_rest(value):
        for stage in stages[1:]:
            value = exchange_finish(row_stage(stage, next_row(value)))
        return value

    def projection_start(vector):
        index = counter["part"]
        counter["part"] += 1
        for rank in range(pm.shape[1]):
            parts[index, rank] = jnp.sum(pm[:, rank] * vector, axis=0).astype(parts.dtype)
        nz = group_size(stages[0])
        return exchange_start(stages[0], parts.at[index], recv_p, index * nz, p_send, p_recv)

    d = beam_backward(d_ref[...])
    pl.semaphore_wait(barrier, sum(group_size(stage) - 1 for stage in stages))
    p_state = projection_start(d)
    seen = beam_seen(d)
    heard = (weight * seen).astype(jnp.bfloat16)
    quadratic = column_sum(seen * heard.astype(jnp.float32)) + column_sum(d * (diag * d))
    z_state = row_stage(stages[0], next_row(to_row([quadratic, column_sum(d * d)])))
    cb = beam_backward(heard)
    projection = exchange_finish(p_state)
    zrow = exchange_finish(z_state)
    total = reduce_rest(zrow + to_row([column_sum(projection * projection)]))
    curve = from_row(total, 0, count)
    norm_now = from_row(total, 1, count)
    step_size = (norm_now / curve)[None]
    estimate = step_size * d
    spread = pm[:, 0] * projection[0][None]
    for rank in range(1, pm.shape[1]):
        spread = spread + pm[:, rank] * projection[rank][None]
    residual = d - step_size * (cb + diag * d + spread)
    z_state = row_stage(stages[0], next_row(to_row([column_sum(residual * residual)])))
    p_state = projection_start(residual)
    cb_residual = beam_backward(beam_forward(residual))
    total = reduce_rest(exchange_finish(z_state))
    projection_residual = exchange_finish(p_state)
    norm_next = from_row(total, 0, count)
    ratio = (norm_next / norm_now)[None]
    direction = residual + ratio * d
    cb_direction = cb_residual + ratio * cb
    projection = projection_residual + ratio * projection
    zrow = exchange_finish(
        row_stage(stages[0], next_row(to_row([column_sum(direction * (cb_direction + diag * direction))])))
    )
    total = reduce_rest(zrow + to_row([column_sum(projection * projection)]))
    curve = from_row(total, 0, count)
    est_ref[...] = estimate
    next_ref[...] = direction
    step_ref[...] = to_row([norm_next / curve])
    for own, size, _, _, copy_to in sent:
        for step in range(1, size):
            copy_to(lax.rem(own + step, size), own).wait_send()


def cg_solve(axis_names, stages, d, beam, chroma, weight, diag, pm):
    reductions = 3
    slots = reductions * sum(group_size(stage) for stage in stages)
    rounds = reductions * len(stages)
    nz = group_size(stages[0])
    vector = jax.ShapeDtypeStruct(d.shape[:2] + beam.shape[1:], jnp.float32)
    row = jax.ShapeDtypeStruct((1, 128), jnp.float32)
    vmem = pl.BlockSpec(memory_space=pltpu.VMEM)
    part_shape = (pm.shape[1],) + vector.shape[1:]
    estimate, direction, step_row = pl.pallas_call(
        functools.partial(cg_kernel, axis_names, stages),
        out_shape=(vector, vector, row),
        in_specs=[vmem] * 6,
        out_specs=(vmem, vmem, vmem),
        scratch_shapes=[
            pltpu.VMEM((2,) + part_shape, jnp.bfloat16),
            pltpu.VMEM((rounds, 1, 128), jnp.float32),
            pltpu.VMEM((2 * nz,) + part_shape, jnp.bfloat16),
            pltpu.VMEM((slots, 1, 128), jnp.float32),
            pltpu.SemaphoreType.DMA((2 * nz,)),
            pltpu.SemaphoreType.DMA((2 * nz,)),
            pltpu.SemaphoreType.DMA((slots,)),
            pltpu.SemaphoreType.DMA((slots,)),
        ],
        compiler_params=pltpu.CompilerParams(collective_id=1, has_side_effects=True),
    )(d, beam, chroma, weight, diag, pm)
    step_size = step_row[0, : d.shape[1]]
    return estimate + step_size[None, :, None] * direction


def make_shards(mesh):
    axis_names = tuple(mesh.axis_names)
    mode_devices = mesh.shape["ma"]
    freq_devices = mesh.shape["freq"]
    if mode_devices % 16 == 0:
        mode_stages = [("ma", 1, 2), ("ma", 2, 8), ("ma", 16, mode_devices // 16)]
    else:
        mode_stages = [("ma", 1, mode_devices)]
    global_stages = mode_stages + [("freq", 1, freq_devices)]
    freq_stages = [("freq", 1, freq_devices)]

    def scalar_sum(*vectors):
        rows = jnp.stack(vectors)
        padded = jnp.pad(rows, ((0, 8 - rows.shape[0]), (0, 128 - rows.shape[1])))
        summed = group_sum(padded, axis_names, global_stages, jnp.float32, 2)
        return [summed[index, : rows.shape[1]] for index in range(len(vectors))]

    def freq_sum(partial_sum):
        shape = partial_sum.shape
        flat = partial_sum.reshape(-1, shape[-1])
        summed = group_sum(flat, axis_names, freq_stages, jnp.bfloat16, 1)
        return summed.reshape(shape)

    def shards(timestream, beam_transfer, chromatic_gain, noise_weight, prior_diagonal, prior_modes):
        spectral_channels = timestream.shape[0]
        device_time_samples = timestream.shape[1]
        noise_realizations = timestream.shape[2]
        antenna_pairs = timestream.shape[3]
        mode_devices_here = mode_devices
        columns = noise_realizations * antenna_pairs // mode_devices_here
        blocks = antenna_pairs // columns
        halves = columns // 128
        send = timestream.reshape(
            spectral_channels, device_time_samples, noise_realizations, blocks, halves, 128
        ).transpose(2, 3, 0, 1, 4, 5)
        send = send.reshape(mode_devices_here, spectral_channels * device_time_samples * halves, 128)
        received = lax.all_to_all(send, "ma", 0, 0, tiled=True)
        received = received.reshape(mode_devices_here, spectral_channels, device_time_samples, columns)
        all_times = mode_devices_here * device_time_samples
        hartley = hartley_table(all_times // 2, all_times)
        hartley_high = hartley.astype(jnp.bfloat16)
        hartley_low = (hartley - hartley_high.astype(jnp.float32)).astype(jnp.bfloat16)
        hartley_high = hartley_high.reshape(all_times // 2, mode_devices_here, device_time_samples)
        hartley_low = hartley_low.reshape(all_times // 2, mode_devices_here, device_time_samples)
        mode_high = jnp.einsum(
            "mit,iftc->mfc", hartley_high, received, preferred_element_type=jnp.float32
        )
        mode_low = jnp.einsum("mit,iftc->mfc", hartley_low, received, preferred_element_type=jnp.float32)
        mode_rows = (mode_high + mode_low).astype(jnp.bfloat16)
        back_rows = lax.all_to_all(mode_rows, "ma", 0, 0, tiled=True)
        resident_modes = back_rows.shape[0] // mode_devices_here
        back_rows = back_rows.reshape(
            noise_realizations, blocks, resident_modes, spectral_channels, columns
        )
        measured_visibility = back_rows.transpose(3, 2, 0, 1, 4).reshape(
            spectral_channels, resident_modes, noise_realizations, antenna_pairs
        )
        chroma = chromatic_gain[:, None, None, :]
        diagonal = prior_diagonal[:, None, None, :]
        weighted = (noise_weight[:, :, None, :] * measured_visibility.astype(jnp.float32)).astype(
            jnp.bfloat16
        )

        assert resident_modes == 1
        if mode_devices % 16 == 0:
            cg_stages = [
                ("freq", [(1, freq_devices)]),
                ("ma", [(1, 2), (16, mode_devices // 16)]),
                ("ma", [(2, 8)]),
            ]
        else:
            cg_stages = [("freq", [(1, freq_devices)]), ("ma", [(1, mode_devices)])]
        diag_rows = prior_diagonal[:, None, :]
        mode_rows4 = prior_modes[:, :, None, :]

        def beam_back(direction):
            low = (chroma * direction).astype(jnp.bfloat16)
            seen = jnp.einsum("fmks,mbs->fmkb", low, beam_transfer, preferred_element_type=jnp.float32)
            heard = (noise_weight[:, :, None, :] * seen).astype(jnp.bfloat16)
            back = jnp.einsum(
                "fmkb,mbs->fmks", heard, beam_transfer, preferred_element_type=jnp.float32
            )
            return (chroma * back)[:, 0]

        direction = weighted[:, 0]
        operands = (beam_transfer[0], chromatic_gain[:, None, :], noise_weight, diag_rows, mode_rows4)
        estimate = cg_solve(axis_names, cg_stages, direction, *operands)
        estimate = estimate[:, None]
        return estimate

    return shards


def solution(mesh):
    in_specs = (
        P("freq", "ma", None, None),
        P("ma", None, None),
        P("freq", None),
        P("freq", "ma", None),
        P("freq", None),
        P("freq", None, None),
    )
    out_specs = P("freq", "ma", None, None)
    return jax.shard_map(make_shards(mesh), mesh=mesh, in_specs=in_specs, out_specs=out_specs, check_vma=False)
```

```python
import functools

import jax
import jax.numpy as jnp
from jax import lax
from jax.experimental import pallas as pl
from jax.experimental.pallas import tpu as pltpu
from jax.sharding import PartitionSpec as P

ITERS = 2
MESH = pl.DeviceIdType.MESH


def hartley_table(rows, cols):
    index_m = jnp.arange(rows, dtype=jnp.int32)[:, None]
    index_t = jnp.arange(cols, dtype=jnp.int32)[None, :]
    phase = (index_m * index_t % cols).astype(jnp.float32)
    angle = 2.0 * jnp.pi * phase / cols
    return (jnp.cos(angle) + jnp.sin(angle)) / jnp.sqrt(jnp.float32(cols))


def inner(left, right):
    return jnp.sum(left * right, axis=(0, 1, 3))


def reduce_kernel(axis_names, stages, x_ref, o_ref, cur, recv, send_sem, recv_sem):
    me = {name: lax.axis_index(name) for name in axis_names}

    def device(axis, coord):
        return tuple(coord if name == axis else me[name] for name in axis_names)

    plan = []
    base = 0
    for axis, stride, size in stages:
        own = (me[axis] // stride) % size
        root = me[axis] - own * stride
        peers = []
        for step in range(1, size):
            other = lax.rem(own + step, size)
            peers.append((other, device(axis, root + other * stride)))
        plan.append((base, own, size, peers))
        base += size

    barrier = pltpu.get_barrier_semaphore()
    for _, _, _, peers in plan:
        for _, peer in peers:
            pl.semaphore_signal(barrier, 1, device_id=peer, device_id_type=MESH)
    pl.semaphore_wait(barrier, sum(len(peers) for _, _, _, peers in plan))

    acc = x_ref[...].astype(jnp.float32)
    for index, (base, own, size, peers) in enumerate(plan):
        cur[index] = acc.astype(cur.dtype)
        copies = []
        for other, peer in peers:
            copy = pltpu.make_async_remote_copy(
                src_ref=cur.at[index],
                dst_ref=recv.at[base + own],
                send_sem=send_sem.at[base + other],
                recv_sem=recv_sem.at[base + own],
                device_id=peer,
                device_id_type=MESH,
            )
            copy.start()
            copies.append(copy)
        recv[base + own] = acc.astype(recv.dtype)
        for other, peer in peers:
            pltpu.make_async_remote_copy(
                src_ref=cur.at[index],
                dst_ref=recv.at[base + other],
                send_sem=send_sem.at[base + other],
                recv_sem=recv_sem.at[base + other],
                device_id=peer,
                device_id_type=MESH,
            ).wait_recv()
        for copy in copies:
            copy.wait_send()
        total = recv[base].astype(jnp.float32)
        for slot in range(1, size):
            total = total + recv[base + slot].astype(jnp.float32)
        acc = total
    o_ref[...] = acc.astype(o_ref.dtype)


def group_sum(x, axis_names, stages, wire_dtype, collective_id):
    slots = sum(size for _, _, size in stages)
    return pl.pallas_call(
        functools.partial(reduce_kernel, axis_names, stages),
        out_shape=jax.ShapeDtypeStruct(x.shape, jnp.float32),
        in_specs=[pl.BlockSpec(memory_space=pltpu.VMEM)],
        out_specs=pl.BlockSpec(memory_space=pltpu.VMEM),
        scratch_shapes=[
            pltpu.VMEM((len(stages),) + x.shape, wire_dtype),
            pltpu.VMEM((slots,) + x.shape, wire_dtype),
            pltpu.SemaphoreType.DMA((slots,)),
            pltpu.SemaphoreType.DMA((slots,)),
        ],
        compiler_params=pltpu.CompilerParams(collective_id=collective_id, has_side_effects=True),
    )(x)


def column_sum(x):
    return jnp.sum(jnp.sum(x, axis=0), axis=1, keepdims=True)


def to_row(columns):
    count = columns[0].shape[0]
    sub = lax.broadcasted_iota(jnp.int32, (count, 128), 0)
    lane = lax.broadcasted_iota(jnp.int32, (count, 128), 1)
    acc = jnp.zeros((count, 128), jnp.float32)
    for index, column in enumerate(columns):
        acc = acc + jnp.where(lane == sub + count * index, jnp.broadcast_to(column, (count, 128)), 0.0)
    return jnp.sum(acc, axis=0, keepdims=True)


def from_row(row, index, count):
    sub = lax.broadcasted_iota(jnp.int32, (count, 128), 0)
    lane = lax.broadcasted_iota(jnp.int32, (count, 128), 1)
    picked = jnp.where(lane == sub + count * index, jnp.broadcast_to(row, (count, 128)), 0.0)
    return jnp.sum(picked, axis=1, keepdims=True)


def group_size(stage):
    size = 1
    for _, extent in stage[1]:
        size *= extent
    return size


def cg_kernel(axis_names, stages, d_ref, beam_ref, chroma_ref, weight_ref, diag_ref, pm_ref,
              est_ref, parts, rows, recv_p, recv_rows, p_send, p_recv, r_send, r_recv):
    me = {name: lax.axis_index(name) for name in axis_names}

    def place(stage):
        axis, dims = stage
        own = 0
        root = me[axis]
        scale = 1
        for stride, size in dims:
            digit = lax.rem(me[axis] // stride, size)
            own = own + digit * scale
            root = root - digit * stride
            scale *= size

        def device(other):
            coord = root
            scale = 1
            for stride, size in dims:
                coord = coord + lax.rem(other // scale, size) * stride
                scale *= size
            return tuple(coord if name == axis else me[name] for name in axis_names)

        return own, device

    barrier = pltpu.get_barrier_semaphore()
    for stage in stages:
        own, device = place(stage)
        for step in range(1, group_size(stage)):
            other = lax.rem(own + step, group_size(stage))
            pl.semaphore_signal(barrier, 1, device_id=device(other), device_id_type=MESH)

    chroma = chroma_ref[...]
    weight = weight_ref[...]
    diag = diag_ref[...]
    pm = pm_ref[...]
    channels, count = d_ref.shape[:2]
    modes = beam_ref.shape[1]

    def beam_forward(vector):
        low = (chroma * vector).astype(jnp.bfloat16).reshape(channels * count, modes)
        seen = lax.dot_general(
            low, beam_ref[...], (((1,), (1,)), ((), ())), preferred_element_type=jnp.float32
        )
        return (weight * seen.reshape(channels, count, -1)).astype(jnp.bfloat16)

    def beam_backward(heard):
        back = jnp.dot(heard.reshape(channels * count, -1), beam_ref[...], preferred_element_type=jnp.float32)
        return chroma * back.reshape(channels, count, modes)


    def exchange_start(stage, src, recv, base, send_sems, recv_sems):
        own, device = place(stage)
        size = group_size(stage)

        def copy_to(other, slot):
            return pltpu.make_async_remote_copy(
                src_ref=src,
                dst_ref=recv.at[base + slot],
                send_sem=send_sems.at[base + other],
                recv_sem=recv_sems.at[base + slot],
                device_id=device(other),
                device_id_type=MESH,
            )

        for step in range(1, size):
            copy_to(lax.rem(own + step, size), own).start()
        recv[base + own] = src[...]
        return own, size, base, recv, copy_to

    sent = []

    def exchange_finish(state):
        own, size, base, recv, copy_to = state
        for step in range(1, size):
            other = lax.rem(own + step, size)
            copy_to(other, other).wait_recv()
        sent.append(state)
        total = recv[base].astype(jnp.float32)
        for slot in range(1, size):
            total = total + recv[base + slot].astype(jnp.float32)
        return total

    counter = {"row": 0, "slot": 0, "part": 0}

    def next_row(value):
        index = counter["row"]
        counter["row"] += 1
        rows[index] = value
        return rows.at[index]

    def row_stage(stage, src):
        base = counter["slot"]
        counter["slot"] += group_size(stage)
        return exchange_start(stage, src, recv_rows, base, r_send, r_recv)

    def reduce_rest(value):
        for stage in stages[1:]:
            value = exchange_finish(row_stage(stage, next_row(value)))
        return value

    def projection_start(vector):
        index = counter["part"]
        counter["part"] += 1
        for rank in range(pm.shape[1]):
            parts[index, rank] = jnp.sum(pm[:, rank] * vector, axis=0).astype(parts.dtype)
        nz = group_size(stages[0])
        return exchange_start(stages[0], parts.at[index], recv_p, index * nz, p_send, p_recv)

    d = beam_backward(d_ref[...])
    pl.semaphore_wait(barrier, sum(group_size(stage) - 1 for stage in stages))
    p_state = projection_start(d)
    cb = beam_backward(beam_forward(d))
    z_state = row_stage(stages[0], next_row(to_row([column_sum(d * (cb + diag * d)), column_sum(d * d)])))
    projection = exchange_finish(p_state)
    zrow = exchange_finish(z_state)
    total = reduce_rest(zrow + to_row([column_sum(projection * projection)]))
    curve = from_row(total, 0, count)
    norm_now = from_row(total, 1, count)
    step_size = (norm_now / curve)[None]
    estimate = step_size * d
    spread = pm[:, 0] * projection[0][None]
    for rank in range(1, pm.shape[1]):
        spread = spread + pm[:, rank] * projection[rank][None]
    residual = d - step_size * (cb + diag * d + spread)
    z_state = row_stage(stages[0], next_row(to_row([column_sum(residual * residual)])))
    p_state = projection_start(residual)
    cb_residual = beam_backward(beam_forward(residual))
    total = reduce_rest(exchange_finish(z_state))
    projection_residual = exchange_finish(p_state)
    norm_next = from_row(total, 0, count)
    ratio = (norm_next / norm_now)[None]
    direction = residual + ratio * d
    cb_direction = cb_residual + ratio * cb
    projection = projection_residual + ratio * projection
    zrow = exchange_finish(
        row_stage(stages[0], next_row(to_row([column_sum(direction * (cb_direction + diag * direction))])))
    )
    total = reduce_rest(zrow + to_row([column_sum(projection * projection)]))
    curve = from_row(total, 0, count)
    est_ref[...] = estimate + (norm_next / curve)[None] * direction
    for own, size, _, _, copy_to in sent:
        for step in range(1, size):
            copy_to(lax.rem(own + step, size), own).wait_send()


def cg_solve(axis_names, stages, d, beam, chroma, weight, diag, pm):
    reductions = 3
    slots = reductions * sum(group_size(stage) for stage in stages)
    rounds = reductions * len(stages)
    nz = group_size(stages[0])
    vector = jax.ShapeDtypeStruct(d.shape[:2] + beam.shape[1:], jnp.float32)
    row = jax.ShapeDtypeStruct((1, 128), jnp.float32)
    vmem = pl.BlockSpec(memory_space=pltpu.VMEM)
    part_shape = (pm.shape[1],) + vector.shape[1:]
    return pl.pallas_call(
        functools.partial(cg_kernel, axis_names, stages),
        out_shape=vector,
        in_specs=[vmem] * 6,
        out_specs=vmem,
        scratch_shapes=[
            pltpu.VMEM((2,) + part_shape, jnp.bfloat16),
            pltpu.VMEM((rounds, 1, 128), jnp.float32),
            pltpu.VMEM((2 * nz,) + part_shape, jnp.bfloat16),
            pltpu.VMEM((slots, 1, 128), jnp.float32),
            pltpu.SemaphoreType.DMA((2 * nz,)),
            pltpu.SemaphoreType.DMA((2 * nz,)),
            pltpu.SemaphoreType.DMA((slots,)),
            pltpu.SemaphoreType.DMA((slots,)),
        ],
        compiler_params=pltpu.CompilerParams(collective_id=1, has_side_effects=True),
    )(d, beam, chroma, weight, diag, pm)


def make_shards(mesh):
    axis_names = tuple(mesh.axis_names)
    mode_devices = mesh.shape["ma"]
    freq_devices = mesh.shape["freq"]
    if mode_devices % 16 == 0:
        mode_stages = [("ma", 1, 2), ("ma", 2, 8), ("ma", 16, mode_devices // 16)]
    else:
        mode_stages = [("ma", 1, mode_devices)]
    global_stages = mode_stages + [("freq", 1, freq_devices)]
    freq_stages = [("freq", 1, freq_devices)]

    def scalar_sum(*vectors):
        rows = jnp.stack(vectors)
        padded = jnp.pad(rows, ((0, 8 - rows.shape[0]), (0, 128 - rows.shape[1])))
        summed = group_sum(padded, axis_names, global_stages, jnp.float32, 2)
        return [summed[index, : rows.shape[1]] for index in range(len(vectors))]

    def freq_sum(partial_sum):
        shape = partial_sum.shape
        flat = partial_sum.reshape(-1, shape[-1])
        summed = group_sum(flat, axis_names, freq_stages, jnp.bfloat16, 1)
        return summed.reshape(shape)

    def shards(timestream, beam_transfer, chromatic_gain, noise_weight, prior_diagonal, prior_modes):
        spectral_channels = timestream.shape[0]
        device_time_samples = timestream.shape[1]
        noise_realizations = timestream.shape[2]
        antenna_pairs = timestream.shape[3]
        mode_devices_here = mode_devices
        columns = noise_realizations * antenna_pairs // mode_devices_here
        blocks = antenna_pairs // columns
        halves = columns // 128
        send = timestream.reshape(
            spectral_channels, device_time_samples, noise_realizations, blocks, halves, 128
        ).transpose(2, 3, 0, 1, 4, 5)
        send = send.reshape(mode_devices_here, spectral_channels * device_time_samples * halves, 128)
        received = lax.all_to_all(send, "ma", 0, 0, tiled=True)
        received = received.reshape(mode_devices_here, spectral_channels, device_time_samples, columns)
        all_times = mode_devices_here * device_time_samples
        hartley = hartley_table(all_times // 2, all_times)
        hartley_high = hartley.astype(jnp.bfloat16)
        hartley_low = (hartley - hartley_high.astype(jnp.float32)).astype(jnp.bfloat16)
        hartley_high = hartley_high.reshape(all_times // 2, mode_devices_here, device_time_samples)
        hartley_low = hartley_low.reshape(all_times // 2, mode_devices_here, device_time_samples)
        mode_high = jnp.einsum(
            "mit,iftc->mfc", hartley_high, received, preferred_element_type=jnp.float32
        )
        mode_low = jnp.einsum("mit,iftc->mfc", hartley_low, received, preferred_element_type=jnp.float32)
        mode_rows = (mode_high + mode_low).astype(jnp.bfloat16)
        back_rows = lax.all_to_all(mode_rows, "ma", 0, 0, tiled=True)
        resident_modes = back_rows.shape[0] // mode_devices_here
        back_rows = back_rows.reshape(
            noise_realizations, blocks, resident_modes, spectral_channels, columns
        )
        measured_visibility = back_rows.transpose(3, 2, 0, 1, 4).reshape(
            spectral_channels, resident_modes, noise_realizations, antenna_pairs
        )
        chroma = chromatic_gain[:, None, None, :]
        diagonal = prior_diagonal[:, None, None, :]
        weighted = (noise_weight[:, :, None, :] * measured_visibility.astype(jnp.float32)).astype(
            jnp.bfloat16
        )

        assert resident_modes == 1
        if mode_devices % 16 == 0:
            cg_stages = [
                ("freq", [(1, freq_devices)]),
                ("ma", [(1, 2), (16, mode_devices // 16)]),
                ("ma", [(2, 8)]),
            ]
        else:
            cg_stages = [("freq", [(1, freq_devices)]), ("ma", [(1, mode_devices)])]
        diag_rows = prior_diagonal[:, None, :]
        mode_rows4 = prior_modes[:, :, None, :]

        def beam_back(direction):
            low = (chroma * direction).astype(jnp.bfloat16)
            seen = jnp.einsum("fmks,mbs->fmkb", low, beam_transfer, preferred_element_type=jnp.float32)
            heard = (noise_weight[:, :, None, :] * seen).astype(jnp.bfloat16)
            back = jnp.einsum(
                "fmkb,mbs->fmks", heard, beam_transfer, preferred_element_type=jnp.float32
            )
            return (chroma * back)[:, 0]

        direction = weighted[:, 0]
        operands = (beam_transfer[0], chromatic_gain[:, None, :], noise_weight, diag_rows, mode_rows4)
        estimate = cg_solve(axis_names, cg_stages, direction, *operands)
        estimate = estimate[:, None]
        return estimate

    return shards


def solution(mesh):
    in_specs = (
        P("freq", "ma", None, None),
        P("ma", None, None),
        P("freq", None),
        P("freq", "ma", None),
        P("freq", None),
        P("freq", None, None),
    )
    out_specs = P("freq", "ma", None, None)
    return jax.shard_map(make_shards(mesh), mesh=mesh, in_specs=in_specs, out_specs=out_specs, check_vma=False)
```

```python
import functools

import jax
import jax.numpy as jnp
from jax import lax
from jax.experimental import pallas as pl
from jax.experimental.pallas import tpu as pltpu
from jax.sharding import PartitionSpec as P

ITERS = 2
MESH = pl.DeviceIdType.MESH


def hartley_table(rows, cols):
    index_m = jnp.arange(rows, dtype=jnp.int32)[:, None]
    index_t = jnp.arange(cols, dtype=jnp.int32)[None, :]
    phase = (index_m * index_t % cols).astype(jnp.float32)
    angle = 2.0 * jnp.pi * phase / cols
    return (jnp.cos(angle) + jnp.sin(angle)) / jnp.sqrt(jnp.float32(cols))


def inner(left, right):
    return jnp.sum(left * right, axis=(0, 1, 3))


def reduce_kernel(axis_names, stages, x_ref, o_ref, cur, recv, send_sem, recv_sem):
    me = {name: lax.axis_index(name) for name in axis_names}

    def device(axis, coord):
        return tuple(coord if name == axis else me[name] for name in axis_names)

    plan = []
    base = 0
    for axis, stride, size in stages:
        own = (me[axis] // stride) % size
        root = me[axis] - own * stride
        peers = []
        for step in range(1, size):
            other = lax.rem(own + step, size)
            peers.append((other, device(axis, root + other * stride)))
        plan.append((base, own, size, peers))
        base += size

    barrier = pltpu.get_barrier_semaphore()
    for _, _, _, peers in plan:
        for _, peer in peers:
            pl.semaphore_signal(barrier, 1, device_id=peer, device_id_type=MESH)
    pl.semaphore_wait(barrier, sum(len(peers) for _, _, _, peers in plan))

    acc = x_ref[...].astype(jnp.float32)
    for index, (base, own, size, peers) in enumerate(plan):
        cur[index] = acc.astype(cur.dtype)
        copies = []
        for other, peer in peers:
            copy = pltpu.make_async_remote_copy(
                src_ref=cur.at[index],
                dst_ref=recv.at[base + own],
                send_sem=send_sem.at[base + other],
                recv_sem=recv_sem.at[base + own],
                device_id=peer,
                device_id_type=MESH,
            )
            copy.start()
            copies.append(copy)
        recv[base + own] = acc.astype(recv.dtype)
        for other, peer in peers:
            pltpu.make_async_remote_copy(
                src_ref=cur.at[index],
                dst_ref=recv.at[base + other],
                send_sem=send_sem.at[base + other],
                recv_sem=recv_sem.at[base + other],
                device_id=peer,
                device_id_type=MESH,
            ).wait_recv()
        for copy in copies:
            copy.wait_send()
        total = recv[base].astype(jnp.float32)
        for slot in range(1, size):
            total = total + recv[base + slot].astype(jnp.float32)
        acc = total
    o_ref[...] = acc.astype(o_ref.dtype)


def group_sum(x, axis_names, stages, wire_dtype, collective_id):
    slots = sum(size for _, _, size in stages)
    return pl.pallas_call(
        functools.partial(reduce_kernel, axis_names, stages),
        out_shape=jax.ShapeDtypeStruct(x.shape, jnp.float32),
        in_specs=[pl.BlockSpec(memory_space=pltpu.VMEM)],
        out_specs=pl.BlockSpec(memory_space=pltpu.VMEM),
        scratch_shapes=[
            pltpu.VMEM((len(stages),) + x.shape, wire_dtype),
            pltpu.VMEM((slots,) + x.shape, wire_dtype),
            pltpu.SemaphoreType.DMA((slots,)),
            pltpu.SemaphoreType.DMA((slots,)),
        ],
        compiler_params=pltpu.CompilerParams(collective_id=collective_id, has_side_effects=True),
    )(x)


def column_sum(x):
    return jnp.sum(jnp.sum(x, axis=0), axis=1, keepdims=True)


def to_row(columns):
    count = columns[0].shape[0]
    sub = lax.broadcasted_iota(jnp.int32, (count, 128), 0)
    lane = lax.broadcasted_iota(jnp.int32, (count, 128), 1)
    acc = jnp.zeros((count, 128), jnp.float32)
    for index, column in enumerate(columns):
        acc = acc + jnp.where(lane == sub + count * index, jnp.broadcast_to(column, (count, 128)), 0.0)
    return jnp.sum(acc, axis=0, keepdims=True)


def from_row(row, index, count):
    sub = lax.broadcasted_iota(jnp.int32, (count, 128), 0)
    lane = lax.broadcasted_iota(jnp.int32, (count, 128), 1)
    picked = jnp.where(lane == sub + count * index, jnp.broadcast_to(row, (count, 128)), 0.0)
    return jnp.sum(picked, axis=1, keepdims=True)


def group_size(stage):
    size = 1
    for _, extent in stage[1]:
        size *= extent
    return size


def cg_kernel(axis_names, stages, d_ref, beam_hbm, chroma_ref, weight_ref, diag_ref, pm_ref,
              est_ref, beam_ref, beam_sems, parts, rows, recv_p, recv_rows, p_send, p_recv, r_send, r_recv):
    me = {name: lax.axis_index(name) for name in axis_names}

    def place(stage):
        axis, dims = stage
        own = 0
        root = me[axis]
        scale = 1
        for stride, size in dims:
            digit = lax.rem(me[axis] // stride, size)
            own = own + digit * scale
            root = root - digit * stride
            scale *= size

        def device(other):
            coord = root
            scale = 1
            for stride, size in dims:
                coord = coord + lax.rem(other // scale, size) * stride
                scale *= size
            return tuple(coord if name == axis else me[name] for name in axis_names)

        return own, device

    barrier = pltpu.get_barrier_semaphore()
    for stage in stages:
        own, device = place(stage)
        for step in range(1, group_size(stage)):
            other = lax.rem(own + step, group_size(stage))
            pl.semaphore_signal(barrier, 1, device_id=device(other), device_id_type=MESH)

    chunks = beam_sems.shape[0]
    rows_per = beam_ref.shape[0] // chunks
    beam_copies = []
    for chunk in range(chunks):
        window = pl.ds(chunk * rows_per, rows_per)
        beam_copy = pltpu.make_async_copy(beam_hbm.at[window], beam_ref.at[window], beam_sems.at[chunk])
        beam_copy.start()
        beam_copies.append(beam_copy)

    chroma = chroma_ref[...]
    weight = weight_ref[...]
    diag = diag_ref[...]
    pm = pm_ref[...]
    channels, count = d_ref.shape[:2]
    modes = beam_ref.shape[1]

    def beam_forward(vector):
        low = (chroma * vector).astype(jnp.bfloat16).reshape(channels * count, modes)
        seen = lax.dot_general(
            low, beam_ref[...], (((1,), (1,)), ((), ())), preferred_element_type=jnp.float32
        )
        return (weight * seen.reshape(channels, count, -1)).astype(jnp.bfloat16)

    def beam_backward(heard):
        back = jnp.dot(heard.reshape(channels * count, -1), beam_ref[...], preferred_element_type=jnp.float32)
        return chroma * back.reshape(channels, count, modes)


    def exchange_start(stage, src, recv, base, send_sems, recv_sems):
        own, device = place(stage)
        size = group_size(stage)

        def copy_to(other, slot):
            return pltpu.make_async_remote_copy(
                src_ref=src,
                dst_ref=recv.at[base + slot],
                send_sem=send_sems.at[base + other],
                recv_sem=recv_sems.at[base + slot],
                device_id=device(other),
                device_id_type=MESH,
            )

        for step in range(1, size):
            copy_to(lax.rem(own + step, size), own).start()
        recv[base + own] = src[...]
        return own, size, base, recv, copy_to

    sent = []

    def exchange_finish(state):
        own, size, base, recv, copy_to = state
        for step in range(1, size):
            other = lax.rem(own + step, size)
            copy_to(other, other).wait_recv()
        sent.append(state)
        total = recv[base].astype(jnp.float32)
        for slot in range(1, size):
            total = total + recv[base + slot].astype(jnp.float32)
        return total

    counter = {"row": 0, "slot": 0, "part": 0}

    def next_row(value):
        index = counter["row"]
        counter["row"] += 1
        rows[index] = value
        return rows.at[index]

    def row_stage(stage, src):
        base = counter["slot"]
        counter["slot"] += group_size(stage)
        return exchange_start(stage, src, recv_rows, base, r_send, r_recv)

    def reduce_rest(value):
        for stage in stages[1:]:
            value = exchange_finish(row_stage(stage, next_row(value)))
        return value

    def projection_start(vector):
        index = counter["part"]
        counter["part"] += 1
        for rank in range(pm.shape[1]):
            parts[index, rank] = jnp.sum(pm[:, rank] * vector, axis=0).astype(parts.dtype)
        nz = group_size(stages[0])
        return exchange_start(stages[0], parts.at[index], recv_p, index * nz, p_send, p_recv)

    weighted = d_ref[...].reshape(channels * count, -1)
    back = None
    for chunk, beam_copy in enumerate(beam_copies):
        beam_copy.wait()
        window = slice(chunk * rows_per, (chunk + 1) * rows_per)
        term = jnp.dot(
            weighted[:, window], beam_ref[window, :], preferred_element_type=jnp.float32
        )
        back = term if back is None else back + term
    d = chroma * back.reshape(channels, count, modes)
    pl.semaphore_wait(barrier, sum(group_size(stage) - 1 for stage in stages))
    p_state = projection_start(d)
    cb = beam_backward(beam_forward(d))
    z_state = row_stage(stages[0], next_row(to_row([column_sum(d * (cb + diag * d)), column_sum(d * d)])))
    projection = exchange_finish(p_state)
    zrow = exchange_finish(z_state)
    total = reduce_rest(zrow + to_row([column_sum(projection * projection)]))
    curve = from_row(total, 0, count)
    norm_now = from_row(total, 1, count)
    step_size = (norm_now / curve)[None]
    estimate = step_size * d
    spread = pm[:, 0] * projection[0][None]
    for rank in range(1, pm.shape[1]):
        spread = spread + pm[:, rank] * projection[rank][None]
    residual = d - step_size * (cb + diag * d + spread)
    z_state = row_stage(stages[0], next_row(to_row([column_sum(residual * residual)])))
    p_state = projection_start(residual)
    cb_residual = beam_backward(beam_forward(residual))
    total = reduce_rest(exchange_finish(z_state))
    projection_residual = exchange_finish(p_state)
    norm_next = from_row(total, 0, count)
    ratio = (norm_next / norm_now)[None]
    direction = residual + ratio * d
    cb_direction = cb_residual + ratio * cb
    projection = projection_residual + ratio * projection
    zrow = exchange_finish(
        row_stage(stages[0], next_row(to_row([column_sum(direction * (cb_direction + diag * direction))])))
    )
    total = reduce_rest(zrow + to_row([column_sum(projection * projection)]))
    curve = from_row(total, 0, count)
    est_ref[...] = estimate + (norm_next / curve)[None] * direction
    for own, size, _, _, copy_to in sent:
        for step in range(1, size):
            copy_to(lax.rem(own + step, size), own).wait_send()


def cg_solve(axis_names, stages, d, beam, chroma, weight, diag, pm):
    reductions = 3
    slots = reductions * sum(group_size(stage) for stage in stages)
    rounds = reductions * len(stages)
    nz = group_size(stages[0])
    vector = jax.ShapeDtypeStruct(d.shape[:2] + beam.shape[1:], jnp.float32)
    row = jax.ShapeDtypeStruct((1, 128), jnp.float32)
    vmem = pl.BlockSpec(memory_space=pltpu.VMEM)
    part_shape = (pm.shape[1],) + vector.shape[1:]
    return pl.pallas_call(
        functools.partial(cg_kernel, axis_names, stages),
        out_shape=vector,
        in_specs=[vmem, pl.BlockSpec(memory_space=pl.ANY)] + [vmem] * 4,
        out_specs=vmem,
        scratch_shapes=[
            pltpu.VMEM(beam.shape, beam.dtype),
            pltpu.SemaphoreType.DMA((4,)),
            pltpu.VMEM((2,) + part_shape, jnp.bfloat16),
            pltpu.VMEM((rounds, 1, 128), jnp.float32),
            pltpu.VMEM((2 * nz,) + part_shape, jnp.bfloat16),
            pltpu.VMEM((slots, 1, 128), jnp.float32),
            pltpu.SemaphoreType.DMA((2 * nz,)),
            pltpu.SemaphoreType.DMA((2 * nz,)),
            pltpu.SemaphoreType.DMA((slots,)),
            pltpu.SemaphoreType.DMA((slots,)),
        ],
        compiler_params=pltpu.CompilerParams(collective_id=1, has_side_effects=True),
    )(d, beam, chroma, weight, diag, pm)


def make_shards(mesh):
    axis_names = tuple(mesh.axis_names)
    mode_devices = mesh.shape["ma"]
    freq_devices = mesh.shape["freq"]
    if mode_devices % 16 == 0:
        mode_stages = [("ma", 1, 2), ("ma", 2, 8), ("ma", 16, mode_devices // 16)]
    else:
        mode_stages = [("ma", 1, mode_devices)]
    global_stages = mode_stages + [("freq", 1, freq_devices)]
    freq_stages = [("freq", 1, freq_devices)]

    def scalar_sum(*vectors):
        rows = jnp.stack(vectors)
        padded = jnp.pad(rows, ((0, 8 - rows.shape[0]), (0, 128 - rows.shape[1])))
        summed = group_sum(padded, axis_names, global_stages, jnp.float32, 2)
        return [summed[index, : rows.shape[1]] for index in range(len(vectors))]

    def freq_sum(partial_sum):
        shape = partial_sum.shape
        flat = partial_sum.reshape(-1, shape[-1])
        summed = group_sum(flat, axis_names, freq_stages, jnp.bfloat16, 1)
        return summed.reshape(shape)

    def shards(timestream, beam_transfer, chromatic_gain, noise_weight, prior_diagonal, prior_modes):
        spectral_channels = timestream.shape[0]
        device_time_samples = timestream.shape[1]
        noise_realizations = timestream.shape[2]
        antenna_pairs = timestream.shape[3]
        mode_devices_here = mode_devices
        columns = noise_realizations * antenna_pairs // mode_devices_here
        blocks = antenna_pairs // columns
        halves = columns // 128
        send = timestream.reshape(
            spectral_channels, device_time_samples, noise_realizations, blocks, halves, 128
        ).transpose(2, 3, 0, 1, 4, 5)
        send = send.reshape(mode_devices_here, spectral_channels * device_time_samples * halves, 128)
        received = lax.all_to_all(send, "ma", 0, 0, tiled=True)
        received = received.reshape(mode_devices_here, spectral_channels, device_time_samples, columns)
        all_times = mode_devices_here * device_time_samples
        hartley = hartley_table(all_times // 2, all_times)
        hartley_high = hartley.astype(jnp.bfloat16)
        hartley_low = (hartley - hartley_high.astype(jnp.float32)).astype(jnp.bfloat16)
        hartley_high = hartley_high.reshape(all_times // 2, mode_devices_here, device_time_samples)
        hartley_low = hartley_low.reshape(all_times // 2, mode_devices_here, device_time_samples)
        mode_high = jnp.einsum(
            "mit,iftc->mfc", hartley_high, received, preferred_element_type=jnp.float32
        )
        mode_low = jnp.einsum("mit,iftc->mfc", hartley_low, received, preferred_element_type=jnp.float32)
        mode_rows = (mode_high + mode_low).astype(jnp.bfloat16)
        back_rows = lax.all_to_all(mode_rows, "ma", 0, 0, tiled=True)
        resident_modes = back_rows.shape[0] // mode_devices_here
        back_rows = back_rows.reshape(
            noise_realizations, blocks, resident_modes, spectral_channels, columns
        )
        measured_visibility = back_rows.transpose(3, 2, 0, 1, 4).reshape(
            spectral_channels, resident_modes, noise_realizations, antenna_pairs
        )
        chroma = chromatic_gain[:, None, None, :]
        diagonal = prior_diagonal[:, None, None, :]
        weighted = (noise_weight[:, :, None, :] * measured_visibility.astype(jnp.float32)).astype(
            jnp.bfloat16
        )

        assert resident_modes == 1
        if mode_devices % 16 == 0:
            cg_stages = [
                ("freq", [(1, freq_devices)]),
                ("ma", [(1, 2), (16, mode_devices // 16)]),
                ("ma", [(2, 8)]),
            ]
        else:
            cg_stages = [("freq", [(1, freq_devices)]), ("ma", [(1, mode_devices)])]
        diag_rows = prior_diagonal[:, None, :]
        mode_rows4 = prior_modes[:, :, None, :]

        def beam_back(direction):
            low = (chroma * direction).astype(jnp.bfloat16)
            seen = jnp.einsum("fmks,mbs->fmkb", low, beam_transfer, preferred_element_type=jnp.float32)
            heard = (noise_weight[:, :, None, :] * seen).astype(jnp.bfloat16)
            back = jnp.einsum(
                "fmkb,mbs->fmks", heard, beam_transfer, preferred_element_type=jnp.float32
            )
            return (chroma * back)[:, 0]

        direction = weighted[:, 0]
        operands = (beam_transfer[0], chromatic_gain[:, None, :], noise_weight, diag_rows, mode_rows4)
        estimate = cg_solve(axis_names, cg_stages, direction, *operands)
        estimate = estimate[:, None]
        return estimate

    return shards


def solution(mesh):
    in_specs = (
        P("freq", "ma", None, None),
        P("ma", None, None),
        P("freq", None),
        P("freq", "ma", None),
        P("freq", None),
        P("freq", None, None),
    )
    out_specs = P("freq", "ma", None, None)
    return jax.shard_map(make_shards(mesh), mesh=mesh, in_specs=in_specs, out_specs=out_specs, check_vma=False)
```

```python
import functools

import jax
import jax.numpy as jnp
from jax import lax
from jax.experimental import pallas as pl
from jax.experimental.pallas import tpu as pltpu
from jax.sharding import PartitionSpec as P

ITERS = 2
MESH = pl.DeviceIdType.MESH


def hartley_table(rows, cols):
    index_m = jnp.arange(rows, dtype=jnp.int32)[:, None]
    index_t = jnp.arange(cols, dtype=jnp.int32)[None, :]
    phase = (index_m * index_t % cols).astype(jnp.float32)
    angle = 2.0 * jnp.pi * phase / cols
    return (jnp.cos(angle) + jnp.sin(angle)) / jnp.sqrt(jnp.float32(cols))


def inner(left, right):
    return jnp.sum(left * right, axis=(0, 1, 3))


def reduce_kernel(axis_names, stages, x_ref, o_ref, cur, recv, send_sem, recv_sem):
    me = {name: lax.axis_index(name) for name in axis_names}

    def device(axis, coord):
        return tuple(coord if name == axis else me[name] for name in axis_names)

    plan = []
    base = 0
    for axis, stride, size in stages:
        own = (me[axis] // stride) % size
        root = me[axis] - own * stride
        peers = []
        for step in range(1, size):
            other = lax.rem(own + step, size)
            peers.append((other, device(axis, root + other * stride)))
        plan.append((base, own, size, peers))
        base += size

    barrier = pltpu.get_barrier_semaphore()
    for _, _, _, peers in plan:
        for _, peer in peers:
            pl.semaphore_signal(barrier, 1, device_id=peer, device_id_type=MESH)
    pl.semaphore_wait(barrier, sum(len(peers) for _, _, _, peers in plan))

    acc = x_ref[...].astype(jnp.float32)
    for index, (base, own, size, peers) in enumerate(plan):
        cur[index] = acc.astype(cur.dtype)
        copies = []
        for other, peer in peers:
            copy = pltpu.make_async_remote_copy(
                src_ref=cur.at[index],
                dst_ref=recv.at[base + own],
                send_sem=send_sem.at[base + other],
                recv_sem=recv_sem.at[base + own],
                device_id=peer,
                device_id_type=MESH,
            )
            copy.start()
            copies.append(copy)
        recv[base + own] = acc.astype(recv.dtype)
        for other, peer in peers:
            pltpu.make_async_remote_copy(
                src_ref=cur.at[index],
                dst_ref=recv.at[base + other],
                send_sem=send_sem.at[base + other],
                recv_sem=recv_sem.at[base + other],
                device_id=peer,
                device_id_type=MESH,
            ).wait_recv()
        for copy in copies:
            copy.wait_send()
        total = recv[base].astype(jnp.float32)
        for slot in range(1, size):
            total = total + recv[base + slot].astype(jnp.float32)
        acc = total
    o_ref[...] = acc.astype(o_ref.dtype)


def group_sum(x, axis_names, stages, wire_dtype, collective_id):
    slots = sum(size for _, _, size in stages)
    return pl.pallas_call(
        functools.partial(reduce_kernel, axis_names, stages),
        out_shape=jax.ShapeDtypeStruct(x.shape, jnp.float32),
        in_specs=[pl.BlockSpec(memory_space=pltpu.VMEM)],
        out_specs=pl.BlockSpec(memory_space=pltpu.VMEM),
        scratch_shapes=[
            pltpu.VMEM((len(stages),) + x.shape, wire_dtype),
            pltpu.VMEM((slots,) + x.shape, wire_dtype),
            pltpu.SemaphoreType.DMA((slots,)),
            pltpu.SemaphoreType.DMA((slots,)),
        ],
        compiler_params=pltpu.CompilerParams(collective_id=collective_id, has_side_effects=True),
    )(x)


def column_sum(x):
    return jnp.sum(jnp.sum(x, axis=0), axis=1, keepdims=True)


def to_row(columns):
    count = columns[0].shape[0]
    sub = lax.broadcasted_iota(jnp.int32, (count, 128), 0)
    lane = lax.broadcasted_iota(jnp.int32, (count, 128), 1)
    acc = jnp.zeros((count, 128), jnp.float32)
    for index, column in enumerate(columns):
        acc = acc + jnp.where(lane == sub + count * index, jnp.broadcast_to(column, (count, 128)), 0.0)
    return jnp.sum(acc, axis=0, keepdims=True)


def from_row(row, index, count):
    sub = lax.broadcasted_iota(jnp.int32, (count, 128), 0)
    lane = lax.broadcasted_iota(jnp.int32, (count, 128), 1)
    picked = jnp.where(lane == sub + count * index, jnp.broadcast_to(row, (count, 128)), 0.0)
    return jnp.sum(picked, axis=1, keepdims=True)


def group_size(stage):
    size = 1
    for _, extent in stage[1]:
        size *= extent
    return size


def cg_kernel(axis_names, stages, d_ref, beam_hbm, chroma_ref, weight_ref, diag_ref, pm_ref,
              est_ref, beam_ref, beam_sems, parts, rows, recv_p, recv_rows, p_send, p_recv, r_send, r_recv):
    me = {name: lax.axis_index(name) for name in axis_names}

    def place(stage):
        axis, dims = stage
        own = 0
        root = me[axis]
        scale = 1
        for stride, size in dims:
            digit = lax.rem(me[axis] // stride, size)
            own = own + digit * scale
            root = root - digit * stride
            scale *= size

        def device(other):
            coord = root
            scale = 1
            for stride, size in dims:
                coord = coord + lax.rem(other // scale, size) * stride
                scale *= size
            return tuple(coord if name == axis else me[name] for name in axis_names)

        return own, device

    barrier = pltpu.get_barrier_semaphore()
    for stage in stages:
        own, device = place(stage)
        for step in range(1, group_size(stage)):
            other = lax.rem(own + step, group_size(stage))
            pl.semaphore_signal(barrier, 1, device_id=device(other), device_id_type=MESH)

    chunks = beam_sems.shape[0]
    rows_per = beam_ref.shape[0] // chunks
    beam_copies = []
    for chunk in range(chunks):
        window = pl.ds(chunk * rows_per, rows_per)
        beam_copy = pltpu.make_async_copy(beam_hbm.at[window], beam_ref.at[window], beam_sems.at[chunk])
        beam_copy.start()
        beam_copies.append(beam_copy)

    chroma = chroma_ref[...]
    weight = weight_ref[...]
    diag = diag_ref[...]
    pm = pm_ref[...]
    channels, count = d_ref.shape[:2]
    modes = beam_ref.shape[1]

    def beam_seen(vector):
        low = (chroma * vector).astype(jnp.bfloat16).reshape(channels * count, modes)
        seen = lax.dot_general(
            low, beam_ref[...], (((1,), (1,)), ((), ())), preferred_element_type=jnp.float32
        )
        return seen.reshape(channels, count, -1)

    def beam_forward(vector):
        return (weight * beam_seen(vector)).astype(jnp.bfloat16)

    def beam_backward(heard):
        back = jnp.dot(heard.reshape(channels * count, -1), beam_ref[...], preferred_element_type=jnp.float32)
        return chroma * back.reshape(channels, count, modes)


    def exchange_start(stage, src, recv, base, send_sems, recv_sems):
        own, device = place(stage)
        size = group_size(stage)

        def copy_to(other, slot):
            return pltpu.make_async_remote_copy(
                src_ref=src,
                dst_ref=recv.at[base + slot],
                send_sem=send_sems.at[base + other],
                recv_sem=recv_sems.at[base + slot],
                device_id=device(other),
                device_id_type=MESH,
            )

        for step in range(1, size):
            copy_to(lax.rem(own + step, size), own).start()
        recv[base + own] = src[...]
        return own, size, base, recv, copy_to

    sent = []

    def exchange_finish(state):
        own, size, base, recv, copy_to = state
        for step in range(1, size):
            other = lax.rem(own + step, size)
            copy_to(other, other).wait_recv()
        sent.append(state)
        total = recv[base].astype(jnp.float32)
        for slot in range(1, size):
            total = total + recv[base + slot].astype(jnp.float32)
        return total

    counter = {"row": 0, "slot": 0, "part": 0}

    def next_row(value):
        index = counter["row"]
        counter["row"] += 1
        rows[index] = value
        return rows.at[index]

    def row_stage(stage, src):
        base = counter["slot"]
        counter["slot"] += group_size(stage)
        return exchange_start(stage, src, recv_rows, base, r_send, r_recv)

    def reduce_rest(value):
        for stage in stages[1:]:
            value = exchange_finish(row_stage(stage, next_row(value)))
        return value

    def projection_start(vector):
        index = counter["part"]
        counter["part"] += 1
        for rank in range(pm.shape[1]):
            parts[index, rank] = jnp.sum(pm[:, rank] * vector, axis=0).astype(parts.dtype)
        nz = group_size(stages[0])
        return exchange_start(stages[0], parts.at[index], recv_p, index * nz, p_send, p_recv)

    weighted = d_ref[...].reshape(channels * count, -1)
    back = None
    for chunk, beam_copy in enumerate(beam_copies):
        beam_copy.wait()
        window = slice(chunk * rows_per, (chunk + 1) * rows_per)
        term = jnp.dot(
            weighted[:, window], beam_ref[window, :], preferred_element_type=jnp.float32
        )
        back = term if back is None else back + term
    d = chroma * back.reshape(channels, count, modes)
    pl.semaphore_wait(barrier, sum(group_size(stage) - 1 for stage in stages))
    p_state = projection_start(d)
    seen = beam_seen(d)
    heard = (weight * seen).astype(jnp.bfloat16)
    quadratic = column_sum(seen * heard.astype(jnp.float32)) + column_sum(d * (diag * d))
    z_state = row_stage(stages[0], next_row(to_row([quadratic, column_sum(d * d)])))
    cb = beam_backward(heard)
    projection = exchange_finish(p_state)
    zrow = exchange_finish(z_state)
    total = reduce_rest(zrow + to_row([column_sum(projection * projection)]))
    curve = from_row(total, 0, count)
    norm_now = from_row(total, 1, count)
    step_size = (norm_now / curve)[None]
    estimate = step_size * d
    spread = pm[:, 0] * projection[0][None]
    for rank in range(1, pm.shape[1]):
        spread = spread + pm[:, rank] * projection[rank][None]
    residual = d - step_size * (cb + diag * d + spread)
    z_state = row_stage(stages[0], next_row(to_row([column_sum(residual * residual)])))
    p_state = projection_start(residual)
    cb_residual = beam_backward(beam_forward(residual))
    total = reduce_rest(exchange_finish(z_state))
    projection_residual = exchange_finish(p_state)
    norm_next = from_row(total, 0, count)
    ratio = (norm_next / norm_now)[None]
    direction = residual + ratio * d
    cb_direction = cb_residual + ratio * cb
    projection = projection_residual + ratio * projection
    zrow = exchange_finish(
        row_stage(stages[0], next_row(to_row([column_sum(direction * (cb_direction + diag * direction))])))
    )
    total = reduce_rest(zrow + to_row([column_sum(projection * projection)]))
    curve = from_row(total, 0, count)
    est_ref[...] = estimate + (norm_next / curve)[None] * direction
    for own, size, _, _, copy_to in sent:
        for step in range(1, size):
            copy_to(lax.rem(own + step, size), own).wait_send()


def cg_solve(axis_names, stages, d, beam, chroma, weight, diag, pm):
    reductions = 3
    slots = reductions * sum(group_size(stage) for stage in stages)
    rounds = reductions * len(stages)
    nz = group_size(stages[0])
    vector = jax.ShapeDtypeStruct(d.shape[:2] + beam.shape[1:], jnp.float32)
    row = jax.ShapeDtypeStruct((1, 128), jnp.float32)
    vmem = pl.BlockSpec(memory_space=pltpu.VMEM)
    part_shape = (pm.shape[1],) + vector.shape[1:]
    return pl.pallas_call(
        functools.partial(cg_kernel, axis_names, stages),
        out_shape=vector,
        in_specs=[vmem, pl.BlockSpec(memory_space=pl.ANY)] + [vmem] * 4,
        out_specs=vmem,
        scratch_shapes=[
            pltpu.VMEM(beam.shape, beam.dtype),
            pltpu.SemaphoreType.DMA((4,)),
            pltpu.VMEM((2,) + part_shape, jnp.bfloat16),
            pltpu.VMEM((rounds, 1, 128), jnp.float32),
            pltpu.VMEM((2 * nz,) + part_shape, jnp.bfloat16),
            pltpu.VMEM((slots, 1, 128), jnp.float32),
            pltpu.SemaphoreType.DMA((2 * nz,)),
            pltpu.SemaphoreType.DMA((2 * nz,)),
            pltpu.SemaphoreType.DMA((slots,)),
            pltpu.SemaphoreType.DMA((slots,)),
        ],
        compiler_params=pltpu.CompilerParams(collective_id=1, has_side_effects=True),
    )(d, beam, chroma, weight, diag, pm)


def make_shards(mesh):
    axis_names = tuple(mesh.axis_names)
    mode_devices = mesh.shape["ma"]
    freq_devices = mesh.shape["freq"]
    if mode_devices % 16 == 0:
        mode_stages = [("ma", 1, 2), ("ma", 2, 8), ("ma", 16, mode_devices // 16)]
    else:
        mode_stages = [("ma", 1, mode_devices)]
    global_stages = mode_stages + [("freq", 1, freq_devices)]
    freq_stages = [("freq", 1, freq_devices)]

    def scalar_sum(*vectors):
        rows = jnp.stack(vectors)
        padded = jnp.pad(rows, ((0, 8 - rows.shape[0]), (0, 128 - rows.shape[1])))
        summed = group_sum(padded, axis_names, global_stages, jnp.float32, 2)
        return [summed[index, : rows.shape[1]] for index in range(len(vectors))]

    def freq_sum(partial_sum):
        shape = partial_sum.shape
        flat = partial_sum.reshape(-1, shape[-1])
        summed = group_sum(flat, axis_names, freq_stages, jnp.bfloat16, 1)
        return summed.reshape(shape)

    def shards(timestream, beam_transfer, chromatic_gain, noise_weight, prior_diagonal, prior_modes):
        spectral_channels = timestream.shape[0]
        device_time_samples = timestream.shape[1]
        noise_realizations = timestream.shape[2]
        antenna_pairs = timestream.shape[3]
        mode_devices_here = mode_devices
        columns = noise_realizations * antenna_pairs // mode_devices_here
        blocks = antenna_pairs // columns
        halves = columns // 128
        send = timestream.reshape(
            spectral_channels, device_time_samples, noise_realizations, blocks, halves, 128
        ).transpose(2, 3, 0, 1, 4, 5)
        send = send.reshape(mode_devices_here, spectral_channels * device_time_samples * halves, 128)
        received = lax.all_to_all(send, "ma", 0, 0, tiled=True)
        received = received.reshape(mode_devices_here, spectral_channels, device_time_samples, columns)
        all_times = mode_devices_here * device_time_samples
        hartley = hartley_table(all_times // 2, all_times)
        hartley_high = hartley.astype(jnp.bfloat16)
        hartley_low = (hartley - hartley_high.astype(jnp.float32)).astype(jnp.bfloat16)
        hartley_high = hartley_high.reshape(all_times // 2, mode_devices_here, device_time_samples)
        hartley_low = hartley_low.reshape(all_times // 2, mode_devices_here, device_time_samples)
        mode_high = jnp.einsum(
            "mit,iftc->mfc", hartley_high, received, preferred_element_type=jnp.float32
        )
        mode_low = jnp.einsum("mit,iftc->mfc", hartley_low, received, preferred_element_type=jnp.float32)
        mode_rows = (mode_high + mode_low).astype(jnp.bfloat16)
        back_rows = lax.all_to_all(mode_rows, "ma", 0, 0, tiled=True)
        resident_modes = back_rows.shape[0] // mode_devices_here
        back_rows = back_rows.reshape(
            noise_realizations, blocks, resident_modes, spectral_channels, columns
        )
        measured_visibility = back_rows.transpose(3, 2, 0, 1, 4).reshape(
            spectral_channels, resident_modes, noise_realizations, antenna_pairs
        )
        chroma = chromatic_gain[:, None, None, :]
        diagonal = prior_diagonal[:, None, None, :]
        weighted = (noise_weight[:, :, None, :] * measured_visibility.astype(jnp.float32)).astype(
            jnp.bfloat16
        )

        assert resident_modes == 1
        if mode_devices % 16 == 0:
            cg_stages = [
                ("freq", [(1, freq_devices)]),
                ("ma", [(1, 2), (16, mode_devices // 16)]),
                ("ma", [(2, 8)]),
            ]
        else:
            cg_stages = [("freq", [(1, freq_devices)]), ("ma", [(1, mode_devices)])]
        diag_rows = prior_diagonal[:, None, :]
        mode_rows4 = prior_modes[:, :, None, :]

        def beam_back(direction):
            low = (chroma * direction).astype(jnp.bfloat16)
            seen = jnp.einsum("fmks,mbs->fmkb", low, beam_transfer, preferred_element_type=jnp.float32)
            heard = (noise_weight[:, :, None, :] * seen).astype(jnp.bfloat16)
            back = jnp.einsum(
                "fmkb,mbs->fmks", heard, beam_transfer, preferred_element_type=jnp.float32
            )
            return (chroma * back)[:, 0]

        direction = weighted[:, 0]
        operands = (beam_transfer[0], chromatic_gain[:, None, :], noise_weight, diag_rows, mode_rows4)
        estimate = cg_solve(axis_names, cg_stages, direction, *operands)
        estimate = estimate[:, None]
        return estimate

    return shards


def solution(mesh):
    in_specs = (
        P("freq", "ma", None, None),
        P("ma", None, None),
        P("freq", None),
        P("freq", "ma", None),
        P("freq", None),
        P("freq", None, None),
    )
    out_specs = P("freq", "ma", None, None)
    return jax.shard_map(make_shards(mesh), mesh=mesh, in_specs=in_specs, out_specs=out_specs, check_vma=False)
```

```python
import functools

import jax
import jax.numpy as jnp
from jax import lax
from jax.experimental import pallas as pl
from jax.experimental.pallas import tpu as pltpu
from jax.sharding import PartitionSpec as P

ITERS = 2
MESH = pl.DeviceIdType.MESH


def hartley_table(rows, cols):
    index_m = jnp.arange(rows, dtype=jnp.int32)[:, None]
    index_t = jnp.arange(cols, dtype=jnp.int32)[None, :]
    phase = (index_m * index_t % cols).astype(jnp.float32)
    angle = 2.0 * jnp.pi * phase / cols
    return (jnp.cos(angle) + jnp.sin(angle)) / jnp.sqrt(jnp.float32(cols))


def inner(left, right):
    return jnp.sum(left * right, axis=(0, 1, 3))


def reduce_kernel(axis_names, stages, x_ref, o_ref, cur, recv, send_sem, recv_sem):
    me = {name: lax.axis_index(name) for name in axis_names}

    def device(axis, coord):
        return tuple(coord if name == axis else me[name] for name in axis_names)

    plan = []
    base = 0
    for axis, stride, size in stages:
        own = (me[axis] // stride) % size
        root = me[axis] - own * stride
        peers = []
        for step in range(1, size):
            other = lax.rem(own + step, size)
            peers.append((other, device(axis, root + other * stride)))
        plan.append((base, own, size, peers))
        base += size

    barrier = pltpu.get_barrier_semaphore()
    for _, _, _, peers in plan:
        for _, peer in peers:
            pl.semaphore_signal(barrier, 1, device_id=peer, device_id_type=MESH)
    pl.semaphore_wait(barrier, sum(len(peers) for _, _, _, peers in plan))

    acc = x_ref[...].astype(jnp.float32)
    for index, (base, own, size, peers) in enumerate(plan):
        cur[index] = acc.astype(cur.dtype)
        copies = []
        for other, peer in peers:
            copy = pltpu.make_async_remote_copy(
                src_ref=cur.at[index],
                dst_ref=recv.at[base + own],
                send_sem=send_sem.at[base + other],
                recv_sem=recv_sem.at[base + own],
                device_id=peer,
                device_id_type=MESH,
            )
            copy.start()
            copies.append(copy)
        recv[base + own] = acc.astype(recv.dtype)
        for other, peer in peers:
            pltpu.make_async_remote_copy(
                src_ref=cur.at[index],
                dst_ref=recv.at[base + other],
                send_sem=send_sem.at[base + other],
                recv_sem=recv_sem.at[base + other],
                device_id=peer,
                device_id_type=MESH,
            ).wait_recv()
        for copy in copies:
            copy.wait_send()
        total = recv[base].astype(jnp.float32)
        for slot in range(1, size):
            total = total + recv[base + slot].astype(jnp.float32)
        acc = total
    o_ref[...] = acc.astype(o_ref.dtype)


def group_sum(x, axis_names, stages, wire_dtype, collective_id):
    slots = sum(size for _, _, size in stages)
    return pl.pallas_call(
        functools.partial(reduce_kernel, axis_names, stages),
        out_shape=jax.ShapeDtypeStruct(x.shape, jnp.float32),
        in_specs=[pl.BlockSpec(memory_space=pltpu.VMEM)],
        out_specs=pl.BlockSpec(memory_space=pltpu.VMEM),
        scratch_shapes=[
            pltpu.VMEM((len(stages),) + x.shape, wire_dtype),
            pltpu.VMEM((slots,) + x.shape, wire_dtype),
            pltpu.SemaphoreType.DMA((slots,)),
            pltpu.SemaphoreType.DMA((slots,)),
        ],
        compiler_params=pltpu.CompilerParams(collective_id=collective_id, has_side_effects=True),
    )(x)


def column_sum(x):
    return jnp.sum(jnp.sum(x, axis=0), axis=1, keepdims=True)


def to_row(columns):
    count = columns[0].shape[0]
    sub = lax.broadcasted_iota(jnp.int32, (count, 128), 0)
    lane = lax.broadcasted_iota(jnp.int32, (count, 128), 1)
    acc = jnp.zeros((count, 128), jnp.float32)
    for index, column in enumerate(columns):
        acc = acc + jnp.where(lane == sub + count * index, jnp.broadcast_to(column, (count, 128)), 0.0)
    return jnp.sum(acc, axis=0, keepdims=True)


def from_row(row, index, count):
    sub = lax.broadcasted_iota(jnp.int32, (count, 128), 0)
    lane = lax.broadcasted_iota(jnp.int32, (count, 128), 1)
    picked = jnp.where(lane == sub + count * index, jnp.broadcast_to(row, (count, 128)), 0.0)
    return jnp.sum(picked, axis=1, keepdims=True)


def group_size(stage):
    size = 1
    for _, extent in stage[1]:
        size *= extent
    return size


def cg_kernel(axis_names, stages, d_ref, beam_hbm, chroma_ref, weight_ref, diag_ref, pm_ref,
              est_ref, beam_ref, beam_sems, parts, rows, recv_p, recv_rows, p_send, p_recv, r_send, r_recv):
    me = {name: lax.axis_index(name) for name in axis_names}

    def place(stage):
        axis, dims = stage
        own = 0
        root = me[axis]
        scale = 1
        for stride, size in dims:
            digit = lax.rem(me[axis] // stride, size)
            own = own + digit * scale
            root = root - digit * stride
            scale *= size

        def device(other):
            coord = root
            scale = 1
            for stride, size in dims:
                coord = coord + lax.rem(other // scale, size) * stride
                scale *= size
            return tuple(coord if name == axis else me[name] for name in axis_names)

        return own, device

    barrier = pltpu.get_barrier_semaphore()
    for stage in stages:
        own, device = place(stage)
        for step in range(1, group_size(stage)):
            other = lax.rem(own + step, group_size(stage))
            pl.semaphore_signal(barrier, 1, device_id=device(other), device_id_type=MESH)

    chunks = beam_sems.shape[0]
    rows_per = beam_ref.shape[0] // chunks
    beam_copies = []
    for chunk in range(chunks):
        window = pl.ds(chunk * rows_per, rows_per)
        beam_copy = pltpu.make_async_copy(beam_hbm.at[window], beam_ref.at[window], beam_sems.at[chunk])
        beam_copy.start()
        beam_copies.append(beam_copy)

    chroma = chroma_ref[...]
    weight = weight_ref[...]
    diag = diag_ref[...]
    pm = pm_ref[...]
    channels, count = d_ref.shape[:2]
    modes = beam_ref.shape[1]

    def beam_seen(vector):
        low = (chroma * vector).astype(jnp.bfloat16).reshape(channels * count, modes)
        seen = lax.dot_general(
            low, beam_ref[...], (((1,), (1,)), ((), ())), preferred_element_type=jnp.float32
        )
        return seen.reshape(channels, count, -1)

    def beam_forward(vector):
        return (weight * beam_seen(vector)).astype(jnp.bfloat16)

    def beam_backward(heard):
        back = jnp.dot(heard.reshape(channels * count, -1), beam_ref[...], preferred_element_type=jnp.float32)
        return chroma * back.reshape(channels, count, modes)


    def exchange_start(stage, src, recv, base, send_sems, recv_sems):
        own, device = place(stage)
        size = group_size(stage)

        def copy_to(other, slot):
            return pltpu.make_async_remote_copy(
                src_ref=src,
                dst_ref=recv.at[base + slot],
                send_sem=send_sems.at[base + other],
                recv_sem=recv_sems.at[base + slot],
                device_id=device(other),
                device_id_type=MESH,
            )

        for step in range(1, size):
            copy_to(lax.rem(own + step, size), own).start()
        recv[base + own] = src[...]
        return own, size, base, recv, copy_to

    sent = []

    def exchange_finish(state):
        own, size, base, recv, copy_to = state
        for step in range(1, size):
            other = lax.rem(own + step, size)
            copy_to(other, other).wait_recv()
        sent.append(state)
        total = recv[base].astype(jnp.float32)
        for slot in range(1, size):
            total = total + recv[base + slot].astype(jnp.float32)
        return total

    counter = {"row": 0, "slot": 0, "part": 0}

    def next_row(value):
        index = counter["row"]
        counter["row"] += 1
        rows[index] = value
        return rows.at[index]

    def row_stage(stage, src):
        base = counter["slot"]
        counter["slot"] += group_size(stage)
        return exchange_start(stage, src, recv_rows, base, r_send, r_recv)

    def reduce_rest(value):
        for stage in stages[1:]:
            value = exchange_finish(row_stage(stage, next_row(value)))
        return value

    def projection_start(vector):
        index = counter["part"]
        counter["part"] += 1
        for rank in range(pm.shape[1]):
            parts[index, rank] = jnp.sum(pm[:, rank] * vector, axis=0).astype(parts.dtype)
        nz = group_size(stages[0])
        return exchange_start(stages[0], parts.at[index], recv_p, index * nz, p_send, p_recv)

    weighted = d_ref[...].reshape(channels * count, -1)
    back = None
    for chunk, beam_copy in enumerate(beam_copies):
        beam_copy.wait()
        window = slice(chunk * rows_per, (chunk + 1) * rows_per)
        term = jnp.dot(
            weighted[:, window], beam_ref[window, :], preferred_element_type=jnp.float32
        )
        back = term if back is None else back + term
    d = chroma * back.reshape(channels, count, modes)
    pl.semaphore_wait(barrier, sum(group_size(stage) - 1 for stage in stages))
    p_state = projection_start(d)
    seen = beam_seen(d)
    heard = (weight * seen).astype(jnp.bfloat16)
    quadratic = column_sum(seen * heard.astype(jnp.float32)) + column_sum(d * (diag * d))
    z_state = row_stage(stages[0], next_row(to_row([quadratic, column_sum(d * d)])))
    cb = beam_backward(heard)
    projection = exchange_finish(p_state)
    zrow = exchange_finish(z_state)
    total = reduce_rest(zrow + to_row([column_sum(projection * projection)]))
    curve = from_row(total, 0, count)
    norm_now = from_row(total, 1, count)
    step_size = (norm_now / curve)[None]
    estimate = step_size * d
    spread = pm[:, 0] * projection[0][None]
    for rank in range(1, pm.shape[1]):
        spread = spread + pm[:, rank] * projection[rank][None]
    residual = d - step_size * (cb + diag * d + spread)
    z_state = row_stage(stages[0], next_row(to_row([column_sum(residual * residual)])))
    cb_residual = beam_backward(beam_forward(residual))
    zrow = exchange_finish(z_state)
    p_state = projection_start(residual)
    total = reduce_rest(zrow)
    projection_residual = exchange_finish(p_state)
    norm_next = from_row(total, 0, count)
    ratio = (norm_next / norm_now)[None]
    direction = residual + ratio * d
    cb_direction = cb_residual + ratio * cb
    projection = projection_residual + ratio * projection
    zrow = exchange_finish(
        row_stage(stages[0], next_row(to_row([column_sum(direction * (cb_direction + diag * direction))])))
    )
    total = reduce_rest(zrow + to_row([column_sum(projection * projection)]))
    curve = from_row(total, 0, count)
    est_ref[...] = estimate + (norm_next / curve)[None] * direction
    for own, size, _, _, copy_to in sent:
        for step in range(1, size):
            copy_to(lax.rem(own + step, size), own).wait_send()


def cg_solve(axis_names, stages, d, beam, chroma, weight, diag, pm):
    reductions = 3
    slots = reductions * sum(group_size(stage) for stage in stages)
    rounds = reductions * len(stages)
    nz = group_size(stages[0])
    vector = jax.ShapeDtypeStruct(d.shape[:2] + beam.shape[1:], jnp.float32)
    row = jax.ShapeDtypeStruct((1, 128), jnp.float32)
    vmem = pl.BlockSpec(memory_space=pltpu.VMEM)
    part_shape = (pm.shape[1],) + vector.shape[1:]
    return pl.pallas_call(
        functools.partial(cg_kernel, axis_names, stages),
        out_shape=vector,
        in_specs=[vmem, pl.BlockSpec(memory_space=pl.ANY)] + [vmem] * 4,
        out_specs=vmem,
        scratch_shapes=[
            pltpu.VMEM(beam.shape, beam.dtype),
            pltpu.SemaphoreType.DMA((4,)),
            pltpu.VMEM((2,) + part_shape, jnp.bfloat16),
            pltpu.VMEM((rounds, 1, 128), jnp.float32),
            pltpu.VMEM((2 * nz,) + part_shape, jnp.bfloat16),
            pltpu.VMEM((slots, 1, 128), jnp.float32),
            pltpu.SemaphoreType.DMA((2 * nz,)),
            pltpu.SemaphoreType.DMA((2 * nz,)),
            pltpu.SemaphoreType.DMA((slots,)),
            pltpu.SemaphoreType.DMA((slots,)),
        ],
        compiler_params=pltpu.CompilerParams(collective_id=1, has_side_effects=True),
    )(d, beam, chroma, weight, diag, pm)


def make_shards(mesh):
    axis_names = tuple(mesh.axis_names)
    mode_devices = mesh.shape["ma"]
    freq_devices = mesh.shape["freq"]
    if mode_devices % 16 == 0:
        mode_stages = [("ma", 1, 2), ("ma", 2, 8), ("ma", 16, mode_devices // 16)]
    else:
        mode_stages = [("ma", 1, mode_devices)]
    global_stages = mode_stages + [("freq", 1, freq_devices)]
    freq_stages = [("freq", 1, freq_devices)]

    def scalar_sum(*vectors):
        rows = jnp.stack(vectors)
        padded = jnp.pad(rows, ((0, 8 - rows.shape[0]), (0, 128 - rows.shape[1])))
        summed = group_sum(padded, axis_names, global_stages, jnp.float32, 2)
        return [summed[index, : rows.shape[1]] for index in range(len(vectors))]

    def freq_sum(partial_sum):
        shape = partial_sum.shape
        flat = partial_sum.reshape(-1, shape[-1])
        summed = group_sum(flat, axis_names, freq_stages, jnp.bfloat16, 1)
        return summed.reshape(shape)

    def shards(timestream, beam_transfer, chromatic_gain, noise_weight, prior_diagonal, prior_modes):
        spectral_channels = timestream.shape[0]
        device_time_samples = timestream.shape[1]
        noise_realizations = timestream.shape[2]
        antenna_pairs = timestream.shape[3]
        mode_devices_here = mode_devices
        columns = noise_realizations * antenna_pairs // mode_devices_here
        blocks = antenna_pairs // columns
        halves = columns // 128
        send = timestream.reshape(
            spectral_channels, device_time_samples, noise_realizations, blocks, halves, 128
        ).transpose(2, 3, 0, 1, 4, 5)
        send = send.reshape(mode_devices_here, spectral_channels * device_time_samples * halves, 128)
        received = lax.all_to_all(send, "ma", 0, 0, tiled=True)
        received = received.reshape(mode_devices_here, spectral_channels, device_time_samples, columns)
        all_times = mode_devices_here * device_time_samples
        hartley = hartley_table(all_times // 2, all_times)
        hartley_high = hartley.astype(jnp.bfloat16)
        hartley_low = (hartley - hartley_high.astype(jnp.float32)).astype(jnp.bfloat16)
        hartley_high = hartley_high.reshape(all_times // 2, mode_devices_here, device_time_samples)
        hartley_low = hartley_low.reshape(all_times // 2, mode_devices_here, device_time_samples)
        mode_high = jnp.einsum(
            "mit,iftc->mfc", hartley_high, received, preferred_element_type=jnp.float32
        )
        mode_low = jnp.einsum("mit,iftc->mfc", hartley_low, received, preferred_element_type=jnp.float32)
        mode_rows = (mode_high + mode_low).astype(jnp.bfloat16)
        back_rows = lax.all_to_all(mode_rows, "ma", 0, 0, tiled=True)
        resident_modes = back_rows.shape[0] // mode_devices_here
        back_rows = back_rows.reshape(
            noise_realizations, blocks, resident_modes, spectral_channels, columns
        )
        measured_visibility = back_rows.transpose(3, 2, 0, 1, 4).reshape(
            spectral_channels, resident_modes, noise_realizations, antenna_pairs
        )
        chroma = chromatic_gain[:, None, None, :]
        diagonal = prior_diagonal[:, None, None, :]
        weighted = (noise_weight[:, :, None, :] * measured_visibility.astype(jnp.float32)).astype(
            jnp.bfloat16
        )

        assert resident_modes == 1
        if mode_devices % 16 == 0:
            cg_stages = [
                ("freq", [(1, freq_devices)]),
                ("ma", [(1, 2), (16, mode_devices // 16)]),
                ("ma", [(2, 8)]),
            ]
        else:
            cg_stages = [("freq", [(1, freq_devices)]), ("ma", [(1, mode_devices)])]
        diag_rows = prior_diagonal[:, None, :]
        mode_rows4 = prior_modes[:, :, None, :]

        def beam_back(direction):
            low = (chroma * direction).astype(jnp.bfloat16)
            seen = jnp.einsum("fmks,mbs->fmkb", low, beam_transfer, preferred_element_type=jnp.float32)
            heard = (noise_weight[:, :, None, :] * seen).astype(jnp.bfloat16)
            back = jnp.einsum(
                "fmkb,mbs->fmks", heard, beam_transfer, preferred_element_type=jnp.float32
            )
            return (chroma * back)[:, 0]

        direction = weighted[:, 0]
        operands = (beam_transfer[0], chromatic_gain[:, None, :], noise_weight, diag_rows, mode_rows4)
        estimate = cg_solve(axis_names, cg_stages, direction, *operands)
        estimate = estimate[:, None]
        return estimate

    return shards


def solution(mesh):
    in_specs = (
        P("freq", "ma", None, None),
        P("ma", None, None),
        P("freq", None),
        P("freq", "ma", None),
        P("freq", None),
        P("freq", None, None),
    )
    out_specs = P("freq", "ma", None, None)
    return jax.shard_map(make_shards(mesh), mesh=mesh, in_specs=in_specs, out_specs=out_specs, check_vma=False)
```

```python
import functools

import jax
import jax.numpy as jnp
from jax import lax
from jax.experimental import pallas as pl
from jax.experimental.pallas import tpu as pltpu
from jax.sharding import PartitionSpec as P

ITERS = 2
MESH = pl.DeviceIdType.MESH


def hartley_table(rows, cols):
    index_m = jnp.arange(rows, dtype=jnp.int32)[:, None]
    index_t = jnp.arange(cols, dtype=jnp.int32)[None, :]
    phase = (index_m * index_t % cols).astype(jnp.float32)
    angle = 2.0 * jnp.pi * phase / cols
    return (jnp.cos(angle) + jnp.sin(angle)) / jnp.sqrt(jnp.float32(cols))


def inner(left, right):
    return jnp.sum(left * right, axis=(0, 1, 3))


def reduce_kernel(axis_names, stages, x_ref, o_ref, cur, recv, send_sem, recv_sem):
    me = {name: lax.axis_index(name) for name in axis_names}

    def device(axis, coord):
        return tuple(coord if name == axis else me[name] for name in axis_names)

    plan = []
    base = 0
    for axis, stride, size in stages:
        own = (me[axis] // stride) % size
        root = me[axis] - own * stride
        peers = []
        for step in range(1, size):
            other = lax.rem(own + step, size)
            peers.append((other, device(axis, root + other * stride)))
        plan.append((base, own, size, peers))
        base += size

    barrier = pltpu.get_barrier_semaphore()
    for _, _, _, peers in plan:
        for _, peer in peers:
            pl.semaphore_signal(barrier, 1, device_id=peer, device_id_type=MESH)
    pl.semaphore_wait(barrier, sum(len(peers) for _, _, _, peers in plan))

    acc = x_ref[...].astype(jnp.float32)
    for index, (base, own, size, peers) in enumerate(plan):
        cur[index] = acc.astype(cur.dtype)
        copies = []
        for other, peer in peers:
            copy = pltpu.make_async_remote_copy(
                src_ref=cur.at[index],
                dst_ref=recv.at[base + own],
                send_sem=send_sem.at[base + other],
                recv_sem=recv_sem.at[base + own],
                device_id=peer,
                device_id_type=MESH,
            )
            copy.start()
            copies.append(copy)
        recv[base + own] = acc.astype(recv.dtype)
        for other, peer in peers:
            pltpu.make_async_remote_copy(
                src_ref=cur.at[index],
                dst_ref=recv.at[base + other],
                send_sem=send_sem.at[base + other],
                recv_sem=recv_sem.at[base + other],
                device_id=peer,
                device_id_type=MESH,
            ).wait_recv()
        for copy in copies:
            copy.wait_send()
        total = recv[base].astype(jnp.float32)
        for slot in range(1, size):
            total = total + recv[base + slot].astype(jnp.float32)
        acc = total
    o_ref[...] = acc.astype(o_ref.dtype)


def group_sum(x, axis_names, stages, wire_dtype, collective_id):
    slots = sum(size for _, _, size in stages)
    return pl.pallas_call(
        functools.partial(reduce_kernel, axis_names, stages),
        out_shape=jax.ShapeDtypeStruct(x.shape, jnp.float32),
        in_specs=[pl.BlockSpec(memory_space=pltpu.VMEM)],
        out_specs=pl.BlockSpec(memory_space=pltpu.VMEM),
        scratch_shapes=[
            pltpu.VMEM((len(stages),) + x.shape, wire_dtype),
            pltpu.VMEM((slots,) + x.shape, wire_dtype),
            pltpu.SemaphoreType.DMA((slots,)),
            pltpu.SemaphoreType.DMA((slots,)),
        ],
        compiler_params=pltpu.CompilerParams(collective_id=collective_id, has_side_effects=True),
    )(x)


def column_sum(x):
    return jnp.sum(jnp.sum(x, axis=0), axis=1, keepdims=True)


def to_row(columns):
    count = columns[0].shape[0]
    sub = lax.broadcasted_iota(jnp.int32, (count, 128), 0)
    lane = lax.broadcasted_iota(jnp.int32, (count, 128), 1)
    acc = jnp.zeros((count, 128), jnp.float32)
    for index, column in enumerate(columns):
        acc = acc + jnp.where(lane == sub + count * index, jnp.broadcast_to(column, (count, 128)), 0.0)
    return jnp.sum(acc, axis=0, keepdims=True)


def from_row(row, index, count):
    sub = lax.broadcasted_iota(jnp.int32, (count, 128), 0)
    lane = lax.broadcasted_iota(jnp.int32, (count, 128), 1)
    picked = jnp.where(lane == sub + count * index, jnp.broadcast_to(row, (count, 128)), 0.0)
    return jnp.sum(picked, axis=1, keepdims=True)


def group_size(stage):
    size = 1
    for _, extent in stage[1]:
        size *= extent
    return size


def cg_kernel(axis_names, stages, d_ref, beam_hbm, chroma_ref, weight_ref, diag_ref, pm_ref,
              est_ref, next_ref, step_ref, beam_ref, beam_sems, parts, rows, recv_p, recv_rows, p_send, p_recv, r_send, r_recv):
    me = {name: lax.axis_index(name) for name in axis_names}

    def place(stage):
        axis, dims = stage
        own = 0
        root = me[axis]
        scale = 1
        for stride, size in dims:
            digit = lax.rem(me[axis] // stride, size)
            own = own + digit * scale
            root = root - digit * stride
            scale *= size

        def device(other):
            coord = root
            scale = 1
            for stride, size in dims:
                coord = coord + lax.rem(other // scale, size) * stride
                scale *= size
            return tuple(coord if name == axis else me[name] for name in axis_names)

        return own, device

    barrier = pltpu.get_barrier_semaphore()
    for stage in stages:
        own, device = place(stage)
        for step in range(1, group_size(stage)):
            other = lax.rem(own + step, group_size(stage))
            pl.semaphore_signal(barrier, 1, device_id=device(other), device_id_type=MESH)

    chunks = beam_sems.shape[0]
    rows_per = beam_ref.shape[0] // chunks
    beam_copies = []
    for chunk in range(chunks):
        window = pl.ds(chunk * rows_per, rows_per)
        beam_copy = pltpu.make_async_copy(beam_hbm.at[window], beam_ref.at[window], beam_sems.at[chunk])
        beam_copy.start()
        beam_copies.append(beam_copy)

    chroma = chroma_ref[...]
    weight = weight_ref[...]
    diag = diag_ref[...]
    pm = pm_ref[...]
    channels, count = d_ref.shape[:2]
    modes = beam_ref.shape[1]

    def beam_seen(vector):
        low = (chroma * vector).astype(jnp.bfloat16).reshape(channels * count, modes)
        seen = lax.dot_general(
            low, beam_ref[...], (((1,), (1,)), ((), ())), preferred_element_type=jnp.float32
        )
        return seen.reshape(channels, count, -1)

    def beam_forward(vector):
        return (weight * beam_seen(vector)).astype(jnp.bfloat16)

    def beam_backward(heard):
        back = jnp.dot(heard.reshape(channels * count, -1), beam_ref[...], preferred_element_type=jnp.float32)
        return chroma * back.reshape(channels, count, modes)


    def exchange_start(stage, src, recv, base, send_sems, recv_sems):
        own, device = place(stage)
        size = group_size(stage)

        def copy_to(other, slot):
            return pltpu.make_async_remote_copy(
                src_ref=src,
                dst_ref=recv.at[base + slot],
                send_sem=send_sems.at[base + other],
                recv_sem=recv_sems.at[base + slot],
                device_id=device(other),
                device_id_type=MESH,
            )

        for step in range(1, size):
            copy_to(lax.rem(own + step, size), own).start()
        recv[base + own] = src[...]
        return own, size, base, recv, copy_to

    sent = []

    def exchange_finish(state):
        own, size, base, recv, copy_to = state
        for step in range(1, size):
            other = lax.rem(own + step, size)
            copy_to(other, other).wait_recv()
        sent.append(state)
        total = recv[base].astype(jnp.float32)
        for slot in range(1, size):
            total = total + recv[base + slot].astype(jnp.float32)
        return total

    counter = {"row": 0, "slot": 0, "part": 0}

    def next_row(value):
        index = counter["row"]
        counter["row"] += 1
        rows[index] = value
        return rows.at[index]

    def row_stage(stage, src):
        base = counter["slot"]
        counter["slot"] += group_size(stage)
        return exchange_start(stage, src, recv_rows, base, r_send, r_recv)

    def reduce_rest(value):
        for stage in stages[1:]:
            value = exchange_finish(row_stage(stage, next_row(value)))
        return value

    def projection_start(vector):
        index = counter["part"]
        counter["part"] += 1
        for rank in range(pm.shape[1]):
            parts[index, rank] = jnp.sum(pm[:, rank] * vector, axis=0).astype(parts.dtype)
        nz = group_size(stages[0])
        return exchange_start(stages[0], parts.at[index], recv_p, index * nz, p_send, p_recv)

    weighted = d_ref[...].reshape(channels * count, -1)
    back = None
    for chunk, beam_copy in enumerate(beam_copies):
        beam_copy.wait()
        window = slice(chunk * rows_per, (chunk + 1) * rows_per)
        term = jnp.dot(
            weighted[:, window], beam_ref[window, :], preferred_element_type=jnp.float32
        )
        back = term if back is None else back + term
    d = chroma * back.reshape(channels, count, modes)
    pl.semaphore_wait(barrier, sum(group_size(stage) - 1 for stage in stages))
    p_state = projection_start(d)
    seen = beam_seen(d)
    heard = (weight * seen).astype(jnp.bfloat16)
    quadratic = column_sum(seen * heard.astype(jnp.float32)) + column_sum(d * (diag * d))
    z_state = row_stage(stages[0], next_row(to_row([quadratic, column_sum(d * d)])))
    cb = beam_backward(heard)
    projection = exchange_finish(p_state)
    zrow = exchange_finish(z_state)
    total = reduce_rest(zrow + to_row([column_sum(projection * projection)]))
    curve = from_row(total, 0, count)
    norm_now = from_row(total, 1, count)
    step_size = (norm_now / curve)[None]
    estimate = step_size * d
    spread = pm[:, 0] * projection[0][None]
    for rank in range(1, pm.shape[1]):
        spread = spread + pm[:, rank] * projection[rank][None]
    residual = d - step_size * (cb + diag * d + spread)
    z_state = row_stage(stages[0], next_row(to_row([column_sum(residual * residual)])))
    p_state = projection_start(residual)
    cb_residual = beam_backward(beam_forward(residual))
    total = reduce_rest(exchange_finish(z_state))
    projection_residual = exchange_finish(p_state)
    norm_next = from_row(total, 0, count)
    ratio = (norm_next / norm_now)[None]
    direction = residual + ratio * d
    cb_direction = cb_residual + ratio * cb
    projection = projection_residual + ratio * projection
    zrow = exchange_finish(
        row_stage(stages[0], next_row(to_row([column_sum(direction * (cb_direction + diag * direction))])))
    )
    total = reduce_rest(zrow + to_row([column_sum(projection * projection)]))
    curve = from_row(total, 0, count)
    est_ref[...] = estimate
    next_ref[...] = direction
    step_ref[...] = to_row([norm_next / curve])
    for own, size, _, _, copy_to in sent:
        for step in range(1, size):
            copy_to(lax.rem(own + step, size), own).wait_send()


def cg_solve(axis_names, stages, d, beam, chroma, weight, diag, pm):
    reductions = 3
    slots = reductions * sum(group_size(stage) for stage in stages)
    rounds = reductions * len(stages)
    nz = group_size(stages[0])
    vector = jax.ShapeDtypeStruct(d.shape[:2] + beam.shape[1:], jnp.float32)
    row = jax.ShapeDtypeStruct((1, 128), jnp.float32)
    vmem = pl.BlockSpec(memory_space=pltpu.VMEM)
    part_shape = (pm.shape[1],) + vector.shape[1:]
    estimate, direction, step_row = pl.pallas_call(
        functools.partial(cg_kernel, axis_names, stages),
        out_shape=(vector, vector, row),
        in_specs=[vmem, pl.BlockSpec(memory_space=pl.ANY)] + [vmem] * 4,
        out_specs=(vmem, vmem, vmem),
        scratch_shapes=[
            pltpu.VMEM(beam.shape, beam.dtype),
            pltpu.SemaphoreType.DMA((4,)),
            pltpu.VMEM((2,) + part_shape, jnp.bfloat16),
            pltpu.VMEM((rounds, 1, 128), jnp.float32),
            pltpu.VMEM((2 * nz,) + part_shape, jnp.bfloat16),
            pltpu.VMEM((slots, 1, 128), jnp.float32),
            pltpu.SemaphoreType.DMA((2 * nz,)),
            pltpu.SemaphoreType.DMA((2 * nz,)),
            pltpu.SemaphoreType.DMA((slots,)),
            pltpu.SemaphoreType.DMA((slots,)),
        ],
        compiler_params=pltpu.CompilerParams(collective_id=1, has_side_effects=True),
    )(d, beam, chroma, weight, diag, pm)
    return pl.pallas_call(
        finish_kernel,
        out_shape=vector,
        in_specs=[vmem] * 3,
        out_specs=vmem,
    )(estimate, direction, step_row)


def finish_kernel(est_ref, direction_ref, step_ref, out_ref):
    count = direction_ref.shape[1]
    step_size = from_row(step_ref[...], 0, count)
    out_ref[...] = est_ref[...] + step_size[None] * direction_ref[...]


def make_shards(mesh):
    axis_names = tuple(mesh.axis_names)
    mode_devices = mesh.shape["ma"]
    freq_devices = mesh.shape["freq"]
    if mode_devices % 16 == 0:
        mode_stages = [("ma", 1, 2), ("ma", 2, 8), ("ma", 16, mode_devices // 16)]
    else:
        mode_stages = [("ma", 1, mode_devices)]
    global_stages = mode_stages + [("freq", 1, freq_devices)]
    freq_stages = [("freq", 1, freq_devices)]

    def scalar_sum(*vectors):
        rows = jnp.stack(vectors)
        padded = jnp.pad(rows, ((0, 8 - rows.shape[0]), (0, 128 - rows.shape[1])))
        summed = group_sum(padded, axis_names, global_stages, jnp.float32, 2)
        return [summed[index, : rows.shape[1]] for index in range(len(vectors))]

    def freq_sum(partial_sum):
        shape = partial_sum.shape
        flat = partial_sum.reshape(-1, shape[-1])
        summed = group_sum(flat, axis_names, freq_stages, jnp.bfloat16, 1)
        return summed.reshape(shape)

    def shards(timestream, beam_transfer, chromatic_gain, noise_weight, prior_diagonal, prior_modes):
        spectral_channels = timestream.shape[0]
        device_time_samples = timestream.shape[1]
        noise_realizations = timestream.shape[2]
        antenna_pairs = timestream.shape[3]
        mode_devices_here = mode_devices
        columns = noise_realizations * antenna_pairs // mode_devices_here
        blocks = antenna_pairs // columns
        halves = columns // 128
        send = timestream.reshape(
            spectral_channels, device_time_samples, noise_realizations, blocks, halves, 128
        ).transpose(2, 3, 0, 1, 4, 5)
        send = send.reshape(mode_devices_here, spectral_channels * device_time_samples * halves, 128)
        received = lax.all_to_all(send, "ma", 0, 0, tiled=True)
        received = received.reshape(mode_devices_here, spectral_channels, device_time_samples, columns)
        all_times = mode_devices_here * device_time_samples
        hartley = hartley_table(all_times // 2, all_times)
        hartley_high = hartley.astype(jnp.bfloat16)
        hartley_low = (hartley - hartley_high.astype(jnp.float32)).astype(jnp.bfloat16)
        hartley_high = hartley_high.reshape(all_times // 2, mode_devices_here, device_time_samples)
        hartley_low = hartley_low.reshape(all_times // 2, mode_devices_here, device_time_samples)
        mode_high = jnp.einsum(
            "mit,iftc->mfc", hartley_high, received, preferred_element_type=jnp.float32
        )
        mode_low = jnp.einsum("mit,iftc->mfc", hartley_low, received, preferred_element_type=jnp.float32)
        mode_rows = (mode_high + mode_low).astype(jnp.bfloat16)
        back_rows = lax.all_to_all(mode_rows, "ma", 0, 0, tiled=True)
        resident_modes = back_rows.shape[0] // mode_devices_here
        back_rows = back_rows.reshape(
            noise_realizations, blocks, resident_modes, spectral_channels, columns
        )
        measured_visibility = back_rows.transpose(3, 2, 0, 1, 4).reshape(
            spectral_channels, resident_modes, noise_realizations, antenna_pairs
        )
        chroma = chromatic_gain[:, None, None, :]
        diagonal = prior_diagonal[:, None, None, :]
        weighted = (noise_weight[:, :, None, :] * measured_visibility.astype(jnp.float32)).astype(
            jnp.bfloat16
        )

        assert resident_modes == 1
        if mode_devices % 16 == 0:
            cg_stages = [
                ("freq", [(1, freq_devices)]),
                ("ma", [(1, 2), (16, mode_devices // 16)]),
                ("ma", [(2, 8)]),
            ]
        else:
            cg_stages = [("freq", [(1, freq_devices)]), ("ma", [(1, mode_devices)])]
        diag_rows = prior_diagonal[:, None, :]
        mode_rows4 = prior_modes[:, :, None, :]

        def beam_back(direction):
            low = (chroma * direction).astype(jnp.bfloat16)
            seen = jnp.einsum("fmks,mbs->fmkb", low, beam_transfer, preferred_element_type=jnp.float32)
            heard = (noise_weight[:, :, None, :] * seen).astype(jnp.bfloat16)
            back = jnp.einsum(
                "fmkb,mbs->fmks", heard, beam_transfer, preferred_element_type=jnp.float32
            )
            return (chroma * back)[:, 0]

        direction = weighted[:, 0]
        operands = (beam_transfer[0], chromatic_gain[:, None, :], noise_weight, diag_rows, mode_rows4)
        estimate = cg_solve(axis_names, cg_stages, direction, *operands)
        estimate = estimate[:, None]
        return estimate

    return shards


def solution(mesh):
    in_specs = (
        P("freq", "ma", None, None),
        P("ma", None, None),
        P("freq", None),
        P("freq", "ma", None),
        P("freq", None),
        P("freq", None, None),
    )
    out_specs = P("freq", "ma", None, None)
    return jax.shard_map(make_shards(mesh), mesh=mesh, in_specs=in_specs, out_specs=out_specs, check_vma=False)
```

```python
import functools

import jax
import jax.numpy as jnp
from jax import lax
from jax.experimental import pallas as pl
from jax.experimental.pallas import tpu as pltpu
from jax.sharding import PartitionSpec as P

ITERS = 2
MESH = pl.DeviceIdType.MESH


def hartley_table(rows, cols):
    index_m = jnp.arange(rows, dtype=jnp.int32)[:, None]
    index_t = jnp.arange(cols, dtype=jnp.int32)[None, :]
    phase = (index_m * index_t % cols).astype(jnp.float32)
    angle = 2.0 * jnp.pi * phase / cols
    return (jnp.cos(angle) + jnp.sin(angle)) / jnp.sqrt(jnp.float32(cols))


def inner(left, right):
    return jnp.sum(left * right, axis=(0, 1, 3))


def reduce_kernel(axis_names, stages, x_ref, o_ref, cur, recv, send_sem, recv_sem):
    me = {name: lax.axis_index(name) for name in axis_names}

    def device(axis, coord):
        return tuple(coord if name == axis else me[name] for name in axis_names)

    plan = []
    base = 0
    for axis, stride, size in stages:
        own = (me[axis] // stride) % size
        root = me[axis] - own * stride
        peers = []
        for step in range(1, size):
            other = lax.rem(own + step, size)
            peers.append((other, device(axis, root + other * stride)))
        plan.append((base, own, size, peers))
        base += size

    barrier = pltpu.get_barrier_semaphore()
    for _, _, _, peers in plan:
        for _, peer in peers:
            pl.semaphore_signal(barrier, 1, device_id=peer, device_id_type=MESH)
    pl.semaphore_wait(barrier, sum(len(peers) for _, _, _, peers in plan))

    acc = x_ref[...].astype(jnp.float32)
    for index, (base, own, size, peers) in enumerate(plan):
        cur[index] = acc.astype(cur.dtype)
        copies = []
        for other, peer in peers:
            copy = pltpu.make_async_remote_copy(
                src_ref=cur.at[index],
                dst_ref=recv.at[base + own],
                send_sem=send_sem.at[base + other],
                recv_sem=recv_sem.at[base + own],
                device_id=peer,
                device_id_type=MESH,
            )
            copy.start()
            copies.append(copy)
        recv[base + own] = acc.astype(recv.dtype)
        for other, peer in peers:
            pltpu.make_async_remote_copy(
                src_ref=cur.at[index],
                dst_ref=recv.at[base + other],
                send_sem=send_sem.at[base + other],
                recv_sem=recv_sem.at[base + other],
                device_id=peer,
                device_id_type=MESH,
            ).wait_recv()
        for copy in copies:
            copy.wait_send()
        total = recv[base].astype(jnp.float32)
        for slot in range(1, size):
            total = total + recv[base + slot].astype(jnp.float32)
        acc = total
    o_ref[...] = acc.astype(o_ref.dtype)


def group_sum(x, axis_names, stages, wire_dtype, collective_id):
    slots = sum(size for _, _, size in stages)
    return pl.pallas_call(
        functools.partial(reduce_kernel, axis_names, stages),
        out_shape=jax.ShapeDtypeStruct(x.shape, jnp.float32),
        in_specs=[pl.BlockSpec(memory_space=pltpu.VMEM)],
        out_specs=pl.BlockSpec(memory_space=pltpu.VMEM),
        scratch_shapes=[
            pltpu.VMEM((len(stages),) + x.shape, wire_dtype),
            pltpu.VMEM((slots,) + x.shape, wire_dtype),
            pltpu.SemaphoreType.DMA((slots,)),
            pltpu.SemaphoreType.DMA((slots,)),
        ],
        compiler_params=pltpu.CompilerParams(collective_id=collective_id, has_side_effects=True),
    )(x)


def column_sum(x):
    return jnp.sum(jnp.sum(x, axis=0), axis=1, keepdims=True)


def to_row(columns):
    count = columns[0].shape[0]
    sub = lax.broadcasted_iota(jnp.int32, (count, 128), 0)
    lane = lax.broadcasted_iota(jnp.int32, (count, 128), 1)
    acc = jnp.zeros((count, 128), jnp.float32)
    for index, column in enumerate(columns):
        acc = acc + jnp.where(lane == sub + count * index, jnp.broadcast_to(column, (count, 128)), 0.0)
    return jnp.sum(acc, axis=0, keepdims=True)


def from_row(row, index, count):
    sub = lax.broadcasted_iota(jnp.int32, (count, 128), 0)
    lane = lax.broadcasted_iota(jnp.int32, (count, 128), 1)
    picked = jnp.where(lane == sub + count * index, jnp.broadcast_to(row, (count, 128)), 0.0)
    return jnp.sum(picked, axis=1, keepdims=True)


def group_size(stage):
    size = 1
    for _, extent in stage[1]:
        size *= extent
    return size


def cg_kernel(axis_names, stages, d_ref, beam_hbm, chroma_ref, weight_ref, diag_ref, pm_ref,
              est_ref, beam_ref, beam_sems, parts, rows, recv_p, recv_rows, p_send, p_recv, r_send, r_recv):
    me = {name: lax.axis_index(name) for name in axis_names}

    def place(stage):
        axis, dims = stage
        own = 0
        root = me[axis]
        scale = 1
        for stride, size in dims:
            digit = lax.rem(me[axis] // stride, size)
            own = own + digit * scale
            root = root - digit * stride
            scale *= size

        def device(other):
            coord = root
            scale = 1
            for stride, size in dims:
                coord = coord + lax.rem(other // scale, size) * stride
                scale *= size
            return tuple(coord if name == axis else me[name] for name in axis_names)

        return own, device

    barrier = pltpu.get_barrier_semaphore()
    for stage in stages:
        own, device = place(stage)
        for step in range(1, group_size(stage)):
            other = lax.rem(own + step, group_size(stage))
            pl.semaphore_signal(barrier, 1, device_id=device(other), device_id_type=MESH)

    chunks = beam_sems.shape[0]
    rows_per = beam_ref.shape[0] // chunks
    beam_copies = []
    for chunk in range(chunks):
        window = pl.ds(chunk * rows_per, rows_per)
        beam_copy = pltpu.make_async_copy(beam_hbm.at[window], beam_ref.at[window], beam_sems.at[chunk])
        beam_copy.start()
        beam_copies.append(beam_copy)

    chroma = chroma_ref[...]
    weight = weight_ref[...]
    diag = diag_ref[...]
    pm = pm_ref[...]
    channels, count = d_ref.shape[:2]
    modes = beam_ref.shape[1]

    def beam_seen(vector):
        low = (chroma * vector).astype(jnp.bfloat16).reshape(channels * count, modes)
        seen = lax.dot_general(
            low, beam_ref[...], (((1,), (1,)), ((), ())), preferred_element_type=jnp.float32
        )
        return seen.reshape(channels, count, -1)

    def beam_forward(vector):
        return (weight * beam_seen(vector)).astype(jnp.bfloat16)

    def beam_backward(heard):
        back = jnp.dot(heard.reshape(channels * count, -1), beam_ref[...], preferred_element_type=jnp.float32)
        return chroma * back.reshape(channels, count, modes)


    def exchange_start(stage, src, recv, base, send_sems, recv_sems):
        own, device = place(stage)
        size = group_size(stage)

        def copy_to(other, slot):
            return pltpu.make_async_remote_copy(
                src_ref=src,
                dst_ref=recv.at[base + slot],
                send_sem=send_sems.at[base + other],
                recv_sem=recv_sems.at[base + slot],
                device_id=device(other),
                device_id_type=MESH,
            )

        for step in range(1, size):
            copy_to(lax.rem(own + step, size), own).start()
        recv[base + own] = src[...]
        return own, size, base, recv, copy_to

    sent = []

    def exchange_finish(state):
        own, size, base, recv, copy_to = state
        for step in range(1, size):
            other = lax.rem(own + step, size)
            copy_to(other, other).wait_recv()
        sent.append(state)
        total = recv[base].astype(jnp.float32)
        for slot in range(1, size):
            total = total + recv[base + slot].astype(jnp.float32)
        return total

    counter = {"row": 0, "slot": 0, "part": 0}

    def next_row(value):
        index = counter["row"]
        counter["row"] += 1
        rows[index] = value
        return rows.at[index]

    def row_stage(stage, src):
        base = counter["slot"]
        counter["slot"] += group_size(stage)
        return exchange_start(stage, src, recv_rows, base, r_send, r_recv)

    def reduce_rest(value):
        for stage in stages[1:]:
            value = exchange_finish(row_stage(stage, next_row(value)))
        return value

    def projection_start(vector):
        index = counter["part"]
        counter["part"] += 1
        for rank in range(pm.shape[1]):
            parts[index, rank] = jnp.sum(pm[:, rank] * vector, axis=0).astype(parts.dtype)
        nz = group_size(stages[0])
        return exchange_start(stages[0], parts.at[index], recv_p, index * nz, p_send, p_recv)

    weighted = d_ref[...].reshape(channels * count, -1)
    back = None
    for chunk, beam_copy in enumerate(beam_copies):
        beam_copy.wait()
        window = slice(chunk * rows_per, (chunk + 1) * rows_per)
        term = jnp.dot(
            weighted[:, window], beam_ref[window, :], preferred_element_type=jnp.float32
        )
        back = term if back is None else back + term
    d = chroma * back.reshape(channels, count, modes)
    pl.semaphore_wait(barrier, sum(group_size(stage) - 1 for stage in stages))
    p_state = projection_start(d)
    seen = beam_seen(d)
    heard = (weight * seen).astype(jnp.bfloat16)
    quadratic = column_sum(seen * heard.astype(jnp.float32)) + column_sum(d * (diag * d))
    z_state = row_stage(stages[0], next_row(to_row([quadratic, column_sum(d * d)])))
    cb = beam_backward(heard)
    projection = exchange_finish(p_state)
    zrow = exchange_finish(z_state)
    total = reduce_rest(zrow + to_row([column_sum(projection * projection)]))
    curve = from_row(total, 0, count)
    norm_now = from_row(total, 1, count)
    step_size = (norm_now / curve)[None]
    estimate = step_size * d
    spread = pm[:, 0] * projection[0][None]
    for rank in range(1, pm.shape[1]):
        spread = spread + pm[:, rank] * projection[rank][None]
    residual = d - step_size * (cb + diag * d + spread)
    z_state = row_stage(stages[0], next_row(to_row([column_sum(residual * residual)])))
    p_state = projection_start(residual)
    cb_residual = beam_backward(beam_forward(residual))
    total = reduce_rest(exchange_finish(z_state))
    projection_residual = exchange_finish(p_state)
    norm_next = from_row(total, 0, count)
    ratio = (norm_next / norm_now)[None]
    direction = residual + ratio * d
    cb_direction = cb_residual + ratio * cb
    projection = projection_residual + ratio * projection
    zrow = exchange_finish(
        row_stage(stages[0], next_row(to_row([column_sum(direction * (cb_direction + diag * direction))])))
    )
    total = reduce_rest(zrow + to_row([column_sum(projection * projection)]))
    curve = from_row(total, 0, count)
    est_ref[...] = estimate + (norm_next / curve)[None] * direction
    for own, size, _, _, copy_to in sent:
        for step in range(1, size):
            copy_to(lax.rem(own + step, size), own).wait_send()


def cg_solve(axis_names, stages, d, beam, chroma, weight, diag, pm):
    reductions = 3
    slots = reductions * sum(group_size(stage) for stage in stages)
    rounds = reductions * len(stages)
    nz = group_size(stages[0])
    vector = jax.ShapeDtypeStruct(d.shape[:2] + beam.shape[1:], jnp.float32)
    row = jax.ShapeDtypeStruct((1, 128), jnp.float32)
    vmem = pl.BlockSpec(memory_space=pltpu.VMEM)
    part_shape = (pm.shape[1],) + vector.shape[1:]
    return pl.pallas_call(
        functools.partial(cg_kernel, axis_names, stages),
        out_shape=vector,
        in_specs=[vmem, pl.BlockSpec(memory_space=pl.ANY)] + [vmem] * 4,
        out_specs=vmem,
        scratch_shapes=[
            pltpu.VMEM(beam.shape, beam.dtype),
            pltpu.SemaphoreType.DMA((8,)),
            pltpu.VMEM((2,) + part_shape, jnp.bfloat16),
            pltpu.VMEM((rounds, 1, 128), jnp.float32),
            pltpu.VMEM((2 * nz,) + part_shape, jnp.bfloat16),
            pltpu.VMEM((slots, 1, 128), jnp.float32),
            pltpu.SemaphoreType.DMA((2 * nz,)),
            pltpu.SemaphoreType.DMA((2 * nz,)),
            pltpu.SemaphoreType.DMA((slots,)),
            pltpu.SemaphoreType.DMA((slots,)),
        ],
        compiler_params=pltpu.CompilerParams(collective_id=1, has_side_effects=True),
    )(d, beam, chroma, weight, diag, pm)


def make_shards(mesh):
    axis_names = tuple(mesh.axis_names)
    mode_devices = mesh.shape["ma"]
    freq_devices = mesh.shape["freq"]
    if mode_devices % 16 == 0:
        mode_stages = [("ma", 1, 2), ("ma", 2, 8), ("ma", 16, mode_devices // 16)]
    else:
        mode_stages = [("ma", 1, mode_devices)]
    global_stages = mode_stages + [("freq", 1, freq_devices)]
    freq_stages = [("freq", 1, freq_devices)]

    def scalar_sum(*vectors):
        rows = jnp.stack(vectors)
        padded = jnp.pad(rows, ((0, 8 - rows.shape[0]), (0, 128 - rows.shape[1])))
        summed = group_sum(padded, axis_names, global_stages, jnp.float32, 2)
        return [summed[index, : rows.shape[1]] for index in range(len(vectors))]

    def freq_sum(partial_sum):
        shape = partial_sum.shape
        flat = partial_sum.reshape(-1, shape[-1])
        summed = group_sum(flat, axis_names, freq_stages, jnp.bfloat16, 1)
        return summed.reshape(shape)

    def shards(timestream, beam_transfer, chromatic_gain, noise_weight, prior_diagonal, prior_modes):
        spectral_channels = timestream.shape[0]
        device_time_samples = timestream.shape[1]
        noise_realizations = timestream.shape[2]
        antenna_pairs = timestream.shape[3]
        mode_devices_here = mode_devices
        columns = noise_realizations * antenna_pairs // mode_devices_here
        blocks = antenna_pairs // columns
        halves = columns // 128
        send = timestream.reshape(
            spectral_channels, device_time_samples, noise_realizations, blocks, halves, 128
        ).transpose(2, 3, 0, 1, 4, 5)
        send = send.reshape(mode_devices_here, spectral_channels * device_time_samples * halves, 128)
        received = lax.all_to_all(send, "ma", 0, 0, tiled=True)
        received = received.reshape(mode_devices_here, spectral_channels, device_time_samples, columns)
        all_times = mode_devices_here * device_time_samples
        hartley = hartley_table(all_times // 2, all_times)
        hartley_high = hartley.astype(jnp.bfloat16)
        hartley_low = (hartley - hartley_high.astype(jnp.float32)).astype(jnp.bfloat16)
        hartley_high = hartley_high.reshape(all_times // 2, mode_devices_here, device_time_samples)
        hartley_low = hartley_low.reshape(all_times // 2, mode_devices_here, device_time_samples)
        mode_high = jnp.einsum(
            "mit,iftc->mfc", hartley_high, received, preferred_element_type=jnp.float32
        )
        mode_low = jnp.einsum("mit,iftc->mfc", hartley_low, received, preferred_element_type=jnp.float32)
        mode_rows = (mode_high + mode_low).astype(jnp.bfloat16)
        back_rows = lax.all_to_all(mode_rows, "ma", 0, 0, tiled=True)
        resident_modes = back_rows.shape[0] // mode_devices_here
        back_rows = back_rows.reshape(
            noise_realizations, blocks, resident_modes, spectral_channels, columns
        )
        measured_visibility = back_rows.transpose(3, 2, 0, 1, 4).reshape(
            spectral_channels, resident_modes, noise_realizations, antenna_pairs
        )
        chroma = chromatic_gain[:, None, None, :]
        diagonal = prior_diagonal[:, None, None, :]
        weighted = (noise_weight[:, :, None, :] * measured_visibility.astype(jnp.float32)).astype(
            jnp.bfloat16
        )

        assert resident_modes == 1
        if mode_devices % 16 == 0:
            cg_stages = [
                ("freq", [(1, freq_devices)]),
                ("ma", [(1, 2), (16, mode_devices // 16)]),
                ("ma", [(2, 8)]),
            ]
        else:
            cg_stages = [("freq", [(1, freq_devices)]), ("ma", [(1, mode_devices)])]
        diag_rows = prior_diagonal[:, None, :]
        mode_rows4 = prior_modes[:, :, None, :]

        def beam_back(direction):
            low = (chroma * direction).astype(jnp.bfloat16)
            seen = jnp.einsum("fmks,mbs->fmkb", low, beam_transfer, preferred_element_type=jnp.float32)
            heard = (noise_weight[:, :, None, :] * seen).astype(jnp.bfloat16)
            back = jnp.einsum(
                "fmkb,mbs->fmks", heard, beam_transfer, preferred_element_type=jnp.float32
            )
            return (chroma * back)[:, 0]

        direction = weighted[:, 0]
        operands = (beam_transfer[0], chromatic_gain[:, None, :], noise_weight, diag_rows, mode_rows4)
        estimate = cg_solve(axis_names, cg_stages, direction, *operands)
        estimate = estimate[:, None]
        return estimate

    return shards


def solution(mesh):
    in_specs = (
        P("freq", "ma", None, None),
        P("ma", None, None),
        P("freq", None),
        P("freq", "ma", None),
        P("freq", None),
        P("freq", None, None),
    )
    out_specs = P("freq", "ma", None, None)
    return jax.shard_map(make_shards(mesh), mesh=mesh, in_specs=in_specs, out_specs=out_specs, check_vma=False)
```

```python
import functools

import jax
import jax.numpy as jnp
from jax import lax
from jax.experimental import pallas as pl
from jax.experimental.pallas import tpu as pltpu
from jax.sharding import PartitionSpec as P

ITERS = 2
MESH = pl.DeviceIdType.MESH


def hartley_table(rows, cols):
    index_m = jnp.arange(rows, dtype=jnp.int32)[:, None]
    index_t = jnp.arange(cols, dtype=jnp.int32)[None, :]
    phase = (index_m * index_t % cols).astype(jnp.float32)
    angle = 2.0 * jnp.pi * phase / cols
    return (jnp.cos(angle) + jnp.sin(angle)) / jnp.sqrt(jnp.float32(cols))


def inner(left, right):
    return jnp.sum(left * right, axis=(0, 1, 3))


def reduce_kernel(axis_names, stages, x_ref, o_ref, cur, recv, send_sem, recv_sem):
    me = {name: lax.axis_index(name) for name in axis_names}

    def device(axis, coord):
        return tuple(coord if name == axis else me[name] for name in axis_names)

    plan = []
    base = 0
    for axis, stride, size in stages:
        own = (me[axis] // stride) % size
        root = me[axis] - own * stride
        peers = []
        for step in range(1, size):
            other = lax.rem(own + step, size)
            peers.append((other, device(axis, root + other * stride)))
        plan.append((base, own, size, peers))
        base += size

    barrier = pltpu.get_barrier_semaphore()
    for _, _, _, peers in plan:
        for _, peer in peers:
            pl.semaphore_signal(barrier, 1, device_id=peer, device_id_type=MESH)
    pl.semaphore_wait(barrier, sum(len(peers) for _, _, _, peers in plan))

    acc = x_ref[...].astype(jnp.float32)
    for index, (base, own, size, peers) in enumerate(plan):
        cur[index] = acc.astype(cur.dtype)
        copies = []
        for other, peer in peers:
            copy = pltpu.make_async_remote_copy(
                src_ref=cur.at[index],
                dst_ref=recv.at[base + own],
                send_sem=send_sem.at[base + other],
                recv_sem=recv_sem.at[base + own],
                device_id=peer,
                device_id_type=MESH,
            )
            copy.start()
            copies.append(copy)
        recv[base + own] = acc.astype(recv.dtype)
        for other, peer in peers:
            pltpu.make_async_remote_copy(
                src_ref=cur.at[index],
                dst_ref=recv.at[base + other],
                send_sem=send_sem.at[base + other],
                recv_sem=recv_sem.at[base + other],
                device_id=peer,
                device_id_type=MESH,
            ).wait_recv()
        for copy in copies:
            copy.wait_send()
        total = recv[base].astype(jnp.float32)
        for slot in range(1, size):
            total = total + recv[base + slot].astype(jnp.float32)
        acc = total
    o_ref[...] = acc.astype(o_ref.dtype)


def group_sum(x, axis_names, stages, wire_dtype, collective_id):
    slots = sum(size for _, _, size in stages)
    return pl.pallas_call(
        functools.partial(reduce_kernel, axis_names, stages),
        out_shape=jax.ShapeDtypeStruct(x.shape, jnp.float32),
        in_specs=[pl.BlockSpec(memory_space=pltpu.VMEM)],
        out_specs=pl.BlockSpec(memory_space=pltpu.VMEM),
        scratch_shapes=[
            pltpu.VMEM((len(stages),) + x.shape, wire_dtype),
            pltpu.VMEM((slots,) + x.shape, wire_dtype),
            pltpu.SemaphoreType.DMA((slots,)),
            pltpu.SemaphoreType.DMA((slots,)),
        ],
        compiler_params=pltpu.CompilerParams(collective_id=collective_id, has_side_effects=True),
    )(x)


def column_sum(x):
    return jnp.sum(jnp.sum(x, axis=0), axis=1, keepdims=True)


def to_row(columns):
    count = columns[0].shape[0]
    sub = lax.broadcasted_iota(jnp.int32, (count, 128), 0)
    lane = lax.broadcasted_iota(jnp.int32, (count, 128), 1)
    acc = jnp.zeros((count, 128), jnp.float32)
    for index, column in enumerate(columns):
        acc = acc + jnp.where(lane == sub + count * index, jnp.broadcast_to(column, (count, 128)), 0.0)
    return jnp.sum(acc, axis=0, keepdims=True)


def from_row(row, index, count):
    sub = lax.broadcasted_iota(jnp.int32, (count, 128), 0)
    lane = lax.broadcasted_iota(jnp.int32, (count, 128), 1)
    picked = jnp.where(lane == sub + count * index, jnp.broadcast_to(row, (count, 128)), 0.0)
    return jnp.sum(picked, axis=1, keepdims=True)


def group_size(stage):
    size = 1
    for _, extent in stage[1]:
        size *= extent
    return size


def cg_kernel(axis_names, stages, d_ref, beam_hbm, chroma_ref, weight_ref, diag_ref, pm_ref,
              est_ref, beam_ref, beam_sems, parts, rows, recv_p, recv_rows, p_send, p_recv, r_send, r_recv):
    me = {name: lax.axis_index(name) for name in axis_names}

    def place(stage):
        axis, dims = stage
        own = 0
        root = me[axis]
        scale = 1
        for stride, size in dims:
            digit = lax.rem(me[axis] // stride, size)
            own = own + digit * scale
            root = root - digit * stride
            scale *= size

        def device(other):
            coord = root
            scale = 1
            for stride, size in dims:
                coord = coord + lax.rem(other // scale, size) * stride
                scale *= size
            return tuple(coord if name == axis else me[name] for name in axis_names)

        return own, device

    barrier = pltpu.get_barrier_semaphore()
    for stage in stages:
        own, device = place(stage)
        for step in range(1, group_size(stage)):
            other = lax.rem(own + step, group_size(stage))
            pl.semaphore_signal(barrier, 1, device_id=device(other), device_id_type=MESH)

    chunks = beam_sems.shape[0]
    rows_per = beam_ref.shape[0] // chunks
    beam_copies = []
    for chunk in range(chunks):
        window = pl.ds(chunk * rows_per, rows_per)
        beam_copy = pltpu.make_async_copy(beam_hbm.at[window], beam_ref.at[window], beam_sems.at[chunk])
        beam_copy.start()
        beam_copies.append(beam_copy)

    chroma = chroma_ref[...]
    weight = weight_ref[...]
    diag = diag_ref[...]
    pm = pm_ref[...]
    channels, count = d_ref.shape[:2]
    modes = beam_ref.shape[1]

    def beam_seen(vector):
        low = (chroma * vector).astype(jnp.bfloat16).reshape(channels * count, modes)
        seen = lax.dot_general(
            low, beam_ref[...], (((1,), (1,)), ((), ())), preferred_element_type=jnp.float32
        )
        return seen.reshape(channels, count, -1)

    def beam_forward(vector):
        return (weight * beam_seen(vector)).astype(jnp.bfloat16)

    def beam_backward(heard):
        back = jnp.dot(heard.reshape(channels * count, -1), beam_ref[...], preferred_element_type=jnp.float32)
        return chroma * back.reshape(channels, count, modes)


    def exchange_start(stage, src, recv, base, send_sems, recv_sems):
        own, device = place(stage)
        size = group_size(stage)

        def copy_to(other, slot):
            return pltpu.make_async_remote_copy(
                src_ref=src,
                dst_ref=recv.at[base + slot],
                send_sem=send_sems.at[base + other],
                recv_sem=recv_sems.at[base + slot],
                device_id=device(other),
                device_id_type=MESH,
            )

        for step in range(1, size):
            copy_to(lax.rem(own + step, size), own).start()
        recv[base + own] = src[...]
        return own, size, base, recv, copy_to

    sent = []

    def exchange_finish(state):
        own, size, base, recv, copy_to = state
        for step in range(1, size):
            other = lax.rem(own + step, size)
            copy_to(other, other).wait_recv()
        sent.append(state)
        total = recv[base].astype(jnp.float32)
        for slot in range(1, size):
            total = total + recv[base + slot].astype(jnp.float32)
        return total

    counter = {"row": 0, "slot": 0, "part": 0}

    def next_row(value):
        index = counter["row"]
        counter["row"] += 1
        rows[index] = value
        return rows.at[index]

    def row_stage(stage, src):
        base = counter["slot"]
        counter["slot"] += group_size(stage)
        return exchange_start(stage, src, recv_rows, base, r_send, r_recv)

    def reduce_rest(value):
        for stage in stages[1:]:
            value = exchange_finish(row_stage(stage, next_row(value)))
        return value

    def projection_start(vector):
        index = counter["part"]
        counter["part"] += 1
        for rank in range(pm.shape[1]):
            parts[index, rank] = jnp.sum(pm[:, rank] * vector, axis=0).astype(parts.dtype)
        nz = group_size(stages[0])
        return exchange_start(stages[0], parts.at[index], recv_p, index * nz, p_send, p_recv)

    weighted = d_ref[...].reshape(channels * count, -1)
    back = None
    for chunk, beam_copy in enumerate(beam_copies):
        beam_copy.wait()
        window = slice(chunk * rows_per, (chunk + 1) * rows_per)
        term = jnp.dot(
            weighted[:, window], beam_ref[window, :], preferred_element_type=jnp.float32
        )
        back = term if back is None else back + term
    d = chroma * back.reshape(channels, count, modes)
    pl.semaphore_wait(barrier, sum(group_size(stage) - 1 for stage in stages))
    p_state = projection_start(d)
    seen = beam_seen(d)
    heard = (weight * seen).astype(jnp.bfloat16)
    quadratic = column_sum(seen * heard.astype(jnp.float32)) + column_sum(d * (diag * d))
    z_state = row_stage(stages[0], next_row(to_row([quadratic, column_sum(d * d)])))
    cb = beam_backward(heard)
    projection = exchange_finish(p_state)
    zrow = exchange_finish(z_state)
    total = reduce_rest(zrow + to_row([column_sum(projection * projection)]))
    curve = from_row(total, 0, count)
    norm_now = from_row(total, 1, count)
    step_size = (norm_now / curve)[None]
    estimate = step_size * d
    spread = pm[:, 0] * projection[0][None]
    for rank in range(1, pm.shape[1]):
        spread = spread + pm[:, rank] * projection[rank][None]
    residual = d - step_size * (cb + diag * d + spread)
    z_state = row_stage(stages[0], next_row(to_row([column_sum(residual * residual)])))
    p_state = projection_start(residual)
    cb_residual = beam_backward(beam_forward(residual))
    total = reduce_rest(exchange_finish(z_state))
    projection_residual = exchange_finish(p_state)
    norm_next = from_row(total, 0, count)
    ratio = (norm_next / norm_now)[None]
    direction = residual + ratio * d
    cb_direction = cb_residual + ratio * cb
    projection = projection_residual + ratio * projection
    zrow = exchange_finish(
        row_stage(stages[0], next_row(to_row([column_sum(direction * (cb_direction + diag * direction))])))
    )
    total = reduce_rest(zrow + to_row([column_sum(projection * projection)]))
    curve = from_row(total, 0, count)
    est_ref[...] = estimate + (norm_next / curve)[None] * direction
    for own, size, _, _, copy_to in sent:
        for step in range(1, size):
            copy_to(lax.rem(own + step, size), own).wait_send()


def cg_solve(axis_names, stages, d, beam, chroma, weight, diag, pm):
    reductions = 3
    slots = reductions * sum(group_size(stage) for stage in stages)
    rounds = reductions * len(stages)
    nz = group_size(stages[0])
    vector = jax.ShapeDtypeStruct(d.shape[:2] + beam.shape[1:], jnp.float32)
    row = jax.ShapeDtypeStruct((1, 128), jnp.float32)
    vmem = pl.BlockSpec(memory_space=pltpu.VMEM)
    part_shape = (pm.shape[1],) + vector.shape[1:]
    return pl.pallas_call(
        functools.partial(cg_kernel, axis_names, stages),
        out_shape=vector,
        in_specs=[vmem, pl.BlockSpec(memory_space=pl.ANY)] + [vmem] * 4,
        out_specs=vmem,
        scratch_shapes=[
            pltpu.VMEM(beam.shape, beam.dtype),
            pltpu.SemaphoreType.DMA((4,)),
            pltpu.VMEM((2,) + part_shape, jnp.bfloat16),
            pltpu.VMEM((rounds, 1, 128), jnp.float32),
            pltpu.VMEM((2 * nz,) + part_shape, jnp.bfloat16),
            pltpu.VMEM((slots, 1, 128), jnp.float32),
            pltpu.SemaphoreType.DMA((2 * nz,)),
            pltpu.SemaphoreType.DMA((2 * nz,)),
            pltpu.SemaphoreType.DMA((slots,)),
            pltpu.SemaphoreType.DMA((slots,)),
        ],
        compiler_params=pltpu.CompilerParams(collective_id=1, has_side_effects=True),
    )(d, beam, chroma, weight, diag, pm)


def make_shards(mesh):
    axis_names = tuple(mesh.axis_names)
    mode_devices = mesh.shape["ma"]
    freq_devices = mesh.shape["freq"]
    if mode_devices % 16 == 0:
        mode_stages = [("ma", 1, 2), ("ma", 2, 8), ("ma", 16, mode_devices // 16)]
    else:
        mode_stages = [("ma", 1, mode_devices)]
    global_stages = mode_stages + [("freq", 1, freq_devices)]
    freq_stages = [("freq", 1, freq_devices)]

    def scalar_sum(*vectors):
        rows = jnp.stack(vectors)
        padded = jnp.pad(rows, ((0, 8 - rows.shape[0]), (0, 128 - rows.shape[1])))
        summed = group_sum(padded, axis_names, global_stages, jnp.float32, 2)
        return [summed[index, : rows.shape[1]] for index in range(len(vectors))]

    def freq_sum(partial_sum):
        shape = partial_sum.shape
        flat = partial_sum.reshape(-1, shape[-1])
        summed = group_sum(flat, axis_names, freq_stages, jnp.bfloat16, 1)
        return summed.reshape(shape)

    def shards(timestream, beam_transfer, chromatic_gain, noise_weight, prior_diagonal, prior_modes):
        spectral_channels = timestream.shape[0]
        device_time_samples = timestream.shape[1]
        noise_realizations = timestream.shape[2]
        antenna_pairs = timestream.shape[3]
        mode_devices_here = mode_devices
        columns = noise_realizations * antenna_pairs // mode_devices_here
        blocks = antenna_pairs // columns
        halves = columns // 128
        send = timestream.reshape(
            spectral_channels, device_time_samples, noise_realizations, blocks, halves, 128
        ).transpose(2, 3, 0, 1, 4, 5)
        send = send.reshape(mode_devices_here, spectral_channels * device_time_samples * halves, 128)
        received = lax.all_to_all(send, "ma", 0, 0, tiled=True)
        received = received.reshape(mode_devices_here, spectral_channels, device_time_samples, columns)
        all_times = mode_devices_here * device_time_samples
        hartley = hartley_table(all_times // 2, all_times)
        hartley_high = hartley.astype(jnp.bfloat16)
        hartley_low = (hartley - hartley_high.astype(jnp.float32)).astype(jnp.bfloat16)
        hartley_high = hartley_high.reshape(all_times // 2, mode_devices_here, device_time_samples)
        hartley_low = hartley_low.reshape(all_times // 2, mode_devices_here, device_time_samples)
        mode_high = jnp.einsum(
            "mit,iftc->mfc", hartley_high, received, preferred_element_type=jnp.float32
        )
        mode_low = jnp.einsum("mit,iftc->mfc", hartley_low, received, preferred_element_type=jnp.float32)
        mode_rows = (mode_high + mode_low).astype(jnp.bfloat16)
        back_rows = lax.all_to_all(mode_rows, "ma", 0, 0, tiled=True)
        resident_modes = back_rows.shape[0] // mode_devices_here
        back_rows = back_rows.reshape(
            noise_realizations, blocks, resident_modes, spectral_channels, columns
        )
        measured_visibility = back_rows.transpose(3, 2, 0, 1, 4).reshape(
            spectral_channels, resident_modes, noise_realizations, antenna_pairs
        )
        chroma = chromatic_gain[:, None, None, :]
        diagonal = prior_diagonal[:, None, None, :]
        weighted = (noise_weight[:, :, None, :] * measured_visibility.astype(jnp.float32)).astype(
            jnp.bfloat16
        )

        assert resident_modes == 1
        if mode_devices % 16 == 0:
            cg_stages = [
                ("freq", [(1, freq_devices)]),
                ("ma", [(2, 8)]),
                ("ma", [(1, 2), (16, mode_devices // 16)]),
            ]
        else:
            cg_stages = [("freq", [(1, freq_devices)]), ("ma", [(1, mode_devices)])]
        diag_rows = prior_diagonal[:, None, :]
        mode_rows4 = prior_modes[:, :, None, :]

        def beam_back(direction):
            low = (chroma * direction).astype(jnp.bfloat16)
            seen = jnp.einsum("fmks,mbs->fmkb", low, beam_transfer, preferred_element_type=jnp.float32)
            heard = (noise_weight[:, :, None, :] * seen).astype(jnp.bfloat16)
            back = jnp.einsum(
                "fmkb,mbs->fmks", heard, beam_transfer, preferred_element_type=jnp.float32
            )
            return (chroma * back)[:, 0]

        direction = weighted[:, 0]
        operands = (beam_transfer[0], chromatic_gain[:, None, :], noise_weight, diag_rows, mode_rows4)
        estimate = cg_solve(axis_names, cg_stages, direction, *operands)
        estimate = estimate[:, None]
        return estimate

    return shards


def solution(mesh):
    in_specs = (
        P("freq", "ma", None, None),
        P("ma", None, None),
        P("freq", None),
        P("freq", "ma", None),
        P("freq", None),
        P("freq", None, None),
    )
    out_specs = P("freq", "ma", None, None)
    return jax.shard_map(make_shards(mesh), mesh=mesh, in_specs=in_specs, out_specs=out_specs, check_vma=False)
```

```python
import functools

import jax
import jax.numpy as jnp
from jax import lax
from jax.experimental import pallas as pl
from jax.experimental.pallas import tpu as pltpu
from jax.sharding import PartitionSpec as P

ITERS = 2
MESH = pl.DeviceIdType.MESH


def hartley_table(rows, cols):
    index_m = jnp.arange(rows, dtype=jnp.int32)[:, None]
    index_t = jnp.arange(cols, dtype=jnp.int32)[None, :]
    phase = (index_m * index_t % cols).astype(jnp.float32)
    angle = 2.0 * jnp.pi * phase / cols
    return (jnp.cos(angle) + jnp.sin(angle)) / jnp.sqrt(jnp.float32(cols))


def inner(left, right):
    return jnp.sum(left * right, axis=(0, 1, 3))


def reduce_kernel(axis_names, stages, x_ref, o_ref, cur, recv, send_sem, recv_sem):
    me = {name: lax.axis_index(name) for name in axis_names}

    def device(axis, coord):
        return tuple(coord if name == axis else me[name] for name in axis_names)

    plan = []
    base = 0
    for axis, stride, size in stages:
        own = (me[axis] // stride) % size
        root = me[axis] - own * stride
        peers = []
        for step in range(1, size):
            other = lax.rem(own + step, size)
            peers.append((other, device(axis, root + other * stride)))
        plan.append((base, own, size, peers))
        base += size

    barrier = pltpu.get_barrier_semaphore()
    for _, _, _, peers in plan:
        for _, peer in peers:
            pl.semaphore_signal(barrier, 1, device_id=peer, device_id_type=MESH)
    pl.semaphore_wait(barrier, sum(len(peers) for _, _, _, peers in plan))

    acc = x_ref[...].astype(jnp.float32)
    for index, (base, own, size, peers) in enumerate(plan):
        cur[index] = acc.astype(cur.dtype)
        copies = []
        for other, peer in peers:
            copy = pltpu.make_async_remote_copy(
                src_ref=cur.at[index],
                dst_ref=recv.at[base + own],
                send_sem=send_sem.at[base + other],
                recv_sem=recv_sem.at[base + own],
                device_id=peer,
                device_id_type=MESH,
            )
            copy.start()
            copies.append(copy)
        recv[base + own] = acc.astype(recv.dtype)
        for other, peer in peers:
            pltpu.make_async_remote_copy(
                src_ref=cur.at[index],
                dst_ref=recv.at[base + other],
                send_sem=send_sem.at[base + other],
                recv_sem=recv_sem.at[base + other],
                device_id=peer,
                device_id_type=MESH,
            ).wait_recv()
        for copy in copies:
            copy.wait_send()
        total = recv[base].astype(jnp.float32)
        for slot in range(1, size):
            total = total + recv[base + slot].astype(jnp.float32)
        acc = total
    o_ref[...] = acc.astype(o_ref.dtype)


def group_sum(x, axis_names, stages, wire_dtype, collective_id):
    slots = sum(size for _, _, size in stages)
    return pl.pallas_call(
        functools.partial(reduce_kernel, axis_names, stages),
        out_shape=jax.ShapeDtypeStruct(x.shape, jnp.float32),
        in_specs=[pl.BlockSpec(memory_space=pltpu.VMEM)],
        out_specs=pl.BlockSpec(memory_space=pltpu.VMEM),
        scratch_shapes=[
            pltpu.VMEM((len(stages),) + x.shape, wire_dtype),
            pltpu.VMEM((slots,) + x.shape, wire_dtype),
            pltpu.SemaphoreType.DMA((slots,)),
            pltpu.SemaphoreType.DMA((slots,)),
        ],
        compiler_params=pltpu.CompilerParams(collective_id=collective_id, has_side_effects=True),
    )(x)


def column_sum(x):
    return jnp.sum(jnp.sum(x, axis=0), axis=1, keepdims=True)


def to_row(columns):
    count = columns[0].shape[0]
    sub = lax.broadcasted_iota(jnp.int32, (count, 128), 0)
    lane = lax.broadcasted_iota(jnp.int32, (count, 128), 1)
    acc = jnp.zeros((count, 128), jnp.float32)
    for index, column in enumerate(columns):
        acc = acc + jnp.where(lane == sub + count * index, jnp.broadcast_to(column, (count, 128)), 0.0)
    return jnp.sum(acc, axis=0, keepdims=True)


def from_row(row, index, count):
    sub = lax.broadcasted_iota(jnp.int32, (count, 128), 0)
    lane = lax.broadcasted_iota(jnp.int32, (count, 128), 1)
    picked = jnp.where(lane == sub + count * index, jnp.broadcast_to(row, (count, 128)), 0.0)
    return jnp.sum(picked, axis=1, keepdims=True)


def group_size(stage):
    size = 1
    for _, extent in stage[1]:
        size *= extent
    return size


def cg_kernel(axis_names, stages, d_ref, beam_hbm, chroma_ref, weight_ref, diag_ref, pm_ref,
              est_ref, beam_ref, beam_sems, parts, rows, recv_p, recv_rows, p_send, p_recv, r_send, r_recv):
    me = {name: lax.axis_index(name) for name in axis_names}

    def place(stage):
        axis, dims = stage
        own = 0
        root = me[axis]
        scale = 1
        for stride, size in dims:
            digit = lax.rem(me[axis] // stride, size)
            own = own + digit * scale
            root = root - digit * stride
            scale *= size

        def device(other):
            coord = root
            scale = 1
            for stride, size in dims:
                coord = coord + lax.rem(other // scale, size) * stride
                scale *= size
            return tuple(coord if name == axis else me[name] for name in axis_names)

        return own, device

    barrier = pltpu.get_barrier_semaphore()
    for stage in stages:
        own, device = place(stage)
        for step in range(1, group_size(stage)):
            other = lax.rem(own + step, group_size(stage))
            pl.semaphore_signal(barrier, 1, device_id=device(other), device_id_type=MESH)

    chunks = beam_sems.shape[0]
    rows_per = beam_ref.shape[0] // chunks
    beam_copies = []
    for chunk in range(chunks):
        window = pl.ds(chunk * rows_per, rows_per)
        beam_copy = pltpu.make_async_copy(beam_hbm.at[window], beam_ref.at[window], beam_sems.at[chunk])
        beam_copy.start()
        beam_copies.append(beam_copy)

    chroma = chroma_ref[...]
    weight = weight_ref[...]
    diag = diag_ref[...]
    pm = pm_ref[...]
    channels, count = d_ref.shape[:2]
    modes = beam_ref.shape[1]

    def beam_seen(vector):
        low = (chroma * vector).astype(jnp.bfloat16).reshape(channels * count, modes)
        seen = lax.dot_general(
            low, beam_ref[...], (((1,), (1,)), ((), ())), preferred_element_type=jnp.float32
        )
        return seen.reshape(channels, count, -1)

    def beam_forward(vector):
        return (weight * beam_seen(vector)).astype(jnp.bfloat16)

    def beam_backward(heard):
        back = jnp.dot(heard.reshape(channels * count, -1), beam_ref[...], preferred_element_type=jnp.float32)
        return chroma * back.reshape(channels, count, modes)


    def exchange_start(stage, src, recv, base, send_sems, recv_sems):
        own, device = place(stage)
        size = group_size(stage)

        def copy_to(other, slot):
            return pltpu.make_async_remote_copy(
                src_ref=src,
                dst_ref=recv.at[base + slot],
                send_sem=send_sems.at[base + other],
                recv_sem=recv_sems.at[base + slot],
                device_id=device(other),
                device_id_type=MESH,
            )

        for step in range(1, size):
            copy_to(lax.rem(own + step, size), own).start()
        recv[base + own] = src[...]
        return own, size, base, recv, copy_to

    sent = []

    def exchange_finish(state):
        own, size, base, recv, copy_to = state
        for step in range(1, size):
            other = lax.rem(own + step, size)
            copy_to(other, other).wait_recv()
        sent.append(state)
        total = recv[base].astype(jnp.float32)
        for slot in range(1, size):
            total = total + recv[base + slot].astype(jnp.float32)
        return total

    counter = {"row": 0, "slot": 0, "part": 0}

    def next_row(value):
        index = counter["row"]
        counter["row"] += 1
        rows[index] = value
        return rows.at[index]

    def row_stage(stage, src):
        base = counter["slot"]
        counter["slot"] += group_size(stage)
        return exchange_start(stage, src, recv_rows, base, r_send, r_recv)

    def reduce_rest(value):
        for stage in stages[1:]:
            value = exchange_finish(row_stage(stage, next_row(value)))
        return value

    def projection_start(vector):
        index = counter["part"]
        counter["part"] += 1
        for rank in range(pm.shape[1]):
            parts[index, rank] = jnp.sum(pm[:, rank] * vector, axis=0).astype(parts.dtype)
        nz = group_size(stages[0])
        return exchange_start(stages[0], parts.at[index], recv_p, index * nz, p_send, p_recv)

    weighted = d_ref[...].reshape(channels * count, -1)
    back = None
    for chunk, beam_copy in enumerate(beam_copies):
        beam_copy.wait()
        window = slice(chunk * rows_per, (chunk + 1) * rows_per)
        term = jnp.dot(
            weighted[:, window], beam_ref[window, :], preferred_element_type=jnp.float32
        )
        back = term if back is None else back + term
    d = chroma * back.reshape(channels, count, modes)
    pl.semaphore_wait(barrier, sum(group_size(stage) - 1 for stage in stages))
    p_state = projection_start(d)
    seen = beam_seen(d)
    heard = (weight * seen).astype(jnp.bfloat16)
    quadratic = column_sum(seen * heard.astype(jnp.float32)) + column_sum(d * (diag * d))
    z_state = row_stage(stages[0], next_row(to_row([quadratic, column_sum(d * d)])))
    cb = beam_backward(heard)
    projection = exchange_finish(p_state)
    zrow = exchange_finish(z_state)
    total = reduce_rest(zrow + to_row([column_sum(projection * projection)]))
    curve = from_row(total, 0, count)
    norm_now = from_row(total, 1, count)
    step_size = (norm_now / curve)[None]
    estimate = step_size * d
    spread = pm[:, 0] * projection[0][None]
    for rank in range(1, pm.shape[1]):
        spread = spread + pm[:, rank] * projection[rank][None]
    residual = d - step_size * (cb + diag * d + spread)
    z_state = row_stage(stages[0], next_row(to_row([column_sum(residual * residual)])))
    p_state = projection_start(residual)
    cb_residual = beam_backward(beam_forward(residual))
    total = reduce_rest(exchange_finish(z_state))
    projection_residual = exchange_finish(p_state)
    norm_next = from_row(total, 0, count)
    ratio = (norm_next / norm_now)[None]
    direction = residual + ratio * d
    cb_direction = cb_residual + ratio * cb
    projection = projection_residual + ratio * projection
    zrow = exchange_finish(
        row_stage(stages[0], next_row(to_row([column_sum(direction * (cb_direction + diag * direction))])))
    )
    total = reduce_rest(zrow + to_row([column_sum(projection * projection)]))
    curve = from_row(total, 0, count)
    est_ref[...] = estimate + (norm_next / curve)[None] * direction
    for own, size, _, _, copy_to in sent:
        for step in range(1, size):
            copy_to(lax.rem(own + step, size), own).wait_send()


def cg_solve(axis_names, stages, d, beam, chroma, weight, diag, pm):
    reductions = 3
    slots = reductions * sum(group_size(stage) for stage in stages)
    rounds = reductions * len(stages)
    nz = group_size(stages[0])
    vector = jax.ShapeDtypeStruct(d.shape[:2] + beam.shape[1:], jnp.float32)
    row = jax.ShapeDtypeStruct((1, 128), jnp.float32)
    vmem = pl.BlockSpec(memory_space=pltpu.VMEM)
    part_shape = (pm.shape[1],) + vector.shape[1:]
    return pl.pallas_call(
        functools.partial(cg_kernel, axis_names, stages),
        out_shape=vector,
        in_specs=[vmem, pl.BlockSpec(memory_space=pl.ANY)] + [vmem] * 4,
        out_specs=vmem,
        scratch_shapes=[
            pltpu.VMEM(beam.shape, beam.dtype),
            pltpu.SemaphoreType.DMA((4,)),
            pltpu.VMEM((2,) + part_shape, jnp.bfloat16),
            pltpu.VMEM((rounds, 1, 128), jnp.float32),
            pltpu.VMEM((2 * nz,) + part_shape, jnp.bfloat16),
            pltpu.VMEM((slots, 1, 128), jnp.float32),
            pltpu.SemaphoreType.DMA((2 * nz,)),
            pltpu.SemaphoreType.DMA((2 * nz,)),
            pltpu.SemaphoreType.DMA((slots,)),
            pltpu.SemaphoreType.DMA((slots,)),
        ],
        compiler_params=pltpu.CompilerParams(collective_id=1, has_side_effects=True),
    )(d, beam, chroma, weight, diag, pm)


def make_shards(mesh):
    axis_names = tuple(mesh.axis_names)
    mode_devices = mesh.shape["ma"]
    freq_devices = mesh.shape["freq"]
    if mode_devices % 16 == 0:
        mode_stages = [("ma", 1, 2), ("ma", 2, 8), ("ma", 16, mode_devices // 16)]
    else:
        mode_stages = [("ma", 1, mode_devices)]
    global_stages = mode_stages + [("freq", 1, freq_devices)]
    freq_stages = [("freq", 1, freq_devices)]

    def scalar_sum(*vectors):
        rows = jnp.stack(vectors)
        padded = jnp.pad(rows, ((0, 8 - rows.shape[0]), (0, 128 - rows.shape[1])))
        summed = group_sum(padded, axis_names, global_stages, jnp.float32, 2)
        return [summed[index, : rows.shape[1]] for index in range(len(vectors))]

    def freq_sum(partial_sum):
        shape = partial_sum.shape
        flat = partial_sum.reshape(-1, shape[-1])
        summed = group_sum(flat, axis_names, freq_stages, jnp.bfloat16, 1)
        return summed.reshape(shape)

    def shards(timestream, beam_transfer, chromatic_gain, noise_weight, prior_diagonal, prior_modes):
        spectral_channels = timestream.shape[0]
        device_time_samples = timestream.shape[1]
        noise_realizations = timestream.shape[2]
        antenna_pairs = timestream.shape[3]
        mode_devices_here = mode_devices
        columns = noise_realizations * antenna_pairs // mode_devices_here
        blocks = antenna_pairs // columns
        halves = columns // 128
        send = timestream.reshape(
            spectral_channels, device_time_samples, noise_realizations, blocks, halves, 128
        ).transpose(2, 3, 0, 1, 4, 5)
        send = send.reshape(mode_devices_here, spectral_channels * device_time_samples * halves, 128)
        received = lax.all_to_all(send, "ma", 0, 0, tiled=True)
        received = received.reshape(mode_devices_here, spectral_channels, device_time_samples, columns)
        all_times = mode_devices_here * device_time_samples
        hartley = hartley_table(all_times // 2, all_times)
        hartley_high = hartley.astype(jnp.bfloat16)
        hartley_low = (hartley - hartley_high.astype(jnp.float32)).astype(jnp.bfloat16)
        hartley_high = hartley_high.reshape(all_times // 2, mode_devices_here, device_time_samples)
        hartley_low = hartley_low.reshape(all_times // 2, mode_devices_here, device_time_samples)
        mode_high = jnp.einsum(
            "mit,iftc->mfc", hartley_high, received, preferred_element_type=jnp.float32
        )
        mode_low = jnp.einsum("mit,iftc->mfc", hartley_low, received, preferred_element_type=jnp.float32)
        mode_rows = (mode_high + mode_low).astype(jnp.bfloat16)
        back_rows = lax.all_to_all(mode_rows, "ma", 0, 0, tiled=True)
        resident_modes = back_rows.shape[0] // mode_devices_here
        back_rows = back_rows.reshape(
            noise_realizations, blocks, resident_modes, spectral_channels, columns
        )
        measured_visibility = back_rows.transpose(3, 2, 0, 1, 4).reshape(
            spectral_channels, resident_modes, noise_realizations, antenna_pairs
        )
        chroma = chromatic_gain[:, None, None, :]
        diagonal = prior_diagonal[:, None, None, :]
        weighted = (noise_weight[:, :, None, :] * measured_visibility.astype(jnp.float32)).astype(
            jnp.bfloat16
        )

        assert resident_modes == 1
        if mode_devices % 16 == 0:
            cg_stages = [
                ("freq", [(1, freq_devices)]),
                ("ma", [(1, 2), (2, 8)]),
                ("ma", [(16, mode_devices // 16)]),
            ]
        else:
            cg_stages = [("freq", [(1, freq_devices)]), ("ma", [(1, mode_devices)])]
        diag_rows = prior_diagonal[:, None, :]
        mode_rows4 = prior_modes[:, :, None, :]

        def beam_back(direction):
            low = (chroma * direction).astype(jnp.bfloat16)
            seen = jnp.einsum("fmks,mbs->fmkb", low, beam_transfer, preferred_element_type=jnp.float32)
            heard = (noise_weight[:, :, None, :] * seen).astype(jnp.bfloat16)
            back = jnp.einsum(
                "fmkb,mbs->fmks", heard, beam_transfer, preferred_element_type=jnp.float32
            )
            return (chroma * back)[:, 0]

        direction = weighted[:, 0]
        operands = (beam_transfer[0], chromatic_gain[:, None, :], noise_weight, diag_rows, mode_rows4)
        estimate = cg_solve(axis_names, cg_stages, direction, *operands)
        estimate = estimate[:, None]
        return estimate

    return shards


def solution(mesh):
    in_specs = (
        P("freq", "ma", None, None),
        P("ma", None, None),
        P("freq", None),
        P("freq", "ma", None),
        P("freq", None),
        P("freq", None, None),
    )
    out_specs = P("freq", "ma", None, None)
    return jax.shard_map(make_shards(mesh), mesh=mesh, in_specs=in_specs, out_specs=out_specs, check_vma=False)
```
